32 devices in a mesh: gx: 2 (over y), gy: 4 (over x, core), gz: 4 (over z).
Axes of the slice: x: 2, y: 2, z: 4, core: 2. Of those that a mesh axis runs over, the one named last changes fastest.
Arguments:
- fluid_state: float32 [4, 32, 64, 512], P(None, 'gx', 'gy', 'gz'), may hold values from -6 to 6
- shell_disp: float32 [3, 32768], P(None, ('gy', 'gz')), may hold values from -6 to 6
- quad_weights: float32 [32, 32, 64], P(('gx', 'gy', 'gz')), may hold values from 0.25 to 1
- quad_elements: int32 [32, 32, 64], P(('gx', 'gy', 'gz')), may hold values from 0 to 32767
- owner_cells: int32 [32, 32, 64], P(('gx', 'gy', 'gz')), may hold values from 0 to 32767
- owner_counts: int32 [32, 32], P(('gx', 'gy', 'gz')), may hold values from 0 to 64, as said below
Outputs:
- fluid_out: float32 [4, 32, 64, 512], P(None, 'gx', 'gy', 'gz')
- shell_out: float32 [3, 32768], P(None, ('gy', 'gz'))
The draws below stay inside these ranges and needn't reach their ends.
Inputs may be any that keep to these rules, and one draw needn't show every extreme that they name: `owner_counts`: some owner has 64 live records from every sender; some owner has none from some sender.
All inputs are finite; a program needn't handle non-finite values.
Results may differ from the reference program's by a relative error of at most 0.000023.
Values sent between devices are 32-bit elements; how exact they have to be, the bound alone decides.
A program may use at most 128 MiB of HBM per device.

```python
import math
import jax
import jax.numpy as jnp
from jax import lax

CX = 16
CY = 16
CZ = 128
SLOT = 64
ITERS = 2
RANKS = 32
NSH = 32768
NX = 32
NY = 64
NZ = 512
N_GY = 4
N_GZ = 4


def draw_owner_counts(key, part):
    key_level, key_drop, key_full, key_empty, key_sender = jax.random.split(jax.random.fold_in(key, 7), 5)
    level = jax.random.randint(key_level, (RANKS, 1), SLOT // 2, SLOT + 1)
    drop = jax.random.randint(key_drop, (RANKS, RANKS), 0, SLOT + 1) % (level // 2 + 1)
    counts = level - drop
    full_owner = jax.random.randint(key_full, (), 0, RANKS)
    offset = jax.random.randint(key_empty, (), 1, RANKS)
    empty_owner = (full_owner + offset) % RANKS
    sender = jax.random.randint(key_sender, (), 0, RANKS)
    rows = jnp.arange(RANKS, dtype=jnp.int32)[:, None]
    columns = jnp.arange(RANKS, dtype=jnp.int32)[None, :]
    counts = jnp.where((rows == empty_owner) & (columns == sender), 0, counts)
    return jnp.where(rows == full_owner, SLOT, counts).astype(jnp.int32)


def touch_ends(drawn, own_key, low, high):
    spot = [jax.random.randint(jax.random.fold_in(own_key, axis), (), 0, length) for axis, length in enumerate(drawn.shape)]
    widest = drawn.shape.index(max(drawn.shape))
    beside = spot[:widest] + [(spot[widest] + 1) % drawn.shape[widest]] + spot[widest + 1:]
    return drawn.at[tuple(spot)].set(low).at[tuple(beside)].set(high)


def shard_levels(stream_key, dims, cuts, least, top_value):
    gain = 1.0
    for position, parts in cuts:
        heights = jax.random.uniform(jax.random.fold_in(jax.random.fold_in(stream_key, 6), position), (parts,), jnp.float32, least / len(cuts), top_value / len(cuts))
        gain = gain * jnp.repeat(jnp.exp(heights), dims[position] // parts).reshape((-1,) + (1,) * (len(dims) - 1 - position))
    return gain


def bell_draw(stream_key, dims, scale, limit, cuts=(), kind=jnp.bfloat16):
    loudness = shard_levels(stream_key, dims, cuts, -0.22, 0.18) if cuts else 1.0
    values = jax.random.normal(stream_key, dims, jnp.float32) * scale * loudness
    return jnp.minimum(jnp.maximum(values, -limit), limit).astype(kind)


def setup_inputs(seed: int = 0) -> dict:
    key_of = jax.random.split(jax.random.key(seed), 7)
    return {
        "fluid_state": bell_draw(key_of[0], (4, NX, NY, NZ), 1.0, 6.0, ((1, 2), (2, 4), (3, 4)), jnp.float32),
        "shell_disp": bell_draw(key_of[1], (3, NSH), 1.0, 6.0, ((1, 16),), jnp.float32),
        "quad_weights": jnp.clip(jnp.exp(math.log(1.0) - 1.3862944 * jax.random.uniform(key_of[2], (RANKS, RANKS, SLOT), jnp.float32) ** shard_levels(key_of[2], (RANKS, RANKS, SLOT), ((0, 32),), -0.2, 0.2)), 0.25, 1.0),
        "quad_elements": touch_ends(jax.random.randint(key_of[3], (RANKS, RANKS, SLOT), 0, NSH), jax.random.fold_in(key_of[3], 1), 0, NSH - 1).astype(jnp.int32),
        "owner_cells": touch_ends(jax.random.randint(key_of[4], (RANKS, RANKS, SLOT), 0, CX * CY * CZ), jax.random.fold_in(key_of[4], 1), 0, (CX * CY * CZ) - 1).astype(jnp.int32),
        "owner_counts": draw_owner_counts(jax.random.fold_in(key_of[6], 71), 0),
    }


advection = 0.2
penalty = 0.5
relaxation = 0.05


def smooth_axis(values, axis):
    length = values.shape[axis] - 2
    lower = lax.slice_in_dim(values, 0, length, axis=axis)
    middle = lax.slice_in_dim(values, 1, length + 1, axis=axis)
    upper = lax.slice_in_dim(values, 2, length + 2, axis=axis)
    return 0.25 * lower + 0.5 * middle + 0.25 * upper


def sweep_fluid(padded):
    smoothed = smooth_axis(smooth_axis(smooth_axis(padded, 1), 2), 3)
    center = padded[:, 1:-1, 1:-1, 1:-1]
    grad_x = 0.5 * (padded[:, 2:, 1:-1, 1:-1] - padded[:, :-2, 1:-1, 1:-1])
    grad_y = 0.5 * (padded[:, 1:-1, 2:, 1:-1] - padded[:, 1:-1, :-2, 1:-1])
    grad_z = 0.5 * (padded[:, 1:-1, 1:-1, 2:] - padded[:, 1:-1, 1:-1, :-2])
    convect = center[0:1] * grad_x + center[1:2] * grad_y + center[2:3] * grad_z
    updated = smoothed - advection * convect
    pressure_grad = jnp.stack([grad_x[3], grad_y[3], grad_z[3]])
    return jnp.concatenate([updated[0:3] - advection * pressure_grad, updated[3:4]], 0)


def reference(fluid_state, shell_disp, quad_weights, quad_elements, owner_cells, owner_counts):
    dest_rank = jnp.arange(RANKS, dtype=jnp.int32)[None, :, None]
    cell_ids = jnp.transpose(owner_cells, (1, 0, 2))
    counts_sd = jnp.transpose(owner_counts, (1, 0))
    slot_index = jnp.arange(SLOT, dtype=jnp.int32)[None, None, :]
    live_mask = (slot_index < counts_sd[:, :, None]).astype(jnp.float32)
    brick_x = dest_rank // (N_GY * N_GZ)
    brick_y = (dest_rank // N_GZ) % N_GY
    brick_z = dest_rank % N_GZ
    index_x = brick_x * CX + cell_ids // (CY * CZ)
    index_y = brick_y * CY + (cell_ids // CZ) % CY
    index_z = brick_z * CZ + cell_ids % CZ
    for iteration in range(ITERS):
        padded = jnp.pad(fluid_state, ((0, 0), (1, 1), (1, 1), (1, 1)))
        halfway = sweep_fluid(padded)
        velocity = halfway[0:3, index_x, index_y, index_z]
        shell_vel = shell_disp[:, quad_elements]
        traction = penalty * quad_weights[None] * (velocity - shell_vel) * live_mask[None]
        forcing = jnp.zeros((3, NX, NY, NZ), jnp.float32).at[:, index_x, index_y, index_z].add(traction)
        fluid_state = jnp.concatenate([halfway[0:3] - forcing, halfway[3:4]], 0)
        node_loads = jnp.zeros((3, NSH), jnp.float32).at[:, quad_elements].add(traction)
        shell_disp = shell_disp + relaxation * node_loads
    return fluid_state, shell_disp
```

```python
import functools

import jax
import jax.numpy as jnp
from jax import lax
from jax.experimental import pallas as pl
from jax.experimental.pallas import tpu as pltpu
from jax.sharding import PartitionSpec as P

ITERS = 2

advection = 0.2
penalty = 0.5
relaxation = 0.05
AXES = ("gx", "gy", "gz")
MESH = pl.DeviceIdType.MESH
F32 = jnp.float32
BF16 = jnp.bfloat16


class Place:
    def __init__(self, sizes):
        self.nx, self.ny, self.nz = sizes
        self.plane = self.nx * self.ny
        self.x, self.y, self.z = (lax.axis_index(a) for a in AXES)
        self.p = self.x * self.ny + self.y

    def plane_peer(self, d):
        p = lax.rem(self.p + d, self.plane)
        return p, (lax.div(p, self.ny), lax.rem(p, self.ny), self.z)

    def line_peer(self, d):
        z = lax.rem(self.z + d, self.nz)
        return z, (self.x, self.y, z)

    def greet(self):
        sem = pltpu.get_barrier_semaphore()
        for d in range(1, self.plane):
            pl.semaphore_signal(sem, inc=1, device_id=self.plane_peer(d)[1], device_id_type=MESH)
        for d in range(1, self.nz):
            pl.semaphore_signal(sem, inc=1, device_id=self.line_peer(d)[1], device_id_type=MESH)
        for dx in range(1, self.nx):
            for d in range(1, self.nz):
                pl.semaphore_signal(sem, inc=1, device_id=self.side_peer(dx, d)[1], device_id_type=MESH)

    def meet(self):
        pl.semaphore_wait(pltpu.get_barrier_semaphore(), self.plane - 1 + self.nx * (self.nz - 1))

    def side_peer(self, dx, d):
        x, z = lax.rem(self.x + dx, self.nx), lax.rem(self.z + d, self.nz)
        return z, (x, self.y, z)


def send(src, dst, sems, k, device):
    return post(src, dst, sems.at[0, k], sems.at[1, k], device)


def post(src, dst, send_sem, recv_sem, device):
    return pltpu.make_async_remote_copy(
        src_ref=src, dst_ref=dst, send_sem=send_sem, recv_sem=recv_sem, device_id=device, device_id_type=MESH,
    )


def start_all(copies):
    for c in copies:
        c.start()
    return copies


def wait_all(copies):
    for c in copies:
        c.wait()


def drain(sem, ref):
    pltpu.make_async_copy(ref, ref, sem).wait()


class Halo:
    def __init__(self, here, count, device_of, srcs, dsts, sems):
        self.has = (here > 0, here < count - 1)
        self.copies = []
        for s in (0, 1):
            there = jnp.clip(here + (2 * s - 1), 0, count - 1)
            self.copies.append(send(srcs[s], dsts[1 - s], sems, s, device_of(there)))

    def start(self):
        for s in (0, 1):
            @pl.when(self.has[s])
            def _():
                self.copies[s].start()

    def wait(self):
        for s in (0, 1):
            @pl.when(self.has[s])
            def _():
                self.copies[s].wait_send()
                self.copies[1 - s].wait_recv()


class Sweep:
    def __init__(self, at, half, fx, sx, sxy, ys, yh, zs, zh, sem_x, sem_y, sem_z):
        self.at, self.half, self.fx, self.sx, self.sxy = at, half, fx, sx, sxy
        self.ys, self.yh, self.zs, self.zh = ys, yh, zs, zh
        self.nf, self.bx, self.by, self.bz = half.shape
        bx = self.bx
        self.hx = Halo(at.x, at.nx, lambda x: (x, at.y, at.z),
                       (fx.at[:, 1], fx.at[:, bx]), (fx.at[:, 0], fx.at[:, bx + 1]), sem_x)
        self.hy = Halo(at.y, at.ny, lambda y: (at.x, y, at.z),
                       (ys.at[0], ys.at[1]), (yh.at[0], yh.at[1]), sem_y)
        self.hz = Halo(at.z, at.nz, lambda z: (at.x, at.y, z),
                       (zs.at[0], zs.at[1]), (zh.at[0], zh.at[1]), sem_z)

    def clear_ends(self):
        for s, edge in ((0, 0), (1, self.bx + 1)):
            @pl.when(jnp.logical_not(self.hx.has[s]))
            def _():
                self.fx[:, edge] = jnp.zeros((self.nf, self.by, self.bz), F32)

            @pl.when(jnp.logical_not(self.hy.has[s]))
            def _():
                self.yh[s] = jnp.zeros(self.yh.shape[1:], F32)

            @pl.when(jnp.logical_not(self.hz.has[s]))
            def _():
                self.zh[s] = jnp.zeros(self.zh.shape[1:], F32)

    def start_x(self):
        self.hx.start()

    def x_then_start_y(self):
        self.hx.wait()

        def step(x, _):
            for c in range(self.nf):
                mid = self.fx[c, x + 1]
                s = 0.25 * self.fx[c, x] + 0.5 * mid + 0.25 * self.fx[c, x + 2]
                self.sx[c, x] = s
                row = c * self.bx + x
                self.ys[0, 0, pl.ds(row, 1), :] = mid[0:1]
                self.ys[1, 0, pl.ds(row, 1), :] = mid[self.by - 1:]
                self.ys[0, 1, pl.ds(row, 1), :] = s[0:1]
                self.ys[1, 1, pl.ds(row, 1), :] = s[self.by - 1:]
            return 0

        lax.fori_loop(0, self.bx, step, 0)
        self.hy.start()

    def shift_y(self, tile, c, x, kind):
        sub = lax.broadcasted_iota(jnp.int32, tile.shape, 0)
        row = c * self.bx + x
        lower = jnp.where(sub == 0, self.yh[0, kind, pl.ds(row, 1), :], pltpu.roll(tile, 1, axis=0))
        upper = jnp.where(sub == self.by - 1, self.yh[1, kind, pl.ds(row, 1), :],
                          pltpu.roll(tile, self.by - 1, axis=0))
        return lower, upper

    def y_then_start_z(self):
        self.hy.wait()
        lane = lax.broadcasted_iota(jnp.int32, (self.by, self.zs.shape[2]), 1)
        group = self.nf * self.bx

        def step(x, faces):
            low, high = faces
            for c in range(self.nf):
                tile = self.sx[c, x]
                lower, upper = self.shift_y(tile, c, x, 1)
                s = 0.25 * lower + 0.5 * tile + 0.25 * upper
                self.sxy[c, x] = s
                raw = self.fx[c, x + 1]
                k = c * self.bx + x
                low = jnp.where(lane == k, raw[:, 0:1], low)
                low = jnp.where(lane == k + group, s[:, 0:1], low)
                high = jnp.where(lane == k, raw[:, self.bz - 1:], high)
                high = jnp.where(lane == k + group, s[:, self.bz - 1:], high)
            return low, high

        zero = jnp.zeros(lane.shape, F32)
        low, high = lax.fori_loop(0, self.bx, step, (zero, zero))
        self.zs[0] = low
        self.zs[1] = high
        self.hz.start()

    def finish(self):
        self.hz.wait()
        lane = lax.broadcasted_iota(jnp.int32, (self.by, self.bz), 1)
        width = self.zs.shape[2]
        group = self.nf * self.bx

        def step(x, _):
            turn = lax.rem(width - x, width)
            low, high = (pltpu.roll(self.zh[s], turn, axis=1) for s in (0, 1))

            def shift_z(tile, k):
                lower = jnp.where(lane == 0, low[:, k:k + 1], pltpu.roll(tile, 1, axis=1))
                upper = jnp.where(lane == self.bz - 1, high[:, k:k + 1], pltpu.roll(tile, self.bz - 1, axis=1))
                return lower, upper

            u = [self.fx[c, x + 1] for c in range(3)]
            for c in range(self.nf):
                raw = self.fx[c, x + 1]
                s = self.sxy[c, x]
                lower, upper = shift_z(s, group + c * self.bx)
                smoothed = 0.25 * lower + 0.5 * s + 0.25 * upper
                grad_x = 0.5 * (self.fx[c, x + 2] - self.fx[c, x])
                lower, upper = self.shift_y(raw, c, x, 0)
                grad_y = 0.5 * (upper - lower)
                lower, upper = shift_z(raw, c * self.bx)
                grad_z = 0.5 * (upper - lower)
                self.half[c, x] = smoothed - advection * (u[0] * grad_x + u[1] * grad_y + u[2] * grad_z)
                if c == 3:
                    for v, g in enumerate((grad_x, grad_y, grad_z)):
                        self.half[v, x] = self.half[v, x] - advection * g
            return 0

        lax.fori_loop(0, self.bx, step, 0)


def sweep_scratch(block):
    nf, bx, by, bz = block
    width = -(-2 * nf * bx // 128) * 128
    dma = pltpu.SemaphoreType.DMA((2, 2))
    return [
        pltpu.VMEM((nf, bx + 2, by, bz), F32), pltpu.VMEM(block, F32), pltpu.VMEM(block, F32),
        pltpu.VMEM((2, 2, nf * bx, bz), F32), pltpu.VMEM((2, 2, nf * bx, bz), F32),
        pltpu.VMEM((2, by, width), F32), pltpu.VMEM((2, by, width), F32), dma, dma, dma,
    ]


class Gather:
    def __init__(self, at, piece, line, nodes, sem):
        self.at, self.piece, self.line, self.nodes = at, piece, line, nodes
        self.line_sent, self.plane_sent, self.plane_here = (sem.at[i] for i in range(3))
        self.line_here = [sem.at[3 + d] for d in range(at.nz)]

    def start(self):
        at = self.at
        for d in range(1, at.nz):
            post(self.piece, self.line.at[at.z], self.line_sent, self.line_here[d], at.line_peer(d)[1]).start()

    def own(self):
        self.to_plane(self.piece, self.at.z)

    def to_plane(self, src, z):
        at = self.at
        for d in range(1, at.plane):
            post(src, self.nodes.at[at.p, z], self.plane_sent, self.plane_here, at.plane_peer(d)[1]).start()

    def forward(self):
        at = self.at
        for d in range(1, at.nz):
            z = lax.rem(at.z + at.nz - d, at.nz)
            drain(self.line_here[d], self.line.at[z])
            self.to_plane(self.line.at[z], z)
        self.nodes[at.p, at.z] = self.piece[...]
        for d in range(1, at.nz):
            z = lax.rem(at.z + at.nz - d, at.nz)
            self.nodes[at.p, z] = self.line[z]

    def wait(self):
        at = self.at
        if at.nz > 1:
            drain(self.line_sent, self.line.at[:at.nz - 1])
        if at.plane > 1:
            drain(self.plane_sent, self.nodes.at[:at.plane - 1])
            drain(self.plane_here, self.nodes.at[:at.plane - 1])


class Reduce:
    def __init__(self, at, terms, landed_p, sums, landed_l, sem):
        self.at, self.terms, self.landed_p, self.sums, self.landed_l = at, terms, landed_p, sums, landed_l
        self.plane_sent, self.line_sent, self.line_here = (sem.at[i] for i in range(3))
        self.plane_here = [sem.at[3 + k] for k in range(at.nz)]
        self.order = list(range(1, at.nz)) + [0]

    def start(self):
        at = self.at
        for k in self.order:
            z = lax.rem(at.z + k, at.nz)
            for d in range(1, at.plane):
                p, device = at.plane_peer(d)
                post(self.terms.at[p, z], self.landed_p.at[k, d - 1], self.plane_sent, self.plane_here[k],
                     device).start()

    def forward(self, spread):
        at = self.at
        self.count = spread * at.nz - 1
        for k in self.order:
            z = lax.rem(at.z + k, at.nz)
            total = self.terms[at.p, z]
            if at.plane > 1:
                drain(self.plane_here[k], self.landed_p.at[k])
            for d in range(1, at.plane):
                total = total + self.landed_p[k, d - 1]
            self.sums[k] = total
            for dx in range(spread):
                if k or dx:
                    post(self.sums.at[k], self.landed_l.at[dx * at.nz + k], self.line_sent, self.line_here,
                         at.side_peer(dx, k)[1]).start()

    def wait(self):
        if self.count:
            drain(self.line_sent, self.landed_l.at[1:self.count + 1])
            drain(self.line_here, self.landed_l.at[1:self.count + 1])
        if self.at.plane > 1:
            drain(self.plane_sent, self.landed_p)

    def total(self, dx):
        nz = self.at.nz
        total = self.sums[0] if dx == 0 else self.landed_l[dx * nz]
        for k in range(1, nz):
            total = total + self.landed_l[dx * nz + k]
        return total


class Couple:
    def __init__(self, sizes, block, cells, records, split, wide, acc_f, acc_n, acc_w, hot_c, hot_n, factor, keep):
        self.sizes = sizes
        self.cells, self.records = cells, records
        self.table, self.wide, self.acc_f, self.acc_n, self.acc_w = split, wide, acc_f, acc_n, acc_w
        self.hot_c, self.hot_n, self.factor, self.keep = hot_c, hot_n, factor, keep
        self.rows, self.lanes = acc_w.shape
        self.size = 3 * self.rows
        self.sources, self.width = cells.shape
        _, self.bx, self.by, self.bz = block
        self.hy = self.by // 2

    def chunks(self, step):
        if self.sources <= 16:
            for q in range(self.sources // 2):
                step(q)
        else:
            pl.loop(0, self.sources // 2)(step)

    def split_store(self, c, value):
        hi = value.astype(BF16)
        self.table[c * self.rows:(c + 1) * self.rows] = hi
        self.table[self.size + c * self.rows:self.size + (c + 1) * self.rows] = (value - hi.astype(F32)).astype(BF16)

    def pieces(self, nodes):
        nx, ny, nz = self.sizes
        comps, pr, pw = nodes.shape[2:]
        lp = min(2, nx)
        rp = nx // lp
        for g in range(nx):
            r0, l0 = (g // lp) * pr, (g % lp) * pw
            for y in range(ny):
                for z in range(nz):
                    for c in range(comps):
                        r = c * self.rows + (y * nz + z) * (rp * pr) + r0
                        yield g * ny + y, z, c, slice(r, r + pr), slice(l0, l0 + pw)

    def both(self, read, q):
        return jnp.concatenate([read(2 * q), read(2 * q + 1)], axis=1)

    def cell(self, q):
        return self.both(lambda i: self.cells[pl.ds(i, 1), :], q)

    def pair(self, i):
        return self.records[i], self.records[i + self.sources]

    def left(self):
        return lax.broadcasted_iota(jnp.int32, (1, self.width), 1) < self.width // 2

    def weight(self, i):
        top, bottom = self.pair(i)
        return jnp.where(self.left(), top, pltpu.roll(bottom, self.width // 2, axis=1))

    def ident(self, i):
        top, bottom = self.pair(i)
        return jnp.where(self.left(), pltpu.roll(top, self.width // 2, axis=1), bottom)

    def hot(self, lane):
        lane_of = lax.broadcasted_iota(jnp.int32, (self.lanes, 2 * self.width), 0)
        return jnp.where(lane_of == lane, 1.0, 0.0).astype(BF16)

    def mask(self, row):
        return lax.broadcasted_iota(jnp.int32, (self.rows, 2 * self.width), 0) == row

    def place_cells(self):
        def step(q):
            cell = self.cell(q)
            y = lax.rem(lax.div(cell, self.bz), self.by)
            x = lax.div(cell, self.by * self.bz)
            self.hot_c[q] = self.hot(lax.div(y, self.hy) * self.bz + lax.rem(cell, self.bz))
            self.keep[q, 0:1] = x * self.hy + lax.rem(y, self.hy)

        self.chunks(step)

    def place_nodes(self):
        total = self.bx * self.by * self.bz

        def step(q):
            node = self.both(self.ident, q).astype(jnp.int32)
            self.hot_n[q] = self.hot(lax.rem(node, self.lanes))
            self.keep[q, 1:2] = lax.div(node, self.lanes)
            self.factor[q] = jnp.where(self.cell(q) < total, penalty * self.both(self.weight, q), 0.0)

        self.chunks(step)

    def cell_place(self, q):
        return self.hot_c[q], self.mask(self.keep[q, 0:1])

    def node_place(self, q):
        return self.hot_n[q], self.mask(self.keep[q, 1:2])

    def find(self, hot, mask):
        found = jnp.dot(self.table[...], hot, preferred_element_type=F32)
        found = found[:self.size] + found[self.size:]
        return [
            jnp.sum(jnp.where(mask, found[c * self.rows:(c + 1) * self.rows], 0.0), axis=0, keepdims=True)
            for c in range(3)
        ]

    def spread(self, hot, mask, terms, acc):
        high = [t.astype(BF16).astype(F32) for t in terms]
        parts = high + [t - h for t, h in zip(terms, high)]
        values = jnp.concatenate([jnp.where(mask, t, 0.0).astype(BF16) for t in parts], axis=0)
        out = lax.dot_general(values, hot, (((1,), (1,)), ((), ())), preferred_element_type=F32)
        n = len(terms) * self.rows
        acc[:n] += out[:n] + out[n:]

    def weights_to_nodes(self, terms):
        self.acc_w[...] = jnp.zeros_like(self.acc_w)

        def step(q):
            hot, mask = self.node_place(q)
            self.spread(hot, mask, [self.factor[q]], self.acc_w)

        self.chunks(step)
        for p, z, c, r, l in self.pieces(terms):
            terms[p, z, c] = self.acc_w[r, l]

    def flow_to_nodes(self, half, terms):
        for c in range(3):
            value = half[c]
            top = value[:, :self.hy].reshape(self.rows, self.bz)
            low = value[:, self.hy:].reshape(self.rows, self.bz)
            self.split_store(c, jnp.concatenate([top, low], axis=1))
        self.acc_n[...] = jnp.zeros_like(self.acc_n)

        def step(q):
            found = self.find(*self.cell_place(q))
            hot, mask = self.node_place(q)
            factor = self.factor[q]
            self.spread(hot, mask, [factor * v for v in found], self.acc_n)

        self.chunks(step)
        for p, z, c, r, l in self.pieces(terms):
            terms[p, z, c] = self.acc_n[r, l]

    def nodes_to_flow(self, nodes, weigh):
        for p, z, c, r, l in self.pieces(nodes):
            self.wide[r, l] = nodes[p, z, c]
        for c in range(3):
            self.split_store(c, self.wide[c * self.rows:(c + 1) * self.rows])
        self.acc_f[...] = jnp.zeros_like(self.acc_f)

        def step(q):
            found = self.find(*self.node_place(q))
            hot, mask = self.cell_place(q)
            factor = self.factor[q]
            terms = [factor * s for s in found] + ([factor] if weigh else [])
            self.spread(hot, mask, terms, self.acc_f)

        self.chunks(step)
        if weigh:
            self.acc_w[...] = 1.0 - self.acc_f[self.size:]

    def push(self, half, fluid, first):
        bx, hy, bz = self.bx, self.hy, self.bz
        rest = self.acc_w[...]
        for c in range(3):
            force = self.acc_f[c * self.rows:(c + 1) * self.rows]
            for s in (0, 1):
                y, l = slice(s * hy, (s + 1) * hy), slice(s * bz, (s + 1) * bz)
                fluid[c, first:first + bx, y] = (
                    half[c, :, y] * rest[:, l].reshape(bx, hy, bz) + force[:, l].reshape(bx, hy, bz))
        fluid[3, first:first + bx] = half[3]


def prepare(sizes, shell_raw, weights, elements, owned, counts, shell, rec, cells, joined, total):
    nx, _, nz = sizes
    pr, pw = shell.shape[2:]
    lp = min(2, nx)
    for g in range(nx):
        for r in range(pr):
            m = ((g // lp) * pr + r) * lp * pw + (g % lp) * pw
            for c in range(3):
                shell[g, c, r:r + 1, :] = shell_raw[c:c + 1, m:m + pw]
    ranks, slots = weights.shape[1:]
    joined[:, :slots] = weights[0]
    joined[:, slots:] = elements[0].astype(F32)
    for i in range(ranks):
        rec[i // nz, i % nz] = joined[i:i + 1, :]
    same = lax.broadcasted_iota(jnp.int32, (ranks, ranks), 0) == lax.broadcasted_iota(jnp.int32, (ranks, ranks), 1)
    count = jnp.sum(jnp.where(same, counts[...].astype(F32), 0.0), axis=1, keepdims=True)
    slot = lax.broadcasted_iota(jnp.int32, (ranks, slots), 1).astype(F32)
    value = jnp.where(slot < count, owned[0], total)
    cells[:, :slots] = value[:ranks // 2]
    cells[:, slots:] = value[ranks // 2:]


def whole_kernel(sizes, fluid_in, shell_in, weights_in, elements_in, owned_in, counts_in, fluid, out, *refs):
    refs = list(refs)
    take = lambda n: [refs.pop(0) for _ in range(n)]
    raw = take(5)
    joined, shell, rec, cells, sem_in = take(5)
    line0, line1, nodes0, nodes1, rec_line, records = take(6)
    half, = take(1)
    terms0, terms1, terms_w = take(3)
    reduce0, reduce1, reduce_w = take(3), take(3), take(3)
    mine, last, result = take(3)
    sem_r, sem_g0, sem_g1, sem_a0, sem_a1, sem_aw = take(6)
    couple_refs = take(9)
    sweep_refs = take(10), take(10)
    at = Place(sizes)
    at.greet()
    first, second = [Sweep(at, half, *r) for r in sweep_refs]
    _, bx, by, bz = half.shape
    here = sweep_refs[0][0].at[:, 1:bx + 1]
    fetches = start_all([pltpu.make_async_copy(fluid_in, here, sem_in.at[0])])
    pairs = list(zip((shell_in, weights_in, elements_in, owned_in, counts_in), raw))
    fetches += start_all([pltpu.make_async_copy(src, dst, sem_in.at[i + 1]) for i, (src, dst) in enumerate(pairs)])
    for sweep in (first, second):
        sweep.clear_ends()
    wait_all(fetches)
    prepare(sizes, *raw, shell, rec, cells, joined, bx * by * bz)
    at.meet()
    couple = Couple(sizes, half.shape, cells, RecordRows(records), *couple_refs)
    gather = Gather(at, shell.at[at.x], line0, nodes0, sem_g0)
    first.start_x()
    for d in range(1, at.nz):
        z, device = at.line_peer(d)
        post(rec.at[:, z], rec_line.at[at.z], sem_r.at[0], sem_r.at[1], device).start()
    gather.start()
    rec_line[at.z] = rec[:, at.z]
    couple.place_cells()
    first.x_then_start_y()
    gather.own()
    if at.nz > 1:
        drain(sem_r.at[0], rec_line.at[:at.nz - 1])
        drain(sem_r.at[1], rec_line.at[:at.nz - 1])
    for d in range(1, at.plane):
        p, device = at.plane_peer(d)
        post(rec_line.at[:, p], records.at[at.p], sem_r.at[2], sem_r.at[3], device).start()
    gather.forward()
    records[at.p] = rec_line[:, at.p]
    first.y_then_start_z()
    if at.plane > 1:
        drain(sem_r.at[2], records.at[:at.plane - 1])
        drain(sem_r.at[3], records.at[:at.plane - 1])
    couple.place_nodes()
    couple.weights_to_nodes(terms_w)
    weigh = Reduce(at, terms_w, *reduce_w, sem_aw)
    weigh.start()
    first.finish()
    couple.flow_to_nodes(half, terms0)
    loads = Reduce(at, terms0, *reduce0, sem_a0)
    loads.start()
    gather.wait()
    couple.nodes_to_flow(nodes0, True)
    couple.push(half, second.fx, 1)
    second.start_x()
    weigh.forward(at.nx)
    loads.forward(1)
    second.x_then_start_y()
    weigh.wait()
    loads.wait()
    mine[...] = shell[at.x] * (1.0 - relaxation * weigh.total(0)) + relaxation * loads.total(0)
    gather = Gather(at, mine, line1, nodes1, sem_g1)
    gather.start()
    gather.own()
    second.y_then_start_z()
    gather.forward()
    second.finish()
    couple.flow_to_nodes(half, terms1)
    loads = Reduce(at, terms1, *reduce1, sem_a1)
    loads.start()
    gather.wait()
    couple.nodes_to_flow(nodes1, False)
    couple.push(half, result, 0)
    leave = pltpu.make_async_copy(result, fluid, sem_in.at[0])
    leave.start()
    loads.forward(at.nx)
    loads.wait()
    for dx in range(at.nx):
        x = lax.rem(at.x + at.nx - dx, at.nx)
        last[x] = (nodes1[x * at.ny + at.y, at.z] * (1.0 - relaxation * weigh.total(dx))
                   + relaxation * loads.total(dx))
    pr, pw = shell.shape[2:]
    lp = min(2, at.nx)
    for g in range(at.nx):
        for r in range(pr):
            m = ((g // lp) * pr + r) * lp * pw + (g % lp) * pw
            for c in range(3):
                out[c:c + 1, m:m + pw] = last[g, c, r:r + 1, :]
    leave.wait()


class RecordRows:
    def __init__(self, records):
        self.records, self.nz = records, records.shape[1]

    def __getitem__(self, i):
        if isinstance(i, int):
            return self.records[i // self.nz, i % self.nz]
        return self.records[lax.div(i, self.nz), lax.rem(i, self.nz)]


def on_device(sizes, fluid_state, shell_disp, quad_weights, quad_elements, owner_cells, owner_counts):
    nx, ny, nz = sizes
    plane = nx * ny
    slots = quad_weights.shape[2]
    ranks = quad_weights.shape[1]
    block = fluid_state.shape
    nodes_here = shell_disp.shape[1]
    lanes = 2 * block[3]
    lp = min(2, nx)
    rp = nx // lp
    pr, pw = nodes_here // lanes // rp, lanes // lp
    piece = (3, pr, pw)
    rec_shape = (plane, nz, 1, 2 * slots)
    shell_shape = (nx,) + piece
    i32 = lambda s: pltpu.VMEM(s, jnp.int32)

    shape = lambda s: jax.ShapeDtypeStruct(s, F32)
    buf = lambda s: pltpu.VMEM(s, F32)
    line = (nz,) + piece
    full = (plane,) + line
    thin = (1, pr, pw)
    sem = lambda n: pltpu.SemaphoreType.DMA((n,))

    def reduce_scratch(spread, item):
        return [buf((nz, max(plane - 1, 1)) + item), buf((nz,) + item), buf((spread * nz,) + item)]

    rows = ny * nz * rp * pr
    steps = ranks // 4
    scratch = [
        buf(shell_disp.shape), buf(quad_weights.shape), i32(quad_elements.shape), i32(owner_cells.shape),
        i32(owner_counts.shape),
        buf((ranks, 2 * slots)), buf(shell_shape), buf(rec_shape), i32((ranks // 2, 2 * slots)), sem(6),
        buf(line), buf(line), buf(full), buf(full), buf((nz, plane, 1, 2 * slots)), buf(rec_shape),
        buf(block), buf(full), buf(full), buf((plane, nz) + thin),
        *reduce_scratch(1, piece), *reduce_scratch(nx, piece), *reduce_scratch(nx, thin),
        buf(piece), buf(shell_shape), buf(block),
        sem(4), sem(3 + nz), sem(3 + nz), sem(3 + nz), sem(3 + nz), sem(3 + nz),
        pltpu.VMEM((6 * rows, lanes), BF16), buf((3 * rows, lanes)), buf((4 * rows, lanes)), buf((3 * rows, lanes)),
        buf((rows, lanes)), pltpu.VMEM((steps, lanes, 4 * slots), BF16), pltpu.VMEM((steps, lanes, 4 * slots), BF16),
        buf((steps, 1, 4 * slots)), i32((steps, 2, 4 * slots)),
        *sweep_scratch(block), *sweep_scratch(block),
    ]
    anywhere, vmem = pl.BlockSpec(memory_space=pl.ANY), pl.BlockSpec(memory_space=pltpu.VMEM)
    fluid, out = pl.pallas_call(
        functools.partial(whole_kernel, sizes),
        out_shape=(shape(block), shape(shell_disp.shape)),
        in_specs=[anywhere] * 6, out_specs=(anywhere, vmem),
        scratch_shapes=scratch,
        compiler_params=pltpu.CompilerParams(collective_id=0, has_side_effects=True, vmem_limit_bytes=56 << 20),
    )(fluid_state, shell_disp, quad_weights, quad_elements, owner_cells, owner_counts)
    return fluid, out


def solution(mesh):
    sizes = tuple(mesh.shape[a] for a in AXES)
    return jax.shard_map(
        functools.partial(on_device, sizes),
        mesh=mesh,
        in_specs=(
            P(None, "gx", "gy", "gz"),
            P(None, ("gy", "gz")),
            P(("gx", "gy", "gz"), None, None),
            P(("gx", "gy", "gz"), None, None),
            P(("gx", "gy", "gz"), None, None),
            P(("gx", "gy", "gz"), None),
        ),
        out_specs=(P(None, "gx", "gy", "gz"), P(None, ("gy", "gz"))),
        check_vma=False,
    )
```

```python
import functools
import itertools
import math

import jax
import jax.numpy as jnp
from jax import lax
from jax.experimental import pallas as pl
from jax.experimental.pallas import tpu as pltpu
from jax.sharding import PartitionSpec as P

ITERS = 2

advection = 0.2
penalty = 0.5
relaxation = 0.05
AXES = ("gx", "gy", "gz")
MESH = pl.DeviceIdType.MESH
F32 = jnp.float32
BF16 = jnp.bfloat16


class Place:
    def __init__(self, sizes):
        self.nx, self.ny, self.nz = sizes
        self.plane = self.nx * self.ny
        self.x, self.y, self.z = (lax.axis_index(a) for a in AXES)
        self.p = self.x * self.ny + self.y

    def plane_peer(self, d):
        p = lax.rem(self.p + d, self.plane)
        return p, (lax.div(p, self.ny), lax.rem(p, self.ny), self.z)

    def line_peer(self, d):
        z = lax.rem(self.z + d, self.nz)
        return z, (self.x, self.y, z)

    def peers(self):
        yield from (self.plane_peer(d)[1] for d in range(1, self.plane))
        for dx in range(self.nx):
            yield from (self.side_peer(dx, d)[1] for d in range(1, self.nz))

    def corners(self):
        sizes, place = (self.nx, self.ny, self.nz), (self.x, self.y, self.z)
        if self.nz > 1 and self.ny > 1:
            for d in itertools.product((-1, 0, 1), (-1, 1), (-1, 1)):
                if d[0] and self.nx == 1:
                    continue
                there = [p + v for p, v in zip(place, d)]
                ok = functools.reduce(jnp.logical_and, [
                    (t >= 0) if v < 0 else (t < n) for t, n, v in zip(there, sizes, d) if v])
                yield ok, tuple(jnp.clip(t, 0, n - 1) for t, n in zip(there, sizes))

    def greet(self):
        sem = pltpu.get_barrier_semaphore()
        for device in self.peers():
            pl.semaphore_signal(sem, inc=1, device_id=device, device_id_type=MESH)
        for ok, device in self.corners():
            @pl.when(ok)
            def _():
                pl.semaphore_signal(sem, inc=1, device_id=device, device_id_type=MESH)

    def meet(self):
        sem = pltpu.get_barrier_semaphore()
        many = self.plane - 1 + self.nx * (self.nz - 1)
        for ok, _ in self.corners():
            many += jnp.where(ok, 1, 0)
        pl.semaphore_wait(sem, many)

    def side_peer(self, dx, d):
        x, z = lax.rem(self.x + dx, self.nx), lax.rem(self.z + d, self.nz)
        return z, (x, self.y, z)


def send(src, dst, sems, k, device):
    return post(src, dst, sems.at[0, k], sems.at[1, k], device)


def post(src, dst, send_sem, recv_sem, device):
    return pltpu.make_async_remote_copy(
        src_ref=src, dst_ref=dst, send_sem=send_sem, recv_sem=recv_sem, device_id=device, device_id_type=MESH,
    )


def start_all(copies):
    for c in copies:
        c.start()
    return copies


def wait_all(copies):
    for c in copies:
        c.wait()


def drain(sem, ref):
    pltpu.make_async_copy(ref, ref, sem).wait()


class Sweep:
    def __init__(self, at, half, fx, ys, yh, xys, xyh, yb, zs, zh, xzh, yzh, xyzh, sem):
        self.at, self.half, self.fx, self.ys, self.yh, self.xys, self.xyh, self.yb = at, half, fx, ys, yh, xys, xyh, yb
        self.zs, self.zh, self.xzh, self.yzh, self.xyzh, self.sem = zs, zh, xzh, yzh, xyzh, sem
        self.nf, self.bx, self.by, self.bz = half.shape
        self.place = (at.x, at.y, at.z)
        self.sizes = (at.nx, at.ny, at.nz)
        self.kinds = [k for k in itertools.product((0, 1), repeat=3)
                      if any(k) and all(n > 1 for n, on in zip(self.sizes, k) if on)]

    def clear(self):
        for edge in (0, self.bx + 1):
            self.fx[:, edge] = jnp.zeros((self.nf, self.by, self.bz), F32)
        for ref in (self.yh, self.xys, self.xyh, self.zh, self.xzh, self.yzh, self.xyzh):
            ref[...] = jnp.zeros(ref.shape, F32)

    def ends(self, kind, d):
        sx, sy, sz = (int(v > 0) for v in d)
        bx, by = self.bx, self.by
        part = self.zs.at[by - 8:by] if sy else self.zs.at[0:8]
        return {
            (1, 0, 0): lambda: (self.fx.at[:, bx if sx else 1], self.fx.at[:, 0 if sx else bx + 1]),
            (0, 1, 0): lambda: (self.ys.at[sy], self.yh.at[1 - sy]),
            (1, 1, 0): lambda: (self.xys.at[2 * sx + sy], self.xyh.at[2 * (1 - sx) + 1 - sy]),
            (0, 0, 1): lambda: (self.zs, self.zh.at[1 - sz]),
            (1, 0, 1): lambda: (self.zs, self.xzh.at[2 * (1 - sx) + 1 - sz]),
            (0, 1, 1): lambda: (part, self.yzh.at[2 * (1 - sy) + 1 - sz]),
            (1, 1, 1): lambda: (part, self.xyzh.at[4 * (1 - sx) + 2 * (1 - sy) + 1 - sz]),
        }[kind]()

    def units(self, kind, n):
        if kind == (1, 0, 0):
            return self.fx.at[:, :n]
        return {
            (0, 1, 0): self.yh, (1, 1, 0): self.xyh, (0, 0, 1): self.zh,
            (1, 0, 1): self.xzh, (0, 1, 1): self.yzh, (1, 1, 1): self.xyzh,
        }[kind].at[:n]

    def start(self, kinds):
        for kind in kinds:
            if kind not in self.kinds:
                continue
            sems = [self.sem.at[2 * self.kinds.index(kind) + i] for i in (0, 1)]
            for d in itertools.product(*[(-1, 1) if on else (0,) for on in kind]):
                there = [p + v for p, v in zip(self.place, d)]
                ok = functools.reduce(jnp.logical_and, [
                    (t >= 0) if v < 0 else (t < n) for t, n, v in zip(there, self.sizes, d) if v])
                device = tuple(jnp.clip(t, 0, n - 1) for t, n in zip(there, self.sizes))
                src, dst = self.ends(kind, d)
                copy = post(src, dst, *sems, device)

                @pl.when(ok)
                def _():
                    copy.start()

    def wait(self):
        many = [jnp.where(p > 0, 1, 0) + jnp.where(p < n - 1, 1, 0) for p, n in zip(self.place, self.sizes)]
        for i, kind in enumerate(self.kinds):
            counts = [(m, (1,) if n == 2 else (1, 2)) for m, n, on in zip(many, self.sizes, kind) if on]
            for values in itertools.product(*[c for _, c in counts]):
                ref = self.units(kind, math.prod(values))
                ok = functools.reduce(jnp.logical_and, [m == v for (m, _), v in zip(counts, values)])

                @pl.when(ok)
                def _():
                    drain(self.sem.at[2 * i], ref)
                    drain(self.sem.at[2 * i + 1], ref)

    def pack(self):
        pair = lax.broadcasted_iota(jnp.int32, (self.by, self.bz), 1) // 2
        face = jnp.zeros((self.by, self.bz), F32)
        for c in range(self.nf):
            for x in range(self.bx):
                k = c * self.bx + x
                raw = self.fx[c, x + 1]
                face = jnp.where(pair == k, pltpu.roll(raw, (2 * k + 1) % self.bz, axis=1), face)
                for s, y in ((0, 0), (1, self.by - 1)):
                    self.ys[s, k:k + 1] = raw[y:y + 1]
                    if x in (0, self.bx - 1):
                        self.xys[2 * int(x > 0) + s, c:c + 1] = raw[y:y + 1]
        self.zs[...] = face

    def along(self, tile, low, high, axis):
        at = lax.broadcasted_iota(jnp.int32, tile.shape, axis)
        n = tile.shape[axis]
        return (jnp.where(at == 0, low, pltpu.roll(tile, 1, axis=axis)),
                jnp.where(at == n - 1, high, pltpu.roll(tile, n - 1, axis=axis)))

    def side_lines(self):
        for s in (0, 1):
            for c in range(self.nf):
                rows = slice(c * self.bx, (c + 1) * self.bx)
                tile = self.yh[s, rows]
                low, high = self.along(tile, self.xyh[s, c:c + 1], self.xyh[2 + s, c:c + 1], 0)
                self.yb[s, rows] = (low + high) + (tile + tile)

    def z_faces(self):
        def thrice(mid, left, right):
            lane = lax.broadcasted_iota(jnp.int32, mid[0].shape, 1)
            even = lane % 2 == 0
            x = (lane // 2) % self.bx
            mid, left, right = (jnp.where(even, *two) for two in (mid, left, right))
            w = 2 * (self.bx - 1)
            low = jnp.where(x == 0, pltpu.roll(left, self.bz - w, axis=1), pltpu.roll(mid, 2, axis=1))
            high = jnp.where(x == self.bx - 1, pltpu.roll(right, w, axis=1), pltpu.roll(mid, self.bz - 2, axis=1))
            return mid, (low + high) + (mid + mid)

        def ends(tile):
            even = lax.broadcasted_iota(jnp.int32, tile.shape, 1) % 2 == 0
            return jnp.where(even, tile, pltpu.roll(tile, self.bz - 2, axis=1))

        two = lambda ref, i: (ref[i], ref[i + 1])
        raw, face = thrice(two(self.zh, 0), two(self.xzh, 0), two(self.xzh, 2))
        _, low = thrice(two(self.yzh, 0), two(self.xyzh, 0), two(self.xyzh, 4))
        _, high = thrice(two(self.yzh, 2), two(self.xyzh, 2), two(self.xyzh, 6))
        low, high = self.along(face, low[7:8], high[0:1], 0)
        return ends(raw), ends((low + high) + (face + face))

    def finish(self):
        self.side_lines()
        raw_ends, smooth_ends = self.z_faces()
        for x in range(self.bx):
            u = [(0.5 * advection) * self.fx[c, x + 1] for c in range(3)]
            for c in (3, 0, 1, 2):
                k = c * self.bx + x
                below, raw, above = (self.fx[c, x + i] for i in range(3))
                gx = above - below
                s = (below + above) + (raw + raw)
                low, high = self.along(raw, self.yh[0, k:k + 1], self.yh[1, k:k + 1], 0)
                gy = high - low
                low, high = self.along(s, self.yb[0, k:k + 1], self.yb[1, k:k + 1], 0)
                s = (low + high) + (s + s)
                turn = (self.bz - 2 * k) % self.bz
                edge = pltpu.roll(raw_ends, turn, axis=1) if turn else raw_ends
                low, high = self.along(raw, edge, edge, 1)
                gz = high - low
                edge = pltpu.roll(smooth_ends, turn, axis=1) if turn else smooth_ends
                low, high = self.along(s, edge, edge, 1)
                s = (low + high) + (s + s)
                new = s * (1.0 / 64.0) - (u[0] * gx + u[1] * gy + u[2] * gz)
                if c == 3:
                    push = [(0.5 * advection) * g for g in (gx, gy, gz)]
                else:
                    new = new - push[c]
                self.half[c, x] = new


def sweep_scratch(block):
    nf, bx, by, bz = block
    rows = nf * bx
    assert 2 * rows == bz and by >= 8
    buf = lambda *s: pltpu.VMEM(s, F32)
    return [
        buf(nf, bx + 2, by, bz), buf(2, rows, bz), buf(2, rows, bz), buf(4, 8, bz), buf(4, 8, bz), buf(2, rows, bz),
        buf(by, bz), buf(2, by, bz), buf(4, by, bz), buf(4, 8, bz), buf(8, 8, bz), pltpu.SemaphoreType.DMA((14,)),
    ]


class Gather:
    def __init__(self, at, piece, line, nodes, sem):
        self.at, self.piece, self.line, self.nodes = at, piece, line, nodes
        self.line_sent, self.plane_sent, self.plane_here = (sem.at[i] for i in range(3))
        self.line_here = [sem.at[3 + d] for d in range(at.nz)]

    def start(self):
        at = self.at
        for d in range(1, at.nz):
            post(self.piece, self.line.at[at.z], self.line_sent, self.line_here[d], at.line_peer(d)[1]).start()

    def own(self):
        self.to_plane(self.piece, self.at.z)

    def to_plane(self, src, z):
        at = self.at
        for d in range(1, at.plane):
            post(src, self.nodes.at[at.p, z], self.plane_sent, self.plane_here, at.plane_peer(d)[1]).start()

    def forward(self):
        at = self.at
        for d in range(1, at.nz):
            z = lax.rem(at.z + at.nz - d, at.nz)
            drain(self.line_here[d], self.line.at[z])
            self.to_plane(self.line.at[z], z)
        self.nodes[at.p, at.z] = self.piece[...]
        for d in range(1, at.nz):
            z = lax.rem(at.z + at.nz - d, at.nz)
            self.nodes[at.p, z] = self.line[z]

    def wait(self):
        at = self.at
        if at.nz > 1:
            drain(self.line_sent, self.line.at[:at.nz - 1])
        if at.plane > 1:
            drain(self.plane_sent, self.nodes.at[:at.plane - 1])
            drain(self.plane_here, self.nodes.at[:at.plane - 1])


class Reduce:
    def __init__(self, at, terms, landed_p, sums, landed_l, sem):
        self.at, self.terms, self.landed_p, self.sums, self.landed_l = at, terms, landed_p, sums, landed_l
        self.plane_sent, self.line_sent, self.line_here = (sem.at[i] for i in range(3))
        self.plane_here = [sem.at[3 + k] for k in range(at.nz)]
        self.order = list(range(1, at.nz)) + [0]

    def start(self):
        at = self.at
        for k in self.order:
            z = lax.rem(at.z + k, at.nz)
            for d in range(1, at.plane):
                p, device = at.plane_peer(d)
                post(self.terms.at[p, z], self.landed_p.at[k, d - 1], self.plane_sent, self.plane_here[k],
                     device).start()

    def forward(self, spread):
        at = self.at
        self.count = spread * at.nz - 1
        for k in self.order:
            z = lax.rem(at.z + k, at.nz)
            total = self.terms[at.p, z]
            if at.plane > 1:
                drain(self.plane_here[k], self.landed_p.at[k])
            for d in range(1, at.plane):
                total = total + self.landed_p[k, d - 1]
            self.sums[k] = total
            for dx in range(spread):
                if k or dx:
                    post(self.sums.at[k], self.landed_l.at[dx * at.nz + k], self.line_sent, self.line_here,
                         at.side_peer(dx, k)[1]).start()

    def wait(self):
        if self.count:
            drain(self.line_sent, self.landed_l.at[1:self.count + 1])
            drain(self.line_here, self.landed_l.at[1:self.count + 1])
        if self.at.plane > 1:
            drain(self.plane_sent, self.landed_p)

    def total(self, dx):
        nz = self.at.nz
        total = self.sums[0] if dx == 0 else self.landed_l[dx * nz]
        for k in range(1, nz):
            total = total + self.landed_l[dx * nz + k]
        return total


class Couple:
    def __init__(self, sizes, block, cells, records, split, wide, acc_f, acc_n, acc_w, hot_c, hot_n, factor, keep):
        self.sizes = sizes
        self.cells, self.records = cells, records
        self.table, self.wide, self.acc_f, self.acc_n, self.acc_w = split, wide, acc_f, acc_n, acc_w
        self.hot_c, self.hot_n, self.factor, self.keep = hot_c, hot_n, factor, keep
        self.rows, self.lanes = acc_w.shape
        self.size = 3 * self.rows
        self.sources, self.width = cells.shape
        _, self.bx, self.by, self.bz = block
        self.hy = self.by // 2

    def chunks(self, step):
        if self.sources <= 16:
            for q in range(self.sources // 2):
                step(q)
        else:
            pl.loop(0, self.sources // 2)(step)

    def split_store(self, c, value):
        hi = value.astype(BF16)
        self.table[c * self.rows:(c + 1) * self.rows] = hi
        self.table[self.size + c * self.rows:self.size + (c + 1) * self.rows] = (value - hi.astype(F32)).astype(BF16)

    def pieces(self, nodes):
        nx, ny, nz = self.sizes
        comps, pr, pw = nodes.shape[2:]
        lp = min(2, nx)
        rp = nx // lp
        for g in range(nx):
            r0, l0 = (g // lp) * pr, (g % lp) * pw
            for y in range(ny):
                for z in range(nz):
                    for c in range(comps):
                        r = c * self.rows + (y * nz + z) * (rp * pr) + r0
                        yield g * ny + y, z, c, slice(r, r + pr), slice(l0, l0 + pw)

    def both(self, read, q):
        return jnp.concatenate([read(2 * q), read(2 * q + 1)], axis=1)

    def cell(self, q):
        return self.both(lambda i: self.cells[pl.ds(i, 1), :], q)

    def pair(self, i):
        return self.records[i], self.records[i + self.sources]

    def left(self):
        return lax.broadcasted_iota(jnp.int32, (1, self.width), 1) < self.width // 2

    def weight(self, i):
        top, bottom = self.pair(i)
        return jnp.where(self.left(), top, pltpu.roll(bottom, self.width // 2, axis=1))

    def ident(self, i):
        top, bottom = self.pair(i)
        return jnp.where(self.left(), pltpu.roll(top, self.width // 2, axis=1), bottom)

    def hot(self, lane):
        lane_of = lax.broadcasted_iota(jnp.int32, (self.lanes, 2 * self.width), 0)
        return jnp.where(lane_of == lane, 1.0, 0.0).astype(BF16)

    def mask(self, row):
        return lax.broadcasted_iota(jnp.int32, (self.rows, 2 * self.width), 0) == row

    def place_cells(self):
        def step(q):
            cell = self.cell(q)
            y = lax.rem(lax.div(cell, self.bz), self.by)
            x = lax.div(cell, self.by * self.bz)
            self.hot_c[q] = self.hot(lax.div(y, self.hy) * self.bz + lax.rem(cell, self.bz))
            self.keep[q, 0:1] = x * self.hy + lax.rem(y, self.hy)

        self.chunks(step)

    def place_nodes(self):
        total = self.bx * self.by * self.bz

        def step(q):
            node = self.both(self.ident, q).astype(jnp.int32)
            self.hot_n[q] = self.hot(lax.rem(node, self.lanes))
            self.keep[q, 1:2] = lax.div(node, self.lanes)
            self.factor[q] = jnp.where(self.cell(q) < total, penalty * self.both(self.weight, q), 0.0)

        self.chunks(step)

    def cell_place(self, q):
        return self.hot_c[q], self.mask(self.keep[q, 0:1])

    def node_place(self, q):
        return self.hot_n[q], self.mask(self.keep[q, 1:2])

    def find(self, hot, mask):
        found = jnp.dot(self.table[...], hot, preferred_element_type=F32)
        found = found[:self.size] + found[self.size:]
        return [
            jnp.sum(jnp.where(mask, found[c * self.rows:(c + 1) * self.rows], 0.0), axis=0, keepdims=True)
            for c in range(3)
        ]

    def spread(self, hot, mask, terms, acc):
        high = [t.astype(BF16).astype(F32) for t in terms]
        parts = high + [t - h for t, h in zip(terms, high)]
        values = jnp.concatenate([jnp.where(mask, t, 0.0).astype(BF16) for t in parts], axis=0)
        out = lax.dot_general(values, hot, (((1,), (1,)), ((), ())), preferred_element_type=F32)
        n = len(terms) * self.rows
        acc[:n] += out[:n] + out[n:]

    def weights_to_nodes(self, terms):
        self.acc_w[...] = jnp.zeros_like(self.acc_w)

        def step(q):
            hot, mask = self.node_place(q)
            self.spread(hot, mask, [self.factor[q]], self.acc_w)

        self.chunks(step)
        for p, z, c, r, l in self.pieces(terms):
            terms[p, z, c] = self.acc_w[r, l]

    def flow_to_nodes(self, half, terms):
        for c in range(3):
            value = half[c]
            top = value[:, :self.hy].reshape(self.rows, self.bz)
            low = value[:, self.hy:].reshape(self.rows, self.bz)
            self.split_store(c, jnp.concatenate([top, low], axis=1))
        self.acc_n[...] = jnp.zeros_like(self.acc_n)

        def step(q):
            found = self.find(*self.cell_place(q))
            hot, mask = self.node_place(q)
            factor = self.factor[q]
            self.spread(hot, mask, [factor * v for v in found], self.acc_n)

        self.chunks(step)
        for p, z, c, r, l in self.pieces(terms):
            terms[p, z, c] = self.acc_n[r, l]

    def nodes_to_flow(self, nodes, weigh):
        for p, z, c, r, l in self.pieces(nodes):
            self.wide[r, l] = nodes[p, z, c]
        for c in range(3):
            self.split_store(c, self.wide[c * self.rows:(c + 1) * self.rows])
        self.acc_f[...] = jnp.zeros_like(self.acc_f)

        def step(q):
            found = self.find(*self.node_place(q))
            hot, mask = self.cell_place(q)
            factor = self.factor[q]
            terms = [factor * s for s in found] + ([factor] if weigh else [])
            self.spread(hot, mask, terms, self.acc_f)

        self.chunks(step)
        if weigh:
            self.acc_w[...] = 1.0 - self.acc_f[self.size:]

    def push(self, half, fluid, first):
        bx, hy, bz = self.bx, self.hy, self.bz
        rest = self.acc_w[...]
        for c in range(3):
            force = self.acc_f[c * self.rows:(c + 1) * self.rows]
            for s in (0, 1):
                y, l = slice(s * hy, (s + 1) * hy), slice(s * bz, (s + 1) * bz)
                fluid[c, first:first + bx, y] = (
                    half[c, :, y] * rest[:, l].reshape(bx, hy, bz) + force[:, l].reshape(bx, hy, bz))
        fluid[3, first:first + bx] = half[3]


def prepare(sizes, shell_raw, weights, elements, owned, counts, shell, rec, cells, joined, total):
    nx, _, nz = sizes
    pr, pw = shell.shape[2:]
    lp = min(2, nx)
    for g in range(nx):
        for r in range(pr):
            m = ((g // lp) * pr + r) * lp * pw + (g % lp) * pw
            for c in range(3):
                shell[g, c, r:r + 1, :] = shell_raw[c:c + 1, m:m + pw]
    ranks, slots = weights.shape[1:]
    joined[:, :slots] = weights[0]
    joined[:, slots:] = elements[0].astype(F32)
    for i in range(ranks):
        rec[i // nz, i % nz] = joined[i:i + 1, :]
    same = lax.broadcasted_iota(jnp.int32, (ranks, ranks), 0) == lax.broadcasted_iota(jnp.int32, (ranks, ranks), 1)
    count = jnp.sum(jnp.where(same, counts[...].astype(F32), 0.0), axis=1, keepdims=True)
    slot = lax.broadcasted_iota(jnp.int32, (ranks, slots), 1).astype(F32)
    value = jnp.where(slot < count, owned[0], total)
    cells[:, :slots] = value[:ranks // 2]
    cells[:, slots:] = value[ranks // 2:]


FAR = ((1, 1, 1), (0, 1, 1), (1, 0, 1), (0, 0, 1), (1, 1, 0))
NEAR = ((0, 1, 0), (1, 0, 0))


def whole_kernel(sizes, fluid_in, shell_in, weights_in, elements_in, owned_in, counts_in, fluid, out, *refs):
    refs = list(refs)
    take = lambda n: [refs.pop(0) for _ in range(n)]
    raw = take(5)
    joined, shell, rec, cells, sem_in = take(5)
    line0, line1, nodes0, nodes1, rec_line, records = take(6)
    half, = take(1)
    terms0, terms1, terms_w = take(3)
    reduce0, reduce1, reduce_w = take(3), take(3), take(3)
    mine, last, result = take(3)
    sem_r, sem_g0, sem_g1, sem_a0, sem_a1, sem_aw = take(6)
    couple_refs = take(9)
    sweep_refs = take(12), take(12)
    at = Place(sizes)
    first, second = [Sweep(at, half, *r) for r in sweep_refs]
    for sweep in (first, second):
        sweep.clear()
    at.greet()
    _, bx, by, bz = half.shape
    here = sweep_refs[0][0].at[:, 1:bx + 1]
    fetches = start_all([pltpu.make_async_copy(fluid_in, here, sem_in.at[0])])
    pairs = list(zip((shell_in, weights_in, elements_in, owned_in, counts_in), raw))
    fetches += start_all([pltpu.make_async_copy(src, dst, sem_in.at[i + 1]) for i, (src, dst) in enumerate(pairs)])
    fetches.pop(0).wait()
    first.pack()
    at.meet()
    first.start(FAR + NEAR)
    wait_all(fetches)
    prepare(sizes, *raw, shell, rec, cells, joined, bx * by * bz)
    couple = Couple(sizes, half.shape, cells, RecordRows(records), *couple_refs)
    gather = Gather(at, shell.at[at.x], line0, nodes0, sem_g0)
    for d in range(1, at.nz):
        z, device = at.line_peer(d)
        post(rec.at[:, z], rec_line.at[at.z], sem_r.at[0], sem_r.at[1], device).start()
    gather.start()
    rec_line[at.z] = rec[:, at.z]
    couple.place_cells()
    if at.nz > 1:
        drain(sem_r.at[0], rec_line.at[:at.nz - 1])
        drain(sem_r.at[1], rec_line.at[:at.nz - 1])
    for d in range(1, at.plane):
        p, device = at.plane_peer(d)
        post(rec_line.at[:, p], records.at[at.p], sem_r.at[2], sem_r.at[3], device).start()
    records[at.p] = rec_line[:, at.p]
    first.wait()
    gather.own()
    gather.forward()
    first.finish()
    if at.plane > 1:
        drain(sem_r.at[2], records.at[:at.plane - 1])
        drain(sem_r.at[3], records.at[:at.plane - 1])
    couple.place_nodes()
    couple.weights_to_nodes(terms_w)
    weigh = Reduce(at, terms_w, *reduce_w, sem_aw)
    weigh.start()
    couple.flow_to_nodes(half, terms0)
    loads = Reduce(at, terms0, *reduce0, sem_a0)
    loads.start()
    gather.wait()
    couple.nodes_to_flow(nodes0, True)
    couple.push(half, second.fx, 1)
    second.pack()
    second.start(FAR + NEAR)
    weigh.forward(at.nx)
    loads.forward(1)
    weigh.wait()
    loads.wait()
    mine[...] = shell[at.x] * (1.0 - relaxation * weigh.total(0)) + relaxation * loads.total(0)
    gather = Gather(at, mine, line1, nodes1, sem_g1)
    gather.start()
    gather.own()
    second.wait()
    second.finish()
    gather.forward()
    couple.flow_to_nodes(half, terms1)
    loads = Reduce(at, terms1, *reduce1, sem_a1)
    loads.start()
    gather.wait()
    couple.nodes_to_flow(nodes1, False)
    couple.push(half, result, 0)
    leave = pltpu.make_async_copy(result, fluid, sem_in.at[0])
    leave.start()
    loads.forward(at.nx)
    loads.wait()
    for dx in range(at.nx):
        x = lax.rem(at.x + at.nx - dx, at.nx)
        last[x] = (nodes1[x * at.ny + at.y, at.z] * (1.0 - relaxation * weigh.total(dx))
                   + relaxation * loads.total(dx))
    pr, pw = shell.shape[2:]
    lp = min(2, at.nx)
    for g in range(at.nx):
        for r in range(pr):
            m = ((g // lp) * pr + r) * lp * pw + (g % lp) * pw
            for c in range(3):
                out[c:c + 1, m:m + pw] = last[g, c, r:r + 1, :]
    leave.wait()


class RecordRows:
    def __init__(self, records):
        self.records, self.nz = records, records.shape[1]

    def __getitem__(self, i):
        if isinstance(i, int):
            return self.records[i // self.nz, i % self.nz]
        return self.records[lax.div(i, self.nz), lax.rem(i, self.nz)]


def on_device(sizes, fluid_state, shell_disp, quad_weights, quad_elements, owner_cells, owner_counts):
    nx, ny, nz = sizes
    plane = nx * ny
    slots = quad_weights.shape[2]
    ranks = quad_weights.shape[1]
    block = fluid_state.shape
    nodes_here = shell_disp.shape[1]
    lanes = 2 * block[3]
    lp = min(2, nx)
    rp = nx // lp
    pr, pw = nodes_here // lanes // rp, lanes // lp
    piece = (3, pr, pw)
    rec_shape = (plane, nz, 1, 2 * slots)
    shell_shape = (nx,) + piece
    i32 = lambda s: pltpu.VMEM(s, jnp.int32)

    shape = lambda s: jax.ShapeDtypeStruct(s, F32)
    buf = lambda s: pltpu.VMEM(s, F32)
    line = (nz,) + piece
    full = (plane,) + line
    thin = (1, pr, pw)
    sem = lambda n: pltpu.SemaphoreType.DMA((n,))

    def reduce_scratch(spread, item):
        return [buf((nz, max(plane - 1, 1)) + item), buf((nz,) + item), buf((spread * nz,) + item)]

    rows = ny * nz * rp * pr
    steps = ranks // 4
    scratch = [
        buf(shell_disp.shape), buf(quad_weights.shape), i32(quad_elements.shape), i32(owner_cells.shape),
        i32(owner_counts.shape),
        buf((ranks, 2 * slots)), buf(shell_shape), buf(rec_shape), i32((ranks // 2, 2 * slots)), sem(6),
        buf(line), buf(line), buf(full), buf(full), buf((nz, plane, 1, 2 * slots)), buf(rec_shape),
        buf(block), buf(full), buf(full), buf((plane, nz) + thin),
        *reduce_scratch(1, piece), *reduce_scratch(nx, piece), *reduce_scratch(nx, thin),
        buf(piece), buf(shell_shape), buf(block),
        sem(4), sem(3 + nz), sem(3 + nz), sem(3 + nz), sem(3 + nz), sem(3 + nz),
        pltpu.VMEM((6 * rows, lanes), BF16), buf((3 * rows, lanes)), buf((4 * rows, lanes)), buf((3 * rows, lanes)),
        buf((rows, lanes)), pltpu.VMEM((steps, lanes, 4 * slots), BF16), pltpu.VMEM((steps, lanes, 4 * slots), BF16),
        buf((steps, 1, 4 * slots)), i32((steps, 2, 4 * slots)),
        *sweep_scratch(block), *sweep_scratch(block),
    ]
    anywhere, vmem = pl.BlockSpec(memory_space=pl.ANY), pl.BlockSpec(memory_space=pltpu.VMEM)
    fluid, out = pl.pallas_call(
        functools.partial(whole_kernel, sizes),
        out_shape=(shape(block), shape(shell_disp.shape)),
        in_specs=[anywhere] * 6, out_specs=(anywhere, vmem),
        scratch_shapes=scratch,
        compiler_params=pltpu.CompilerParams(collective_id=0, has_side_effects=True, vmem_limit_bytes=56 << 20),
    )(fluid_state, shell_disp, quad_weights, quad_elements, owner_cells, owner_counts)
    return fluid, out


def solution(mesh):
    sizes = tuple(mesh.shape[a] for a in AXES)
    return jax.shard_map(
        functools.partial(on_device, sizes),
        mesh=mesh,
        in_specs=(
            P(None, "gx", "gy", "gz"),
            P(None, ("gy", "gz")),
            P(("gx", "gy", "gz"), None, None),
            P(("gx", "gy", "gz"), None, None),
            P(("gx", "gy", "gz"), None, None),
            P(("gx", "gy", "gz"), None),
        ),
        out_specs=(P(None, "gx", "gy", "gz"), P(None, ("gy", "gz"))),
        check_vma=False,
    )
```

```python
import functools
import itertools
import math

import jax
import jax.numpy as jnp
from jax import lax
from jax.experimental import pallas as pl
from jax.experimental.pallas import tpu as pltpu
from jax.sharding import PartitionSpec as P

ITERS = 2

advection = 0.2
penalty = 0.5
relaxation = 0.05
AXES = ("gx", "gy", "gz")
MESH = pl.DeviceIdType.MESH
F32 = jnp.float32
BF16 = jnp.bfloat16


class Place:
    def __init__(self, sizes):
        self.nx, self.ny, self.nz = sizes
        self.plane = self.nx * self.ny
        self.x, self.y, self.z = (lax.axis_index(a) for a in AXES)
        self.p = self.x * self.ny + self.y
        assert self.ny % 2 == 0
        self.half, self.yc, self.par = self.ny // 2, lax.div(self.y, 2), lax.rem(self.y, 2)
        self.team, self.h = self.nx * self.half, self.x * self.half + self.yc
        self.mate = (self.x, self.y + 1 - 2 * self.par, self.z)

    def team_peer(self, d):
        h = lax.rem(self.h + d, self.team)
        return h, (lax.div(h, self.half), 2 * lax.rem(h, self.half) + self.par, self.z)

    def plane_peer(self, d):
        p = lax.rem(self.p + d, self.plane)
        return p, (lax.div(p, self.ny), lax.rem(p, self.ny), self.z)

    def line_peer(self, d):
        z = lax.rem(self.z + d, self.nz)
        return z, (self.x, self.y, z)

    def peers(self):
        yield from (self.plane_peer(d)[1] for d in range(1, self.plane))
        for dx in range(self.nx):
            yield from (self.side_peer(dx, d)[1] for d in range(1, self.nz))

    def corners(self):
        sizes, place = (self.nx, self.ny, self.nz), (self.x, self.y, self.z)
        if self.nz > 1 and self.ny > 1:
            for d in itertools.product((-1, 0, 1), (-1, 1), (-1, 1)):
                if d[0] and self.nx == 1:
                    continue
                there = [p + v for p, v in zip(place, d)]
                ok = functools.reduce(jnp.logical_and, [
                    (t >= 0) if v < 0 else (t < n) for t, n, v in zip(there, sizes, d) if v])
                yield ok, tuple(jnp.clip(t, 0, n - 1) for t, n in zip(there, sizes))

    def greet(self):
        sem = pltpu.get_barrier_semaphore()
        for device in self.peers():
            pl.semaphore_signal(sem, inc=1, device_id=device, device_id_type=MESH)
        for ok, device in self.corners():
            @pl.when(ok)
            def _():
                pl.semaphore_signal(sem, inc=1, device_id=device, device_id_type=MESH)

    def meet(self):
        sem = pltpu.get_barrier_semaphore()
        many = self.plane - 1 + self.nx * (self.nz - 1)
        for ok, _ in self.corners():
            many += jnp.where(ok, 1, 0)
        pl.semaphore_wait(sem, many)

    def side_peer(self, dx, d):
        x, z = lax.rem(self.x + dx, self.nx), lax.rem(self.z + d, self.nz)
        return z, (x, self.y, z)


def send(src, dst, sems, k, device):
    return post(src, dst, sems.at[0, k], sems.at[1, k], device)


def post(src, dst, send_sem, recv_sem, device):
    return pltpu.make_async_remote_copy(
        src_ref=src, dst_ref=dst, send_sem=send_sem, recv_sem=recv_sem, device_id=device, device_id_type=MESH,
    )


def start_all(copies):
    for c in copies:
        c.start()
    return copies


def wait_all(copies):
    for c in copies:
        c.wait()


def drain(sem, ref):
    pltpu.make_async_copy(ref, ref, sem).wait()


class Sweep:
    def __init__(self, at, half, fx, ys, yh, xys, xyh, yb, zs, zh, xzh, yzh, xyzh, sem):
        self.at, self.half, self.fx, self.ys, self.yh, self.xys, self.xyh, self.yb = at, half, fx, ys, yh, xys, xyh, yb
        self.zs, self.zh, self.xzh, self.yzh, self.xyzh, self.sem = zs, zh, xzh, yzh, xyzh, sem
        self.nf, self.bx, self.by, self.bz = half.shape
        self.place = (at.x, at.y, at.z)
        self.sizes = (at.nx, at.ny, at.nz)
        self.kinds = [k for k in itertools.product((0, 1), repeat=3)
                      if any(k) and all(n > 1 for n, on in zip(self.sizes, k) if on)]

    def clear(self):
        for edge in (0, self.bx + 1):
            self.fx[:, edge] = jnp.zeros((self.nf, self.by, self.bz), F32)
        for ref in (self.yh, self.xys, self.xyh, self.zh, self.xzh, self.yzh, self.xyzh):
            ref[...] = jnp.zeros(ref.shape, F32)

    def ends(self, kind, d):
        sx, sy, sz = (int(v > 0) for v in d)
        bx, by = self.bx, self.by
        part = self.zs.at[by - 8:by] if sy else self.zs.at[0:8]
        return {
            (1, 0, 0): lambda: (self.fx.at[:, bx if sx else 1], self.fx.at[:, 0 if sx else bx + 1]),
            (0, 1, 0): lambda: (self.ys.at[sy], self.yh.at[1 - sy]),
            (1, 1, 0): lambda: (self.xys.at[2 * sx + sy], self.xyh.at[2 * (1 - sx) + 1 - sy]),
            (0, 0, 1): lambda: (self.zs, self.zh.at[1 - sz]),
            (1, 0, 1): lambda: (self.zs, self.xzh.at[2 * (1 - sx) + 1 - sz]),
            (0, 1, 1): lambda: (part, self.yzh.at[2 * (1 - sy) + 1 - sz]),
            (1, 1, 1): lambda: (part, self.xyzh.at[4 * (1 - sx) + 2 * (1 - sy) + 1 - sz]),
        }[kind]()

    def units(self, kind, n):
        if kind == (1, 0, 0):
            return self.fx.at[:, :n]
        return {
            (0, 1, 0): self.yh, (1, 1, 0): self.xyh, (0, 0, 1): self.zh,
            (1, 0, 1): self.xzh, (0, 1, 1): self.yzh, (1, 1, 1): self.xyzh,
        }[kind].at[:n]

    def start(self, kinds):
        for kind in kinds:
            if kind not in self.kinds:
                continue
            sems = [self.sem.at[2 * self.kinds.index(kind) + i] for i in (0, 1)]
            for d in itertools.product(*[(-1, 1) if on else (0,) for on in kind]):
                there = [p + v for p, v in zip(self.place, d)]
                ok = functools.reduce(jnp.logical_and, [
                    (t >= 0) if v < 0 else (t < n) for t, n, v in zip(there, self.sizes, d) if v])
                device = tuple(jnp.clip(t, 0, n - 1) for t, n in zip(there, self.sizes))
                src, dst = self.ends(kind, d)
                copy = post(src, dst, *sems, device)

                @pl.when(ok)
                def _():
                    copy.start()

    def wait(self):
        many = [jnp.where(p > 0, 1, 0) + jnp.where(p < n - 1, 1, 0) for p, n in zip(self.place, self.sizes)]
        for i, kind in enumerate(self.kinds):
            counts = [(m, (1,) if n == 2 else (1, 2)) for m, n, on in zip(many, self.sizes, kind) if on]
            for values in itertools.product(*[c for _, c in counts]):
                ref = self.units(kind, math.prod(values))
                ok = functools.reduce(jnp.logical_and, [m == v for (m, _), v in zip(counts, values)])

                @pl.when(ok)
                def _():
                    drain(self.sem.at[2 * i], ref)
                    drain(self.sem.at[2 * i + 1], ref)

    def pack(self):
        pair = lax.broadcasted_iota(jnp.int32, (self.by, self.bz), 1) // 2
        face = jnp.zeros((self.by, self.bz), F32)
        for c in range(self.nf):
            for x in range(self.bx):
                k = c * self.bx + x
                raw = self.fx[c, x + 1]
                face = jnp.where(pair == k, pltpu.roll(raw, (2 * k + 1) % self.bz, axis=1), face)
                for s, y in ((0, 0), (1, self.by - 1)):
                    self.ys[s, k:k + 1] = raw[y:y + 1]
                    if x in (0, self.bx - 1):
                        self.xys[2 * int(x > 0) + s, c:c + 1] = raw[y:y + 1]
        self.zs[...] = face

    def along(self, tile, low, high, axis):
        at = lax.broadcasted_iota(jnp.int32, tile.shape, axis)
        n = tile.shape[axis]
        return (jnp.where(at == 0, low, pltpu.roll(tile, 1, axis=axis)),
                jnp.where(at == n - 1, high, pltpu.roll(tile, n - 1, axis=axis)))

    def side_lines(self):
        for s in (0, 1):
            for c in range(self.nf):
                rows = slice(c * self.bx, (c + 1) * self.bx)
                tile = self.yh[s, rows]
                low, high = self.along(tile, self.xyh[s, c:c + 1], self.xyh[2 + s, c:c + 1], 0)
                self.yb[s, rows] = (low + high) + (tile + tile)

    def z_faces(self):
        def thrice(mid, left, right):
            lane = lax.broadcasted_iota(jnp.int32, mid[0].shape, 1)
            even = lane % 2 == 0
            x = (lane // 2) % self.bx
            mid, left, right = (jnp.where(even, *two) for two in (mid, left, right))
            w = 2 * (self.bx - 1)
            low = jnp.where(x == 0, pltpu.roll(left, self.bz - w, axis=1), pltpu.roll(mid, 2, axis=1))
            high = jnp.where(x == self.bx - 1, pltpu.roll(right, w, axis=1), pltpu.roll(mid, self.bz - 2, axis=1))
            return mid, (low + high) + (mid + mid)

        def ends(tile):
            even = lax.broadcasted_iota(jnp.int32, tile.shape, 1) % 2 == 0
            return jnp.where(even, tile, pltpu.roll(tile, self.bz - 2, axis=1))

        two = lambda ref, i: (ref[i], ref[i + 1])
        raw, face = thrice(two(self.zh, 0), two(self.xzh, 0), two(self.xzh, 2))
        _, low = thrice(two(self.yzh, 0), two(self.xyzh, 0), two(self.xyzh, 4))
        _, high = thrice(two(self.yzh, 2), two(self.xyzh, 2), two(self.xyzh, 6))
        low, high = self.along(face, low[7:8], high[0:1], 0)
        return ends(raw), ends((low + high) + (face + face))

    def finish(self):
        self.side_lines()
        raw_ends, smooth_ends = self.z_faces()
        for x in range(self.bx):
            u = [(0.5 * advection) * self.fx[c, x + 1] for c in range(3)]
            for c in (3, 0, 1, 2):
                k = c * self.bx + x
                below, raw, above = (self.fx[c, x + i] for i in range(3))
                gx = above - below
                s = (below + above) + (raw + raw)
                low, high = self.along(raw, self.yh[0, k:k + 1], self.yh[1, k:k + 1], 0)
                gy = high - low
                low, high = self.along(s, self.yb[0, k:k + 1], self.yb[1, k:k + 1], 0)
                s = (low + high) + (s + s)
                turn = (self.bz - 2 * k) % self.bz
                edge = pltpu.roll(raw_ends, turn, axis=1) if turn else raw_ends
                low, high = self.along(raw, edge, edge, 1)
                gz = high - low
                edge = pltpu.roll(smooth_ends, turn, axis=1) if turn else smooth_ends
                low, high = self.along(s, edge, edge, 1)
                s = (low + high) + (s + s)
                new = s * (1.0 / 64.0) - (u[0] * gx + u[1] * gy + u[2] * gz)
                if c == 3:
                    push = [(0.5 * advection) * g for g in (gx, gy, gz)]
                else:
                    new = new - push[c]
                self.half[c, x] = new


def sweep_scratch(block):
    nf, bx, by, bz = block
    rows = nf * bx
    assert 2 * rows == bz and by >= 8
    buf = lambda *s: pltpu.VMEM(s, F32)
    return [
        buf(nf, bx + 2, by, bz), buf(2, rows, bz), buf(2, rows, bz), buf(4, 8, bz), buf(4, 8, bz), buf(2, rows, bz),
        buf(by, bz), buf(2, by, bz), buf(4, by, bz), buf(4, 8, bz), buf(8, 8, bz), pltpu.SemaphoreType.DMA((14,)),
    ]


class Gather:
    def __init__(self, at, piece, line, nodes, sem):
        self.at, self.piece, self.line, self.nodes = at, piece, line, nodes
        self.line_sent, self.plane_sent, self.plane_here = (sem.at[i] for i in range(3))
        self.line_here = [sem.at[3 + d] for d in range(at.nz)]

    def start(self):
        at = self.at
        for d in range(1, at.nz):
            post(self.piece, self.line.at[at.z], self.line_sent, self.line_here[d], at.line_peer(d)[1]).start()

    def own(self):
        self.nodes[self.at.h, self.at.z] = self.piece[...]
        self.to_plane(self.piece, self.at.z)

    def to_plane(self, src, z):
        at = self.at
        for d in range(1, at.team):
            post(src, self.nodes.at[at.h, z], self.plane_sent, self.plane_here, at.team_peer(d)[1]).start()

    def forward(self, d):
        at = self.at
        z = lax.rem(at.z + at.nz - d, at.nz)
        drain(self.line_here[d], self.line.at[z])
        self.to_plane(self.line.at[z], z)
        self.nodes[at.h, z] = self.line[z]

    def wait(self):
        at = self.at
        if at.nz > 1:
            drain(self.line_sent, self.line.at[:at.nz - 1])
        if at.team > 1:
            drain(self.plane_sent, self.nodes.at[:at.team - 1])
            drain(self.plane_here, self.nodes.at[:at.team - 1])


class Reduce:
    def __init__(self, at, terms, landed_p, sums, landed_l, sem):
        self.at, self.terms, self.landed_p, self.sums, self.landed_l = at, terms, landed_p, sums, landed_l
        self.plane_sent, self.line_sent, self.line_here = (sem.at[i] for i in range(3))
        self.plane_here = [sem.at[3 + k] for k in range(at.nz)]
        self.order = list(range(1, at.nz)) + [0]

    def start(self):
        at = self.at
        for k in self.order:
            z = lax.rem(at.z + k, at.nz)
            for d in range(1, at.team):
                p, device = at.team_peer(d)
                post(self.terms.at[p, z], self.landed_p.at[k, d - 1], self.plane_sent, self.plane_here[k],
                     device).start()

    def forward(self, spread):
        at = self.at
        self.count = spread * at.nz - 1
        for k in self.order:
            z = lax.rem(at.z + k, at.nz)
            total = self.terms[at.h, z]
            if at.team > 1:
                drain(self.plane_here[k], self.landed_p.at[k])
            for d in range(1, at.team):
                total = total + self.landed_p[k, d - 1]
            self.sums[k] = total
            for dx in range(spread):
                if k or dx:
                    post(self.sums.at[k], self.landed_l.at[dx * at.nz + k], self.line_sent, self.line_here,
                         at.side_peer(dx, k)[1]).start()

    def wait(self):
        if self.count:
            drain(self.line_sent, self.landed_l.at[1:self.count + 1])
            drain(self.line_here, self.landed_l.at[1:self.count + 1])
        if self.at.team > 1:
            drain(self.plane_sent, self.landed_p)

    def total(self, dx):
        nz = self.at.nz
        total = self.sums[0] if dx == 0 else self.landed_l[dx * nz]
        for k in range(1, nz):
            total = total + self.landed_l[dx * nz + k]
        return total


class Couple:
    def __init__(self, at, block, cells, records, refs):
        self.at, self.cells, self.records = at, cells, records
        (self.table_c, self.table_n, self.wide, self.acc_f, self.acc_n, self.acc_w, self.rest, self.hot_c, self.hot_n,
         self.factor, self.keep_c, self.keep_n, self.found, self.values) = refs
        self.rows_c, self.lanes = self.rest.shape
        self.rows_n = self.acc_w.shape[0]
        self.sources, self.width = cells.shape[1:]
        _, self.bx, self.by, self.bz = block
        self.hy = self.by // 2
        self.plain = self.sources <= 16

    def chunks(self, step):
        if self.plain:
            for q in range(self.sources // 2):
                step(q)
        else:
            pl.loop(0, self.sources // 2)(step)

    def fresh(self, acc):
        if not self.plain:
            acc[...] = jnp.zeros_like(acc)

    def split_store(self, table, rows, c, value):
        hi = value.astype(BF16)
        table[c * rows:(c + 1) * rows] = hi
        table[(3 + c) * rows:(4 + c) * rows] = (value - hi.astype(F32)).astype(BF16)

    def pieces(self, nodes):
        at = self.at
        comps, pr, pw = nodes.shape[2:]
        lp = min(2, at.nx)
        rp = at.nx // lp
        for g in range(at.nx):
            r0, l0 = (g // lp) * pr, (g % lp) * pw
            for y in range(at.half):
                for z in range(at.nz):
                    for c in range(comps):
                        r = c * self.rows_n + (y * at.nz + z) * (rp * pr) + r0
                        yield g * at.half + y, z, c, slice(r, r + pr), slice(l0, l0 + pw)

    def both(self, read, q):
        return jnp.concatenate([read(2 * q), read(2 * q + 1)], axis=1)

    def cell(self, s, q):
        return self.both(lambda i: self.cells[s, pl.ds(i, 1), :], q)

    def left(self):
        return lax.broadcasted_iota(jnp.int32, (1, self.width), 1) < self.width // 2

    def weight(self, s, i):
        top, bottom = self.records(s, i), self.records(s, i + self.sources)
        return jnp.where(self.left(), top, pltpu.roll(bottom, self.width // 2, axis=1))

    def ident(self, s, i):
        top, bottom = self.records(s, i), self.records(s, i + self.sources)
        return jnp.where(self.left(), pltpu.roll(top, self.width // 2, axis=1), bottom)

    def hot(self, lane):
        lane_of = lax.broadcasted_iota(jnp.int32, (self.lanes, 2 * self.width), 0)
        return jnp.where(lane_of == lane, 1.0, 0.0).astype(BF16)

    def place_cells(self):
        def step(q):
            cell = self.cell(0, q)
            y = lax.rem(lax.div(cell, self.bz), self.by)
            x = lax.div(cell, self.by * self.bz)
            self.hot_c[q] = self.hot(lax.div(y, self.hy) * self.bz + lax.rem(cell, self.bz))
            self.keep_c[q] = x * self.hy + lax.rem(y, self.hy)

        self.chunks(step)

    def place_nodes(self, s):
        total = self.bx * self.by * self.bz
        line = self.rows_n // self.at.half

        def step(q):
            node = self.both(lambda i: self.ident(s, i), q).astype(jnp.int32)
            row = lax.div(node, self.lanes)
            y = lax.div(row, line)
            self.hot_n[s, q] = self.hot(lax.rem(node, self.lanes))
            self.keep_n[s, q] = jnp.where(lax.rem(y, 2) == self.at.par, lax.div(y, 2) * line + lax.rem(row, line), -1)
            weight = self.both(lambda i: self.weight(s, i), q)
            self.factor[s, q] = jnp.where(self.cell(s, q) < total, penalty * weight, 0.0)

        self.chunks(step)

    def find(self, table, rows, hot, row):
        mask = lax.broadcasted_iota(jnp.int32, (rows, 2 * self.width), 0) == row
        found = jnp.dot(table[...], hot, preferred_element_type=F32)
        found = found[:3 * rows] + found[3 * rows:]
        return [
            jnp.sum(jnp.where(mask, found[c * rows:(c + 1) * rows], 0.0), axis=0, keepdims=True) for c in range(3)
        ]

    def spread(self, hot, row, terms, acc, rows, first):
        mask = lax.broadcasted_iota(jnp.int32, (rows, 2 * self.width), 0) == row
        high = [t.astype(BF16).astype(F32) for t in terms]
        parts = high + [t - h for t, h in zip(terms, high)]
        values = jnp.concatenate([jnp.where(mask, t, 0.0).astype(BF16) for t in parts], axis=0)
        out = lax.dot_general(values, hot, (((1,), (1,)), ((), ())), preferred_element_type=F32)
        n = len(terms) * rows
        out = out[:n] + out[n:]
        if first:
            acc[:n] = out
        else:
            acc[:n] += out

    def first(self, q):
        return self.plain and q == 0

    def weights_to_nodes(self, terms):
        self.fresh(self.acc_w)
        for s in (0, 1):
            self.chunks(lambda q: self.spread(self.hot_n[s, q], self.keep_n[s, q], [self.factor[s, q]], self.acc_w,
                                              self.rows_n, s == 0 and self.first(q)))
        for p, z, c, r, l in self.pieces(terms):
            terms[p, z, c] = self.acc_w[r, l]

    def find_cells(self, half):
        for c in range(3):
            value = half[c]
            top = value[:, :self.hy].reshape(self.rows_c, self.bz)
            low = value[:, self.hy:].reshape(self.rows_c, self.bz)
            self.split_store(self.table_c, self.rows_c, c, jnp.concatenate([top, low], axis=1))

        def step(q):
            for c, v in enumerate(self.find(self.table_c, self.rows_c, self.hot_c[q], self.keep_c[q])):
                self.found[q, c:c + 1] = v

        self.chunks(step)

    def swap(self, src, dst, sem):
        copy = post(src, dst, sem.at[0], sem.at[1], self.at.mate)
        copy.start()
        return copy

    def weigh_found(self):
        def step(q):
            self.values[0, q] = self.found[q] * self.factor[0, q]

        self.chunks(step)

    def spread_nodes(self, s, incoming):
        if s == 0:
            self.fresh(self.acc_n)

        def step(q):
            terms = [incoming[q, c:c + 1] for c in range(3)]
            self.spread(self.hot_n[s, q], self.keep_n[s, q], terms, self.acc_n, self.rows_n, s == 0 and self.first(q))

        self.chunks(step)

    def store_terms(self, terms):
        for p, z, c, r, l in self.pieces(terms):
            terms[p, z, c] = self.acc_n[r, l]

    def find_nodes(self, s, outgoing):
        def step(q):
            for c, v in enumerate(self.find(self.table_n, self.rows_n, self.hot_n[s, q], self.keep_n[s, q])):
                outgoing[q, c:c + 1] = v

        self.chunks(step)

    def load_nodes(self, nodes):
        for p, z, c, r, l in self.pieces(nodes):
            self.wide[r, l] = nodes[p, z, c]
        for c in range(3):
            self.split_store(self.table_n, self.rows_n, c, self.wide[c * self.rows_n:(c + 1) * self.rows_n])

    def spread_cells(self, incoming, weigh):
        self.fresh(self.acc_f)

        def step(q):
            factor = self.factor[0, q]
            terms = [factor * (self.found[q, c:c + 1] + incoming[q, c:c + 1]) for c in range(3)]
            terms += [factor] if weigh else []
            self.spread(self.hot_c[q], self.keep_c[q], terms, self.acc_f, self.rows_c, self.first(q))

        self.chunks(step)
        if weigh:
            self.rest[...] = 1.0 - self.acc_f[3 * self.rows_c:]

    def push(self, half, fluid, first):
        bx, hy, bz = self.bx, self.hy, self.bz
        rest = self.rest[...]
        for c in range(3):
            force = self.acc_f[c * self.rows_c:(c + 1) * self.rows_c]
            for s in (0, 1):
                y, l = slice(s * hy, (s + 1) * hy), slice(s * bz, (s + 1) * bz)
                fluid[c, first:first + bx, y] = (
                    half[c, :, y] * rest[:, l].reshape(bx, hy, bz) + force[:, l].reshape(bx, hy, bz))
        fluid[3, first:first + bx] = half[3]


def prepare(sizes, shell_raw, weights, elements, owned, counts, shell, rec, cells, joined, total):
    nx, _, nz = sizes
    pr, pw = shell.shape[2:]
    lp = min(2, nx)
    for g in range(nx):
        for r in range(pr):
            m = ((g // lp) * pr + r) * lp * pw + (g % lp) * pw
            for c in range(3):
                shell[g, c, r:r + 1, :] = shell_raw[c:c + 1, m:m + pw]
    ranks, slots = weights.shape[1:]
    joined[:, :slots] = weights[0]
    joined[:, slots:] = elements[0].astype(F32)
    for i in range(ranks):
        rec[i // nz, i % nz] = joined[i:i + 1, :]
    same = lax.broadcasted_iota(jnp.int32, (ranks, ranks), 0) == lax.broadcasted_iota(jnp.int32, (ranks, ranks), 1)
    count = jnp.sum(jnp.where(same, counts[...].astype(F32), 0.0), axis=1, keepdims=True)
    slot = lax.broadcasted_iota(jnp.int32, (ranks, slots), 1).astype(F32)
    value = jnp.where(slot < count, owned[0], total)
    cells[0, :, :slots] = value[:ranks // 2]
    cells[0, :, slots:] = value[ranks // 2:]


FAR = ((1, 1, 1), (0, 1, 1), (1, 0, 1), (0, 0, 1), (1, 1, 0))
NEAR = ((0, 1, 0), (1, 0, 0))


def whole_kernel(sizes, fluid_in, shell_in, weights_in, elements_in, owned_in, counts_in, fluid, out, *refs):
    refs = list(refs)
    take = lambda n: [refs.pop(0) for _ in range(n)]
    raw = take(5)
    joined, shell, rec, cells, sem_in = take(5)
    line0, line1, nodes0, nodes1, rec_line, records = take(6)
    half, = take(1)
    terms0, terms1, terms_w = take(3)
    reduce0, reduce1, reduce_w = take(3), take(3), take(3)
    mine, last, result = take(3)
    sem_r, sem_g0, sem_g1, sem_a0, sem_a1, sem_aw, sem_m = take(7)
    swapped = take(4)
    couple_refs = take(14)
    sweep_refs = take(12), take(12)
    at = Place(sizes)
    first, second = [Sweep(at, half, *r) for r in sweep_refs]
    for sweep in (first, second):
        sweep.clear()
    at.greet()
    _, bx, by, bz = half.shape
    here = sweep_refs[0][0].at[:, 1:bx + 1]
    fetches = start_all([pltpu.make_async_copy(fluid_in, here, sem_in.at[0])])
    pairs = list(zip((shell_in, weights_in, elements_in, owned_in, counts_in), raw))
    fetches += start_all([pltpu.make_async_copy(src, dst, sem_in.at[i + 1]) for i, (src, dst) in enumerate(pairs)])
    fetches.pop(0).wait()
    first.pack()
    at.meet()
    first.start(FAR + NEAR)
    wait_all(fetches)
    prepare(sizes, *raw, shell, rec, cells, joined, bx * by * bz)
    sems = [sem_m.at[2 * i:2 * i + 2] for i in range(5)]
    read = lambda s, i: records[i // at.nz, i % at.nz, at.par if s == 0 else 1 - at.par]
    couple = Couple(at, half.shape, cells, read, couple_refs)
    gather = Gather(at, shell.at[at.x], line0, nodes0, sem_g0)
    for d in range(1, at.nz):
        z, device = at.line_peer(d)
        post(rec.at[:, z], rec_line.at[at.z], sem_r.at[0], sem_r.at[1], device).start()
    swaps = [couple.swap(cells.at[0], cells.at[1], sems[0])]
    gather.start()
    rec_line[at.z] = rec[:, at.z]
    couple.place_cells()
    if at.nz > 1:
        drain(sem_r.at[0], rec_line.at[:at.nz - 1])
        drain(sem_r.at[1], rec_line.at[:at.nz - 1])
    for d in range(1, at.plane):
        p, device = at.plane_peer(d)
        post(rec_line.at[:, pl.ds(2 * lax.div(p, 2), 2)], records.at[at.p], sem_r.at[2], sem_r.at[3], device).start()
    records[at.p] = rec_line[:, pl.ds(2 * lax.div(at.p, 2), 2)]
    first.wait()
    gather.own()
    first.finish()
    couple.find_cells(half)
    for d in range(1, at.nz):
        gather.forward(d)
    drain(sem_r.at[2], records.at[:at.plane - 1])
    drain(sem_r.at[3], records.at[:at.plane - 1])
    couple.place_nodes(0)
    couple.weigh_found()
    swaps[0].wait()
    swaps = [couple.swap(couple.values.at[0], couple.values.at[1], sems[1])]
    couple.place_nodes(1)
    couple.weights_to_nodes(terms_w)
    weigh = Reduce(at, terms_w, *reduce_w, sem_aw)
    weigh.start()
    couple.spread_nodes(0, couple.values.at[0])
    swaps[0].wait()
    couple.spread_nodes(1, couple.values.at[1])
    couple.store_terms(terms0)
    loads = Reduce(at, terms0, *reduce0, sem_a0)
    loads.start()

    gather.wait()
    couple.load_nodes(nodes0)
    couple.find_nodes(1, swapped[0])
    swaps = [couple.swap(swapped[0], swapped[1], sems[2])]
    couple.find_nodes(0, couple.found)
    swaps[0].wait()
    couple.spread_cells(swapped[1], True)
    couple.push(half, second.fx, 1)
    second.pack()
    second.start(FAR + NEAR)
    weigh.forward(at.nx)
    loads.forward(1)
    weigh.wait()
    loads.wait()
    mine[...] = shell[at.x] * (1.0 - relaxation * weigh.total(0)) + relaxation * loads.total(0)
    gather = Gather(at, mine, line1, nodes1, sem_g1)
    gather.start()
    gather.own()
    second.wait()
    second.finish()
    couple.find_cells(half)
    couple.weigh_found()
    swaps = [couple.swap(couple.values.at[0], couple.values.at[1], sems[3])]
    if at.nz > 1:
        gather.forward(1)
    couple.spread_nodes(0, couple.values.at[0])
    if at.nz > 2:
        gather.forward(2)
    swaps[0].wait()
    couple.spread_nodes(1, couple.values.at[1])
    couple.store_terms(terms1)
    loads = Reduce(at, terms1, *reduce1, sem_a1)
    loads.start()
    for d in range(3, at.nz):
        gather.forward(d)
    gather.wait()
    couple.load_nodes(nodes1)
    couple.find_nodes(1, swapped[2])
    swaps = [couple.swap(swapped[2], swapped[3], sems[4])]
    couple.find_nodes(0, couple.found)
    swaps[0].wait()
    couple.spread_cells(swapped[3], False)
    couple.push(half, result, 0)
    leave = pltpu.make_async_copy(result, fluid, sem_in.at[0])
    leave.start()
    loads.forward(at.nx)
    loads.wait()
    for dx in range(at.nx):
        x = lax.rem(at.x + at.nx - dx, at.nx)
        last[x] = (nodes1[x * at.half + at.yc, at.z] * (1.0 - relaxation * weigh.total(dx))
                   + relaxation * loads.total(dx))
    pr, pw = shell.shape[2:]
    lp = min(2, at.nx)
    for g in range(at.nx):
        for r in range(pr):
            m = ((g // lp) * pr + r) * lp * pw + (g % lp) * pw
            for c in range(3):
                out[c:c + 1, m:m + pw] = last[g, c, r:r + 1, :]
    leave.wait()


def on_device(sizes, fluid_state, shell_disp, quad_weights, quad_elements, owner_cells, owner_counts):
    nx, ny, nz = sizes
    plane = nx * ny
    slots = quad_weights.shape[2]
    ranks = quad_weights.shape[1]
    block = fluid_state.shape
    nodes_here = shell_disp.shape[1]
    lanes = 2 * block[3]
    lp = min(2, nx)
    rp = nx // lp
    pr, pw = nodes_here // lanes // rp, lanes // lp
    piece = (3, pr, pw)
    rec_shape = (plane, nz, 1, 2 * slots)
    shell_shape = (nx,) + piece
    i32 = lambda s: pltpu.VMEM(s, jnp.int32)

    shape = lambda s: jax.ShapeDtypeStruct(s, F32)
    buf = lambda s: pltpu.VMEM(s, F32)
    line = (nz,) + piece
    team = plane // 2
    full = (team,) + line
    thin = (1, pr, pw)
    sem = lambda n: pltpu.SemaphoreType.DMA((n,))

    def reduce_scratch(spread, item):
        return [buf((nz, max(team - 1, 1)) + item), buf((nz,) + item), buf((spread * nz,) + item)]

    rows_n = ny * nz * rp * pr // 2
    rows_c = block[1] * block[2] // 2
    steps, wide = ranks // 4, 4 * slots
    half16 = lambda *s: pltpu.VMEM(s, BF16)
    scratch = [
        buf(shell_disp.shape), buf(quad_weights.shape), i32(quad_elements.shape), i32(owner_cells.shape),
        i32(owner_counts.shape),
        buf((ranks, 2 * slots)), buf(shell_shape), buf(rec_shape), i32((2, ranks // 2, 2 * slots)), sem(6),
        buf(line), buf(line), buf(full), buf(full), buf((nz, plane, 1, 2 * slots)), buf((plane, nz, 2, 1, 2 * slots)),
        buf(block), buf(full), buf(full), buf((team, nz) + thin),
        *reduce_scratch(1, piece), *reduce_scratch(nx, piece), *reduce_scratch(nx, thin),
        buf(piece), buf(shell_shape), buf(block),
        sem(4), sem(3 + nz), sem(3 + nz), sem(3 + nz), sem(3 + nz), sem(3 + nz), sem(10),
        *[buf((steps, 3, wide))] * 4,
        half16(6 * rows_c, lanes), half16(6 * rows_n, lanes), buf((3 * rows_n, lanes)), buf((4 * rows_c, lanes)),
        buf((3 * rows_n, lanes)), buf((rows_n, lanes)), buf((rows_c, lanes)),
        half16(steps, lanes, wide), half16(2, steps, lanes, wide), buf((2, steps, 1, wide)),
        i32((steps, 1, wide)), i32((2, steps, 1, wide)), buf((steps, 3, wide)), buf((2, steps, 3, wide)),
        *sweep_scratch(block), *sweep_scratch(block),
    ]
    anywhere, vmem = pl.BlockSpec(memory_space=pl.ANY), pl.BlockSpec(memory_space=pltpu.VMEM)
    fluid, out = pl.pallas_call(
        functools.partial(whole_kernel, sizes),
        out_shape=(shape(block), shape(shell_disp.shape)),
        in_specs=[anywhere] * 6, out_specs=(anywhere, vmem),
        scratch_shapes=scratch,
        compiler_params=pltpu.CompilerParams(collective_id=0, has_side_effects=True, vmem_limit_bytes=56 << 20),
    )(fluid_state, shell_disp, quad_weights, quad_elements, owner_cells, owner_counts)
    return fluid, out


def solution(mesh):
    sizes = tuple(mesh.shape[a] for a in AXES)
    return jax.shard_map(
        functools.partial(on_device, sizes),
        mesh=mesh,
        in_specs=(
            P(None, "gx", "gy", "gz"),
            P(None, ("gy", "gz")),
            P(("gx", "gy", "gz"), None, None),
            P(("gx", "gy", "gz"), None, None),
            P(("gx", "gy", "gz"), None, None),
            P(("gx", "gy", "gz"), None),
        ),
        out_specs=(P(None, "gx", "gy", "gz"), P(None, ("gy", "gz"))),
        check_vma=False,
    )
```

```python
import functools
import itertools
import math

import jax
import jax.numpy as jnp
from jax import lax
from jax.experimental import pallas as pl
from jax.experimental.pallas import tpu as pltpu
from jax.sharding import PartitionSpec as P

ITERS = 2

advection = 0.2
penalty = 0.5
relaxation = 0.05
AXES = ("gx", "gy", "gz")
MESH = pl.DeviceIdType.MESH
F32 = jnp.float32
BF16 = jnp.bfloat16


class Place:
    def __init__(self, sizes):
        self.nx, self.ny, self.nz = sizes
        self.plane = self.nx * self.ny
        self.x, self.y, self.z = (lax.axis_index(a) for a in AXES)
        self.p = self.x * self.ny + self.y
        assert self.ny % 2 == 0
        self.half, self.yc, self.par = self.ny // 2, lax.div(self.y, 2), lax.rem(self.y, 2)
        self.team, self.h = self.nx * self.half, self.x * self.half + self.yc
        self.mate = (self.x, self.y + 1 - 2 * self.par, self.z)

    def team_peer(self, d):
        h = lax.rem(self.h + d, self.team)
        return h, (lax.div(h, self.half), 2 * lax.rem(h, self.half) + self.par, self.z)

    def plane_peer(self, d):
        p = lax.rem(self.p + d, self.plane)
        return p, (lax.div(p, self.ny), lax.rem(p, self.ny), self.z)

    def line_peer(self, d):
        z = lax.rem(self.z + d, self.nz)
        return z, (self.x, self.y, z)

    def peers(self):
        yield from (self.plane_peer(d)[1] for d in range(1, self.plane))
        for dx in range(self.nx):
            yield from (self.side_peer(dx, d)[1] for d in range(1, self.nz))

    def corners(self):
        sizes, place = (self.nx, self.ny, self.nz), (self.x, self.y, self.z)
        if self.nz > 1 and self.ny > 1:
            for d in itertools.product((-1, 0, 1), (-1, 1), (-1, 1)):
                if d[0] and self.nx == 1:
                    continue
                there = [p + v for p, v in zip(place, d)]
                ok = functools.reduce(jnp.logical_and, [
                    (t >= 0) if v < 0 else (t < n) for t, n, v in zip(there, sizes, d) if v])
                yield ok, tuple(jnp.clip(t, 0, n - 1) for t, n in zip(there, sizes))

    def greet(self):
        sem = pltpu.get_barrier_semaphore()
        for device in self.peers():
            pl.semaphore_signal(sem, inc=1, device_id=device, device_id_type=MESH)
        for ok, device in self.corners():
            @pl.when(ok)
            def _():
                pl.semaphore_signal(sem, inc=1, device_id=device, device_id_type=MESH)

    def meet(self):
        sem = pltpu.get_barrier_semaphore()
        many = self.plane - 1 + self.nx * (self.nz - 1)
        for ok, _ in self.corners():
            many += jnp.where(ok, 1, 0)
        pl.semaphore_wait(sem, many)

    def side_peer(self, dx, d):
        x, z = lax.rem(self.x + dx, self.nx), lax.rem(self.z + d, self.nz)
        return z, (x, self.y, z)


def send(src, dst, sems, k, device):
    return post(src, dst, sems.at[0, k], sems.at[1, k], device)


def post(src, dst, send_sem, recv_sem, device):
    return pltpu.make_async_remote_copy(
        src_ref=src, dst_ref=dst, send_sem=send_sem, recv_sem=recv_sem, device_id=device, device_id_type=MESH,
    )


def start_all(copies):
    for c in copies:
        c.start()
    return copies


def wait_all(copies):
    for c in copies:
        c.wait()


def drain(sem, ref):
    pltpu.make_async_copy(ref, ref, sem).wait()


class Sweep:
    def __init__(self, at, half, fx, ys, yh, xys, xyh, yb, zs, zh, xzh, yzh, xyzh, sem):
        self.at, self.half, self.fx, self.ys, self.yh, self.xys, self.xyh, self.yb = at, half, fx, ys, yh, xys, xyh, yb
        self.zs, self.zh, self.xzh, self.yzh, self.xyzh, self.sem = zs, zh, xzh, yzh, xyzh, sem
        self.nf, self.bx, self.by, self.bz = half.shape
        self.place = (at.x, at.y, at.z)
        self.sizes = (at.nx, at.ny, at.nz)
        self.kinds = [k for k in itertools.product((0, 1), repeat=3)
                      if any(k) and all(n > 1 for n, on in zip(self.sizes, k) if on)]

    def clear(self):
        for edge in (0, self.bx + 1):
            self.fx[:, edge] = jnp.zeros((self.nf, self.by, self.bz), F32)
        for ref in (self.yh, self.xys, self.xyh, self.zh, self.xzh, self.yzh, self.xyzh):
            ref[...] = jnp.zeros(ref.shape, F32)

    def ends(self, kind, d):
        sx, sy, sz = (int(v > 0) for v in d)
        bx, by = self.bx, self.by
        part = self.zs.at[by - 8:by] if sy else self.zs.at[0:8]
        return {
            (1, 0, 0): lambda: (self.fx.at[:, bx if sx else 1], self.fx.at[:, 0 if sx else bx + 1]),
            (0, 1, 0): lambda: (self.ys.at[sy], self.yh.at[1 - sy]),
            (1, 1, 0): lambda: (self.xys.at[2 * sx + sy], self.xyh.at[2 * (1 - sx) + 1 - sy]),
            (0, 0, 1): lambda: (self.zs, self.zh.at[1 - sz]),
            (1, 0, 1): lambda: (self.zs, self.xzh.at[2 * (1 - sx) + 1 - sz]),
            (0, 1, 1): lambda: (part, self.yzh.at[2 * (1 - sy) + 1 - sz]),
            (1, 1, 1): lambda: (part, self.xyzh.at[4 * (1 - sx) + 2 * (1 - sy) + 1 - sz]),
        }[kind]()

    def units(self, kind, n):
        if kind == (1, 0, 0):
            return self.fx.at[:, :n]
        return {
            (0, 1, 0): self.yh, (1, 1, 0): self.xyh, (0, 0, 1): self.zh,
            (1, 0, 1): self.xzh, (0, 1, 1): self.yzh, (1, 1, 1): self.xyzh,
        }[kind].at[:n]

    def start(self, kinds):
        for kind in kinds:
            if kind not in self.kinds:
                continue
            sems = [self.sem.at[2 * self.kinds.index(kind) + i] for i in (0, 1)]
            for d in itertools.product(*[(-1, 1) if on else (0,) for on in kind]):
                there = [p + v for p, v in zip(self.place, d)]
                ok = functools.reduce(jnp.logical_and, [
                    (t >= 0) if v < 0 else (t < n) for t, n, v in zip(there, self.sizes, d) if v])
                device = tuple(jnp.clip(t, 0, n - 1) for t, n in zip(there, self.sizes))
                src, dst = self.ends(kind, d)
                copy = post(src, dst, *sems, device)

                @pl.when(ok)
                def _():
                    copy.start()

    def wait(self):
        many = [jnp.where(p > 0, 1, 0) + jnp.where(p < n - 1, 1, 0) for p, n in zip(self.place, self.sizes)]
        for i, kind in enumerate(self.kinds):
            counts = [(m, (1,) if n == 2 else (1, 2)) for m, n, on in zip(many, self.sizes, kind) if on]
            for values in itertools.product(*[c for _, c in counts]):
                ref = self.units(kind, math.prod(values))
                ok = functools.reduce(jnp.logical_and, [m == v for (m, _), v in zip(counts, values)])

                @pl.when(ok)
                def _():
                    drain(self.sem.at[2 * i], ref)
                    drain(self.sem.at[2 * i + 1], ref)

    def pack(self):
        pair = lax.broadcasted_iota(jnp.int32, (self.by, self.bz), 1) // 2
        face = jnp.zeros((self.by, self.bz), F32)
        for c in range(self.nf):
            for x in range(self.bx):
                k = c * self.bx + x
                raw = self.fx[c, x + 1]
                face = jnp.where(pair == k, pltpu.roll(raw, (2 * k + 1) % self.bz, axis=1), face)
                for s, y in ((0, 0), (1, self.by - 1)):
                    self.ys[s, k:k + 1] = raw[y:y + 1]
                    if x in (0, self.bx - 1):
                        self.xys[2 * int(x > 0) + s, c:c + 1] = raw[y:y + 1]
        self.zs[...] = face

    def along(self, tile, low, high, axis):
        at = lax.broadcasted_iota(jnp.int32, tile.shape, axis)
        n = tile.shape[axis]
        return (jnp.where(at == 0, low, pltpu.roll(tile, 1, axis=axis)),
                jnp.where(at == n - 1, high, pltpu.roll(tile, n - 1, axis=axis)))

    def side_lines(self):
        for s in (0, 1):
            for c in range(self.nf):
                rows = slice(c * self.bx, (c + 1) * self.bx)
                tile = self.yh[s, rows]
                low, high = self.along(tile, self.xyh[s, c:c + 1], self.xyh[2 + s, c:c + 1], 0)
                self.yb[s, rows] = (low + high) + (tile + tile)

    def z_faces(self):
        def thrice(mid, left, right):
            lane = lax.broadcasted_iota(jnp.int32, mid[0].shape, 1)
            even = lane % 2 == 0
            x = (lane // 2) % self.bx
            mid, left, right = (jnp.where(even, *two) for two in (mid, left, right))
            w = 2 * (self.bx - 1)
            low = jnp.where(x == 0, pltpu.roll(left, self.bz - w, axis=1), pltpu.roll(mid, 2, axis=1))
            high = jnp.where(x == self.bx - 1, pltpu.roll(right, w, axis=1), pltpu.roll(mid, self.bz - 2, axis=1))
            return mid, (low + high) + (mid + mid)

        def ends(tile):
            even = lax.broadcasted_iota(jnp.int32, tile.shape, 1) % 2 == 0
            return jnp.where(even, tile, pltpu.roll(tile, self.bz - 2, axis=1))

        two = lambda ref, i: (ref[i], ref[i + 1])
        raw, face = thrice(two(self.zh, 0), two(self.xzh, 0), two(self.xzh, 2))
        _, low = thrice(two(self.yzh, 0), two(self.xyzh, 0), two(self.xyzh, 4))
        _, high = thrice(two(self.yzh, 2), two(self.xyzh, 2), two(self.xyzh, 6))
        low, high = self.along(face, low[7:8], high[0:1], 0)
        return ends(raw), ends((low + high) + (face + face))

    def finish(self):
        self.side_lines()
        raw_ends, smooth_ends = self.z_faces()
        for x in range(self.bx):
            u = [(0.5 * advection) * self.fx[c, x + 1] for c in range(3)]
            for c in (3, 0, 1, 2):
                k = c * self.bx + x
                below, raw, above = (self.fx[c, x + i] for i in range(3))
                gx = above - below
                s = (below + above) + (raw + raw)
                low, high = self.along(raw, self.yh[0, k:k + 1], self.yh[1, k:k + 1], 0)
                gy = high - low
                low, high = self.along(s, self.yb[0, k:k + 1], self.yb[1, k:k + 1], 0)
                s = (low + high) + (s + s)
                turn = (self.bz - 2 * k) % self.bz
                edge = pltpu.roll(raw_ends, turn, axis=1) if turn else raw_ends
                low, high = self.along(raw, edge, edge, 1)
                gz = high - low
                edge = pltpu.roll(smooth_ends, turn, axis=1) if turn else smooth_ends
                low, high = self.along(s, edge, edge, 1)
                s = (low + high) + (s + s)
                new = s * (1.0 / 64.0) - (u[0] * gx + u[1] * gy + u[2] * gz)
                if c == 3:
                    push = [(0.5 * advection) * g for g in (gx, gy, gz)]
                else:
                    new = new - push[c]
                self.half[c, x] = new


def sweep_scratch(block):
    nf, bx, by, bz = block
    rows = nf * bx
    assert 2 * rows == bz and by >= 8
    buf = lambda *s: pltpu.VMEM(s, F32)
    return [
        buf(nf, bx + 2, by, bz), buf(2, rows, bz), buf(2, rows, bz), buf(4, 8, bz), buf(4, 8, bz), buf(2, rows, bz),
        buf(by, bz), buf(2, by, bz), buf(4, by, bz), buf(4, 8, bz), buf(8, 8, bz), pltpu.SemaphoreType.DMA((14,)),
    ]


class Gather:
    def __init__(self, at, piece, line, nodes, sem):
        self.at, self.piece, self.line, self.nodes = at, piece, line, nodes
        self.line_sent, self.plane_sent, self.plane_here = (sem.at[i] for i in range(3))
        self.line_here = [sem.at[3 + d] for d in range(at.nz)]

    def start(self):
        at = self.at
        for d in range(1, at.nz):
            post(self.piece, self.line.at[at.z], self.line_sent, self.line_here[d], at.line_peer(d)[1]).start()

    def own(self):
        self.nodes[self.at.h, self.at.z] = self.piece[...]
        self.to_plane(self.piece, self.at.z)

    def to_plane(self, src, z):
        at = self.at
        for d in range(1, at.team):
            post(src, self.nodes.at[at.h, z], self.plane_sent, self.plane_here, at.team_peer(d)[1]).start()

    def forward(self, d):
        at = self.at
        z = lax.rem(at.z + at.nz - d, at.nz)
        drain(self.line_here[d], self.line.at[z])
        self.to_plane(self.line.at[z], z)
        self.nodes[at.h, z] = self.line[z]

    def wait(self):
        at = self.at
        if at.nz > 1:
            drain(self.line_sent, self.line.at[:at.nz - 1])
        if at.team > 1:
            drain(self.plane_sent, self.nodes.at[:at.team - 1])
            drain(self.plane_here, self.nodes.at[:at.team - 1])


class Reduce:
    def __init__(self, at, terms, landed_p, sums, landed_l, sem):
        self.at, self.terms, self.landed_p, self.sums, self.landed_l = at, terms, landed_p, sums, landed_l
        self.plane_sent, self.line_sent, self.line_here = (sem.at[i] for i in range(3))
        self.plane_here = [sem.at[3 + k] for k in range(at.nz)]
        self.order = list(range(1, at.nz)) + [0]

    def start(self):
        at = self.at
        for k in self.order:
            z = lax.rem(at.z + k, at.nz)
            for d in range(1, at.team):
                p, device = at.team_peer(d)
                post(self.terms.at[p, z], self.landed_p.at[k, d - 1], self.plane_sent, self.plane_here[k],
                     device).start()

    def forward(self, spread):
        at = self.at
        self.count = spread * at.nz - 1
        for k in self.order:
            z = lax.rem(at.z + k, at.nz)
            total = self.terms[at.h, z]
            if at.team > 1:
                drain(self.plane_here[k], self.landed_p.at[k])
            for d in range(1, at.team):
                total = total + self.landed_p[k, d - 1]
            self.sums[k] = total
            for dx in range(spread):
                if k or dx:
                    post(self.sums.at[k], self.landed_l.at[dx * at.nz + k], self.line_sent, self.line_here,
                         at.side_peer(dx, k)[1]).start()

    def wait(self):
        if self.count:
            drain(self.line_sent, self.landed_l.at[1:self.count + 1])
            drain(self.line_here, self.landed_l.at[1:self.count + 1])
        if self.at.team > 1:
            drain(self.plane_sent, self.landed_p)

    def total(self, dx):
        nz = self.at.nz
        total = self.sums[0] if dx == 0 else self.landed_l[dx * nz]
        for k in range(1, nz):
            total = total + self.landed_l[dx * nz + k]
        return total


class Couple:
    def __init__(self, at, block, cells, records, refs):
        self.at, self.cells, self.records = at, cells, records
        (self.table_c, self.table_n, self.wide, self.acc_f, self.acc_n, self.rest, self.hot_c, self.hot_n,
         self.factor, self.keep_c, self.keep_n, self.found, self.values) = refs
        self.rows_c, self.lanes = self.rest.shape
        self.rows_n = self.acc_n.shape[0] // 4
        self.sources, self.width = cells.shape[1:]
        _, self.bx, self.by, self.bz = block
        self.hy = self.by // 2
        self.plain = self.sources <= 16

    def chunks(self, step):
        if self.plain:
            for q in range(self.sources // 2):
                step(q)
        else:
            pl.loop(0, self.sources // 2)(step)

    def fresh(self, acc):
        if not self.plain:
            acc[...] = jnp.zeros_like(acc)

    def split_store(self, table, rows, c, value):
        hi = value.astype(BF16)
        table[c * rows:(c + 1) * rows] = hi
        table[(3 + c) * rows:(4 + c) * rows] = (value - hi.astype(F32)).astype(BF16)

    def pieces(self, nodes):
        at = self.at
        comps, pr, pw = nodes.shape[2:]
        lp = min(2, at.nx)
        rp = at.nx // lp
        for g in range(at.nx):
            r0, l0 = (g // lp) * pr, (g % lp) * pw
            for y in range(at.half):
                for z in range(at.nz):
                    for c in range(comps):
                        r = c * self.rows_n + (y * at.nz + z) * (rp * pr) + r0
                        yield g * at.half + y, z, c, slice(r, r + pr), slice(l0, l0 + pw)

    def both(self, read, q):
        return jnp.concatenate([read(2 * q), read(2 * q + 1)], axis=1)

    def cell(self, s, q):
        return self.both(lambda i: self.cells[s, pl.ds(i, 1), :], q)

    def left(self):
        return lax.broadcasted_iota(jnp.int32, (1, self.width), 1) < self.width // 2

    def weight(self, s, i):
        top, bottom = self.records(s, i), self.records(s, i + self.sources)
        return jnp.where(self.left(), top, pltpu.roll(bottom, self.width // 2, axis=1))

    def ident(self, s, i):
        top, bottom = self.records(s, i), self.records(s, i + self.sources)
        return jnp.where(self.left(), pltpu.roll(top, self.width // 2, axis=1), bottom)

    def hot(self, lane):
        lane_of = lax.broadcasted_iota(jnp.int32, (self.lanes, 2 * self.width), 0)
        return jnp.where(lane_of == lane, 1.0, 0.0).astype(BF16)

    def place_cells(self):
        def step(q):
            cell = self.cell(0, q)
            y = lax.rem(lax.div(cell, self.bz), self.by)
            x = lax.div(cell, self.by * self.bz)
            self.hot_c[q] = self.hot(lax.div(y, self.hy) * self.bz + lax.rem(cell, self.bz))
            self.keep_c[q] = x * self.hy + lax.rem(y, self.hy)

        self.chunks(step)

    def place_nodes(self, s):
        total = self.bx * self.by * self.bz
        line = self.rows_n // self.at.half

        def step(q):
            node = self.both(lambda i: self.ident(s, i), q).astype(jnp.int32)
            row = lax.div(node, self.lanes)
            y = lax.div(row, line)
            self.hot_n[s, q] = self.hot(lax.rem(node, self.lanes))
            self.keep_n[s, q] = jnp.where(lax.rem(y, 2) == self.at.par, lax.div(y, 2) * line + lax.rem(row, line), -1)
            weight = self.both(lambda i: self.weight(s, i), q)
            self.factor[s, q] = jnp.where(self.cell(s, q) < total, penalty * weight, 0.0)

        self.chunks(step)

    def find(self, table, rows, hot, row):
        mask = lax.broadcasted_iota(jnp.int32, (rows, 2 * self.width), 0) == row
        found = jnp.dot(table[...], hot, preferred_element_type=F32)
        found = found[:3 * rows] + found[3 * rows:]
        return [
            jnp.sum(jnp.where(mask, found[c * rows:(c + 1) * rows], 0.0), axis=0, keepdims=True) for c in range(3)
        ]

    def spread(self, hot, row, terms, acc, rows, first):
        mask = lax.broadcasted_iota(jnp.int32, (rows, 2 * self.width), 0) == row
        high = [t.astype(BF16).astype(F32) for t in terms]
        parts = high + [t - h for t, h in zip(terms, high)]
        values = jnp.concatenate([jnp.where(mask, t, 0.0).astype(BF16) for t in parts], axis=0)
        out = lax.dot_general(values, hot, (((1,), (1,)), ((), ())), preferred_element_type=F32)
        n = len(terms) * rows
        out = out[:n] + out[n:]
        if first:
            acc[:n] = out
        else:
            acc[:n] += out

    def first(self, q):
        return self.plain and q == 0

    def find_cells(self, half):
        for c in range(3):
            value = half[c]
            top = value[:, :self.hy].reshape(self.rows_c, self.bz)
            low = value[:, self.hy:].reshape(self.rows_c, self.bz)
            self.split_store(self.table_c, self.rows_c, c, jnp.concatenate([top, low], axis=1))

        def step(q):
            for c, v in enumerate(self.find(self.table_c, self.rows_c, self.hot_c[q], self.keep_c[q])):
                self.found[q, c:c + 1] = v

        self.chunks(step)

    def swap(self, src, dst, sem):
        copy = post(src, dst, sem.at[0], sem.at[1], self.at.mate)
        copy.start()
        return copy

    def weigh_found(self):
        def step(q):
            self.values[0, q] = self.found[q] * self.factor[0, q]

        self.chunks(step)

    def spread_nodes(self, s, incoming, weigh):
        if s == 0:
            self.fresh(self.acc_n)

        def step(q):
            terms = [incoming[q, c:c + 1] for c in range(3)] + ([self.factor[s, q]] if weigh else [])
            self.spread(self.hot_n[s, q], self.keep_n[s, q], terms, self.acc_n, self.rows_n, s == 0 and self.first(q))

        self.chunks(step)

    def store_terms(self, terms):
        for p, z, c, r, l in self.pieces(terms):
            terms[p, z, c] = self.acc_n[r, l]

    def find_nodes(self, s, outgoing):
        def step(q):
            for c, v in enumerate(self.find(self.table_n, self.rows_n, self.hot_n[s, q], self.keep_n[s, q])):
                outgoing[q, c:c + 1] = v

        self.chunks(step)

    def load_nodes(self, nodes):
        for p, z, c, r, l in self.pieces(nodes):
            self.wide[r, l] = nodes[p, z, c]
        for c in range(3):
            self.split_store(self.table_n, self.rows_n, c, self.wide[c * self.rows_n:(c + 1) * self.rows_n])

    def spread_cells(self, incoming, weigh):
        self.fresh(self.acc_f)

        def step(q):
            factor = self.factor[0, q]
            terms = [factor * (self.found[q, c:c + 1] + incoming[q, c:c + 1]) for c in range(3)]
            terms += [factor] if weigh else []
            self.spread(self.hot_c[q], self.keep_c[q], terms, self.acc_f, self.rows_c, self.first(q))

        self.chunks(step)
        if weigh:
            self.rest[...] = 1.0 - self.acc_f[3 * self.rows_c:]

    def push(self, half, fluid, first):
        bx, hy, bz = self.bx, self.hy, self.bz
        rest = self.rest[...]
        for c in range(3):
            force = self.acc_f[c * self.rows_c:(c + 1) * self.rows_c]
            for s in (0, 1):
                y, l = slice(s * hy, (s + 1) * hy), slice(s * bz, (s + 1) * bz)
                fluid[c, first:first + bx, y] = (
                    half[c, :, y] * rest[:, l].reshape(bx, hy, bz) + force[:, l].reshape(bx, hy, bz))
        fluid[3, first:first + bx] = half[3]


def prepare(sizes, shell_raw, weights, elements, owned, counts, shell, rec, cells, joined, total):
    nx, _, nz = sizes
    pr, pw = shell.shape[2:]
    lp = min(2, nx)
    for g in range(nx):
        for r in range(pr):
            m = ((g // lp) * pr + r) * lp * pw + (g % lp) * pw
            for c in range(3):
                shell[g, c, r:r + 1, :] = shell_raw[c:c + 1, m:m + pw]
    ranks, slots = weights.shape[1:]
    joined[:, :slots] = weights[0]
    joined[:, slots:] = elements[0].astype(F32)
    for i in range(ranks):
        rec[i // nz, i % nz] = joined[i:i + 1, :]
    same = lax.broadcasted_iota(jnp.int32, (ranks, ranks), 0) == lax.broadcasted_iota(jnp.int32, (ranks, ranks), 1)
    count = jnp.sum(jnp.where(same, counts[...].astype(F32), 0.0), axis=1, keepdims=True)
    slot = lax.broadcasted_iota(jnp.int32, (ranks, slots), 1).astype(F32)
    value = jnp.where(slot < count, owned[0], total)
    cells[0, :, :slots] = value[:ranks // 2]
    cells[0, :, slots:] = value[ranks // 2:]


FAR = ((1, 1, 1), (0, 1, 1), (1, 0, 1), (0, 0, 1), (1, 1, 0))
NEAR = ((0, 1, 0), (1, 0, 0))


def whole_kernel(sizes, fluid_in, shell_in, weights_in, elements_in, owned_in, counts_in, fluid, out, *refs):
    refs = list(refs)
    take = lambda n: [refs.pop(0) for _ in range(n)]
    raw = take(5)
    joined, shell, rec, cells, sem_in = take(5)
    line0, line1, nodes0, nodes1, rec_line, records = take(6)
    half, = take(1)
    terms0, terms1, ours = take(3)
    reduce0, reduce1 = take(3), take(3)
    mine, last, result = take(3)
    sem_r, sem_g0, sem_g1, sem_a0, sem_a1, sem_w, sem_m = take(7)
    swapped = take(4)
    couple_refs = take(13)
    sweep_refs = take(12), take(12)
    at = Place(sizes)
    first, second = [Sweep(at, half, *r) for r in sweep_refs]
    for sweep in (first, second):
        sweep.clear()
    at.greet()
    _, bx, by, bz = half.shape
    here = sweep_refs[0][0].at[:, 1:bx + 1]
    fetches = start_all([pltpu.make_async_copy(fluid_in, here, sem_in.at[0])])
    pairs = list(zip((shell_in, weights_in, elements_in, owned_in, counts_in), raw))
    fetches += start_all([pltpu.make_async_copy(src, dst, sem_in.at[i + 1]) for i, (src, dst) in enumerate(pairs)])
    fetches.pop(0).wait()
    first.pack()
    at.meet()
    first.start(FAR + NEAR)
    wait_all(fetches)
    prepare(sizes, *raw, shell, rec, cells, joined, bx * by * bz)
    sems = [sem_m.at[2 * i:2 * i + 2] for i in range(5)]
    read = lambda s, i: records[i // at.nz, i % at.nz, at.par if s == 0 else 1 - at.par]
    couple = Couple(at, half.shape, cells, read, couple_refs)
    gather = Gather(at, shell.at[at.x], line0, nodes0, sem_g0)
    for d in range(1, at.nz):
        z, device = at.line_peer(d)
        post(rec.at[:, z], rec_line.at[at.z], sem_r.at[0], sem_r.at[1], device).start()
    swaps = [couple.swap(cells.at[0], cells.at[1], sems[0])]
    gather.start()
    rec_line[at.z] = rec[:, at.z]
    couple.place_cells()
    if at.nz > 1:
        drain(sem_r.at[0], rec_line.at[:at.nz - 1])
        drain(sem_r.at[1], rec_line.at[:at.nz - 1])
    for d in range(1, at.plane):
        p, device = at.plane_peer(d)
        post(rec_line.at[:, pl.ds(2 * lax.div(p, 2), 2)], records.at[at.p], sem_r.at[2], sem_r.at[3], device).start()
    records[at.p] = rec_line[:, pl.ds(2 * lax.div(at.p, 2), 2)]
    first.wait()
    gather.own()
    first.finish()
    couple.find_cells(half)
    for d in range(1, at.nz):
        gather.forward(d)
    drain(sem_r.at[2], records.at[:at.plane - 1])
    drain(sem_r.at[3], records.at[:at.plane - 1])
    couple.place_nodes(0)
    couple.weigh_found()
    swaps[0].wait()
    swaps = [couple.swap(couple.values.at[0], couple.values.at[1], sems[1])]
    couple.place_nodes(1)
    couple.spread_nodes(0, couple.values.at[0], True)
    swaps[0].wait()
    couple.spread_nodes(1, couple.values.at[1], True)
    couple.store_terms(terms0)
    loads = Reduce(at, terms0, *reduce0, sem_a0)
    loads.start()

    gather.wait()
    couple.load_nodes(nodes0)
    couple.find_nodes(1, swapped[0])
    swaps = [couple.swap(swapped[0], swapped[1], sems[2])]
    couple.find_nodes(0, couple.found)
    swaps[0].wait()
    couple.spread_cells(swapped[1], True)
    couple.push(half, second.fx, 1)
    second.pack()
    second.start(FAR + NEAR)
    loads.forward(1)
    loads.wait()
    total = loads.total(0)
    ours[at.x] = 1.0 - relaxation * total[3:]
    mine[...] = shell[at.x] * (1.0 - relaxation * total[3:]) + relaxation * total[:3]
    gather = Gather(at, mine, line1, nodes1, sem_g1)
    gather.start()
    gather.own()
    for dx in range(1, at.nx):
        device = (lax.rem(at.x + dx, at.nx), at.y, at.z)
        post(ours.at[at.x], ours.at[at.x], sem_w.at[0], sem_w.at[1], device).start()
    second.wait()
    if at.nz > 1:
        gather.forward(1)
    second.finish()
    for d in range(2, at.nz):
        gather.forward(d)
    couple.find_cells(half)
    couple.weigh_found()
    swaps = [couple.swap(couple.values.at[0], couple.values.at[1], sems[3])]
    couple.spread_nodes(0, couple.values.at[0], False)
    swaps[0].wait()
    couple.spread_nodes(1, couple.values.at[1], False)
    couple.store_terms(terms1)
    loads = Reduce(at, terms1, *reduce1, sem_a1)
    loads.start()
    gather.wait()
    couple.load_nodes(nodes1)
    couple.find_nodes(1, swapped[2])
    swaps = [couple.swap(swapped[2], swapped[3], sems[4])]
    couple.find_nodes(0, couple.found)
    loads.forward(at.nx)
    swaps[0].wait()
    couple.spread_cells(swapped[3], False)
    couple.push(half, result, 0)
    leave = pltpu.make_async_copy(result, fluid, sem_in.at[0])
    leave.start()
    if at.nx > 1:
        drain(sem_w.at[0], ours.at[:at.nx - 1])
        drain(sem_w.at[1], ours.at[:at.nx - 1])
    loads.wait()
    for dx in range(at.nx):
        x = lax.rem(at.x + at.nx - dx, at.nx)
        last[x] = nodes1[x * at.half + at.yc, at.z] * ours[x] + relaxation * loads.total(dx)
    pr, pw = shell.shape[2:]
    lp = min(2, at.nx)
    for g in range(at.nx):
        for r in range(pr):
            m = ((g // lp) * pr + r) * lp * pw + (g % lp) * pw
            for c in range(3):
                out[c:c + 1, m:m + pw] = last[g, c, r:r + 1, :]
    leave.wait()


def on_device(sizes, fluid_state, shell_disp, quad_weights, quad_elements, owner_cells, owner_counts):
    nx, ny, nz = sizes
    plane = nx * ny
    slots = quad_weights.shape[2]
    ranks = quad_weights.shape[1]
    block = fluid_state.shape
    nodes_here = shell_disp.shape[1]
    lanes = 2 * block[3]
    lp = min(2, nx)
    rp = nx // lp
    pr, pw = nodes_here // lanes // rp, lanes // lp
    piece = (3, pr, pw)
    rec_shape = (plane, nz, 1, 2 * slots)
    shell_shape = (nx,) + piece
    i32 = lambda s: pltpu.VMEM(s, jnp.int32)

    shape = lambda s: jax.ShapeDtypeStruct(s, F32)
    buf = lambda s: pltpu.VMEM(s, F32)
    line = (nz,) + piece
    team = plane // 2
    full = (team,) + line
    four, thin = (4, pr, pw), (1, pr, pw)
    sem = lambda n: pltpu.SemaphoreType.DMA((n,))

    def reduce_scratch(spread, item):
        return [buf((nz, max(team - 1, 1)) + item), buf((nz,) + item), buf((spread * nz,) + item)]

    rows_n = ny * nz * rp * pr // 2
    rows_c = block[1] * block[2] // 2
    steps, wide = ranks // 4, 4 * slots
    half16 = lambda *s: pltpu.VMEM(s, BF16)
    scratch = [
        buf(shell_disp.shape), buf(quad_weights.shape), i32(quad_elements.shape), i32(owner_cells.shape),
        i32(owner_counts.shape),
        buf((ranks, 2 * slots)), buf(shell_shape), buf(rec_shape), i32((2, ranks // 2, 2 * slots)), sem(6),
        buf(line), buf(line), buf(full), buf(full), buf((nz, plane, 1, 2 * slots)), buf((plane, nz, 2, 1, 2 * slots)),
        buf(block), buf((team, nz) + four), buf(full), buf((nx,) + thin),
        *reduce_scratch(1, four), *reduce_scratch(nx, piece),
        buf(piece), buf(shell_shape), buf(block),
        sem(4), sem(3 + nz), sem(3 + nz), sem(3 + nz), sem(3 + nz), sem(2), sem(10),
        *[buf((steps, 3, wide))] * 4,
        half16(6 * rows_c, lanes), half16(6 * rows_n, lanes), buf((3 * rows_n, lanes)), buf((4 * rows_c, lanes)),
        buf((4 * rows_n, lanes)), buf((rows_c, lanes)),
        half16(steps, lanes, wide), half16(2, steps, lanes, wide), buf((2, steps, 1, wide)),
        i32((steps, 1, wide)), i32((2, steps, 1, wide)), buf((steps, 3, wide)), buf((2, steps, 3, wide)),
        *sweep_scratch(block), *sweep_scratch(block),
    ]
    anywhere, vmem = pl.BlockSpec(memory_space=pl.ANY), pl.BlockSpec(memory_space=pltpu.VMEM)
    fluid, out = pl.pallas_call(
        functools.partial(whole_kernel, sizes),
        out_shape=(shape(block), shape(shell_disp.shape)),
        in_specs=[anywhere] * 6, out_specs=(anywhere, vmem),
        scratch_shapes=scratch,
        compiler_params=pltpu.CompilerParams(collective_id=0, has_side_effects=True, vmem_limit_bytes=56 << 20),
    )(fluid_state, shell_disp, quad_weights, quad_elements, owner_cells, owner_counts)
    return fluid, out


def solution(mesh):
    sizes = tuple(mesh.shape[a] for a in AXES)
    return jax.shard_map(
        functools.partial(on_device, sizes),
        mesh=mesh,
        in_specs=(
            P(None, "gx", "gy", "gz"),
            P(None, ("gy", "gz")),
            P(("gx", "gy", "gz"), None, None),
            P(("gx", "gy", "gz"), None, None),
            P(("gx", "gy", "gz"), None, None),
            P(("gx", "gy", "gz"), None),
        ),
        out_specs=(P(None, "gx", "gy", "gz"), P(None, ("gy", "gz"))),
        check_vma=False,
    )
```

```python
import functools
import itertools
import math

import jax
import jax.numpy as jnp
from jax import lax
from jax.experimental import pallas as pl
from jax.experimental.pallas import tpu as pltpu
from jax.sharding import PartitionSpec as P

ITERS = 2

advection = 0.2
penalty = 0.5
relaxation = 0.05
AXES = ("gx", "gy", "gz")
MESH = pl.DeviceIdType.MESH
F32 = jnp.float32
BF16 = jnp.bfloat16


class Place:
    def __init__(self, sizes):
        self.nx, self.ny, self.nz = sizes
        self.plane = self.nx * self.ny
        self.x, self.y, self.z = (lax.axis_index(a) for a in AXES)
        self.p = self.x * self.ny + self.y
        assert self.ny % 2 == 0
        self.half, self.yc, self.par = self.ny // 2, lax.div(self.y, 2), lax.rem(self.y, 2)
        self.team, self.h = self.nx * self.half, self.x * self.half + self.yc
        self.mate = (self.x, self.y + 1 - 2 * self.par, self.z)

    def team_peer(self, d):
        h = lax.rem(self.h + d, self.team)
        return h, (lax.div(h, self.half), 2 * lax.rem(h, self.half) + self.par, self.z)

    def plane_peer(self, d):
        p = lax.rem(self.p + d, self.plane)
        return p, (lax.div(p, self.ny), lax.rem(p, self.ny), self.z)

    def line_peer(self, d):
        z = lax.rem(self.z + d, self.nz)
        return z, (self.x, self.y, z)

    def peers(self):
        yield from (self.plane_peer(d)[1] for d in range(1, self.plane))
        for dx in range(self.nx):
            yield from (self.side_peer(dx, d)[1] for d in range(1, self.nz))

    def corners(self):
        sizes, place = (self.nx, self.ny, self.nz), (self.x, self.y, self.z)
        if self.nz > 1 and self.ny > 1:
            for d in itertools.product((-1, 0, 1), (-1, 1), (-1, 1)):
                if d[0] and self.nx == 1:
                    continue
                there = [p + v for p, v in zip(place, d)]
                ok = functools.reduce(jnp.logical_and, [
                    (t >= 0) if v < 0 else (t < n) for t, n, v in zip(there, sizes, d) if v])
                yield ok, tuple(jnp.clip(t, 0, n - 1) for t, n in zip(there, sizes))

    def greet(self):
        sem = pltpu.get_barrier_semaphore()
        for device in self.peers():
            pl.semaphore_signal(sem, inc=1, device_id=device, device_id_type=MESH)
        for ok, device in self.corners():
            @pl.when(ok)
            def _():
                pl.semaphore_signal(sem, inc=1, device_id=device, device_id_type=MESH)

    def meet(self):
        sem = pltpu.get_barrier_semaphore()
        many = self.plane - 1 + self.nx * (self.nz - 1)
        for ok, _ in self.corners():
            many += jnp.where(ok, 1, 0)
        pl.semaphore_wait(sem, many)

    def side_peer(self, dx, d):
        x, z = lax.rem(self.x + dx, self.nx), lax.rem(self.z + d, self.nz)
        return z, (x, self.y, z)


def send(src, dst, sems, k, device):
    return post(src, dst, sems.at[0, k], sems.at[1, k], device)


def post(src, dst, send_sem, recv_sem, device):
    return pltpu.make_async_remote_copy(
        src_ref=src, dst_ref=dst, send_sem=send_sem, recv_sem=recv_sem, device_id=device, device_id_type=MESH,
    )


def start_all(copies):
    for c in copies:
        c.start()
    return copies


def wait_all(copies):
    for c in copies:
        c.wait()


def drain(sem, ref):
    pltpu.make_async_copy(ref, ref, sem).wait()


class Sweep:
    def __init__(self, at, half, fx, ys, yh, xys, xyh, yb, zs, zh, xzh, yzh, xyzh, sem):
        self.at, self.half, self.fx, self.ys, self.yh, self.xys, self.xyh, self.yb = at, half, fx, ys, yh, xys, xyh, yb
        self.zs, self.zh, self.xzh, self.yzh, self.xyzh, self.sem = zs, zh, xzh, yzh, xyzh, sem
        self.nf, self.bx, self.by, self.bz = half.shape
        self.place = (at.x, at.y, at.z)
        self.sizes = (at.nx, at.ny, at.nz)
        self.kinds = [k for k in itertools.product((0, 1), repeat=3)
                      if any(k) and all(n > 1 for n, on in zip(self.sizes, k) if on)]

    def clear(self):
        for edge in (0, self.bx + 1):
            self.fx[:, edge] = jnp.zeros((self.nf, self.by, self.bz), F32)
        for ref in (self.yh, self.xys, self.xyh, self.zh, self.xzh, self.yzh, self.xyzh):
            ref[...] = jnp.zeros(ref.shape, F32)

    def ends(self, kind, d):
        sx, sy, sz = (int(v > 0) for v in d)
        bx, by = self.bx, self.by
        part = self.zs.at[by - 8:by] if sy else self.zs.at[0:8]
        return {
            (1, 0, 0): lambda: (self.fx.at[:, bx if sx else 1], self.fx.at[:, 0 if sx else bx + 1]),
            (0, 1, 0): lambda: (self.ys.at[sy], self.yh.at[1 - sy]),
            (1, 1, 0): lambda: (self.xys.at[2 * sx + sy], self.xyh.at[2 * (1 - sx) + 1 - sy]),
            (0, 0, 1): lambda: (self.zs, self.zh.at[1 - sz]),
            (1, 0, 1): lambda: (self.zs, self.xzh.at[2 * (1 - sx) + 1 - sz]),
            (0, 1, 1): lambda: (part, self.yzh.at[2 * (1 - sy) + 1 - sz]),
            (1, 1, 1): lambda: (part, self.xyzh.at[4 * (1 - sx) + 2 * (1 - sy) + 1 - sz]),
        }[kind]()

    def units(self, kind, n):
        if kind == (1, 0, 0):
            return self.fx.at[:, :n]
        return {
            (0, 1, 0): self.yh, (1, 1, 0): self.xyh, (0, 0, 1): self.zh,
            (1, 0, 1): self.xzh, (0, 1, 1): self.yzh, (1, 1, 1): self.xyzh,
        }[kind].at[:n]

    def start(self, kinds):
        for kind in kinds:
            if kind not in self.kinds:
                continue
            sems = [self.sem.at[2 * self.kinds.index(kind) + i] for i in (0, 1)]
            for d in itertools.product(*[(-1, 1) if on else (0,) for on in kind]):
                there = [p + v for p, v in zip(self.place, d)]
                ok = functools.reduce(jnp.logical_and, [
                    (t >= 0) if v < 0 else (t < n) for t, n, v in zip(there, self.sizes, d) if v])
                device = tuple(jnp.clip(t, 0, n - 1) for t, n in zip(there, self.sizes))
                src, dst = self.ends(kind, d)
                copy = post(src, dst, *sems, device)

                @pl.when(ok)
                def _():
                    copy.start()

    def wait(self):
        many = [jnp.where(p > 0, 1, 0) + jnp.where(p < n - 1, 1, 0) for p, n in zip(self.place, self.sizes)]
        for i, kind in enumerate(self.kinds):
            counts = [(m, (1,) if n == 2 else (1, 2)) for m, n, on in zip(many, self.sizes, kind) if on]
            for values in itertools.product(*[c for _, c in counts]):
                ref = self.units(kind, math.prod(values))
                ok = functools.reduce(jnp.logical_and, [m == v for (m, _), v in zip(counts, values)])

                @pl.when(ok)
                def _():
                    drain(self.sem.at[2 * i], ref)
                    drain(self.sem.at[2 * i + 1], ref)

    def pack(self):
        pair = lax.broadcasted_iota(jnp.int32, (self.by, self.bz), 1) // 2
        face = jnp.zeros((self.by, self.bz), F32)
        for c in range(self.nf):
            for x in range(self.bx):
                k = c * self.bx + x
                raw = self.fx[c, x + 1]
                face = jnp.where(pair == k, pltpu.roll(raw, (2 * k + 1) % self.bz, axis=1), face)
                for s, y in ((0, 0), (1, self.by - 1)):
                    self.ys[s, k:k + 1] = raw[y:y + 1]
                    if x in (0, self.bx - 1):
                        self.xys[2 * int(x > 0) + s, c:c + 1] = raw[y:y + 1]
        self.zs[...] = face

    def along(self, tile, low, high, axis):
        at = lax.broadcasted_iota(jnp.int32, tile.shape, axis)
        n = tile.shape[axis]
        return (jnp.where(at == 0, low, pltpu.roll(tile, 1, axis=axis)),
                jnp.where(at == n - 1, high, pltpu.roll(tile, n - 1, axis=axis)))

    def side_lines(self):
        for s in (0, 1):
            for c in range(self.nf):
                rows = slice(c * self.bx, (c + 1) * self.bx)
                tile = self.yh[s, rows]
                low, high = self.along(tile, self.xyh[s, c:c + 1], self.xyh[2 + s, c:c + 1], 0)
                self.yb[s, rows] = (low + high) + (tile + tile)

    def z_faces(self):
        def thrice(mid, left, right):
            lane = lax.broadcasted_iota(jnp.int32, mid[0].shape, 1)
            even = lane % 2 == 0
            x = (lane // 2) % self.bx
            mid, left, right = (jnp.where(even, *two) for two in (mid, left, right))
            w = 2 * (self.bx - 1)
            low = jnp.where(x == 0, pltpu.roll(left, self.bz - w, axis=1), pltpu.roll(mid, 2, axis=1))
            high = jnp.where(x == self.bx - 1, pltpu.roll(right, w, axis=1), pltpu.roll(mid, self.bz - 2, axis=1))
            return mid, (low + high) + (mid + mid)

        def ends(tile):
            even = lax.broadcasted_iota(jnp.int32, tile.shape, 1) % 2 == 0
            return jnp.where(even, tile, pltpu.roll(tile, self.bz - 2, axis=1))

        two = lambda ref, i: (ref[i], ref[i + 1])
        raw, face = thrice(two(self.zh, 0), two(self.xzh, 0), two(self.xzh, 2))
        _, low = thrice(two(self.yzh, 0), two(self.xyzh, 0), two(self.xyzh, 4))
        _, high = thrice(two(self.yzh, 2), two(self.xyzh, 2), two(self.xyzh, 6))
        low, high = self.along(face, low[7:8], high[0:1], 0)
        return ends(raw), ends((low + high) + (face + face))

    def finish(self):
        self.side_lines()
        raw_ends, smooth_ends = self.z_faces()
        for x in range(self.bx):
            u = [(0.5 * advection) * self.fx[c, x + 1] for c in range(3)]
            for c in (3, 0, 1, 2):
                k = c * self.bx + x
                below, raw, above = (self.fx[c, x + i] for i in range(3))
                gx = above - below
                s = (below + above) + (raw + raw)
                low, high = self.along(raw, self.yh[0, k:k + 1], self.yh[1, k:k + 1], 0)
                gy = high - low
                low, high = self.along(s, self.yb[0, k:k + 1], self.yb[1, k:k + 1], 0)
                s = (low + high) + (s + s)
                turn = (self.bz - 2 * k) % self.bz
                edge = pltpu.roll(raw_ends, turn, axis=1) if turn else raw_ends
                low, high = self.along(raw, edge, edge, 1)
                gz = high - low
                edge = pltpu.roll(smooth_ends, turn, axis=1) if turn else smooth_ends
                low, high = self.along(s, edge, edge, 1)
                s = (low + high) + (s + s)
                new = s * (1.0 / 64.0) - (u[0] * gx + u[1] * gy + u[2] * gz)
                if c == 3:
                    push = [(0.5 * advection) * g for g in (gx, gy, gz)]
                else:
                    new = new - push[c]
                self.half[c, x] = new


def sweep_scratch(block):
    nf, bx, by, bz = block
    rows = nf * bx
    assert 2 * rows == bz and by >= 8
    buf = lambda *s: pltpu.VMEM(s, F32)
    return [
        buf(nf, bx + 2, by, bz), buf(2, rows, bz), buf(2, rows, bz), buf(4, 8, bz), buf(4, 8, bz), buf(2, rows, bz),
        buf(by, bz), buf(2, by, bz), buf(4, by, bz), buf(4, 8, bz), buf(8, 8, bz), pltpu.SemaphoreType.DMA((14,)),
    ]


class Gather:
    def __init__(self, at, piece, line, nodes, sem):
        self.at, self.piece, self.line, self.nodes = at, piece, line, nodes
        self.line_sent, self.plane_sent, self.plane_here = (sem.at[i] for i in range(3))
        self.line_here = [sem.at[3 + d] for d in range(at.nz)]

    def start(self):
        at = self.at
        for d in range(1, at.nz):
            post(self.piece, self.line.at[at.z], self.line_sent, self.line_here[d], at.line_peer(d)[1]).start()

    def own(self):
        self.nodes[self.at.h, self.at.z] = self.piece[...]
        self.to_plane(self.piece, self.at.z)

    def to_plane(self, src, z):
        at = self.at
        for d in range(1, at.team):
            post(src, self.nodes.at[at.h, z], self.plane_sent, self.plane_here, at.team_peer(d)[1]).start()

    def forward(self, d):
        at = self.at
        z = lax.rem(at.z + at.nz - d, at.nz)
        drain(self.line_here[d], self.line.at[z])
        self.to_plane(self.line.at[z], z)
        self.nodes[at.h, z] = self.line[z]

    def wait(self):
        at = self.at
        if at.nz > 1:
            drain(self.line_sent, self.line.at[:at.nz - 1])
        if at.team > 1:
            drain(self.plane_sent, self.nodes.at[:at.team - 1])
            drain(self.plane_here, self.nodes.at[:at.team - 1])


class Reduce:
    def __init__(self, at, terms, landed_p, sums, landed_l, sem):
        self.at, self.terms, self.landed_p, self.sums, self.landed_l = at, terms, landed_p, sums, landed_l
        self.plane_sent, self.line_sent, self.line_here = (sem.at[i] for i in range(3))
        self.plane_here = [sem.at[3 + k] for k in range(at.nz)]
        self.order = list(range(1, at.nz)) + [0]

    def start(self):
        at = self.at
        for k in self.order:
            z = lax.rem(at.z + k, at.nz)
            for d in range(1, at.team):
                p, device = at.team_peer(d)
                post(self.terms.at[p, z], self.landed_p.at[k, d - 1], self.plane_sent, self.plane_here[k],
                     device).start()

    def forward(self, spread):
        at = self.at
        self.count = spread * at.nz - 1
        for k in self.order:
            z = lax.rem(at.z + k, at.nz)
            total = self.terms[at.h, z]
            if at.team > 1:
                drain(self.plane_here[k], self.landed_p.at[k])
            for d in range(1, at.team):
                total = total + self.landed_p[k, d - 1]
            self.sums[k] = total
            for dx in range(spread):
                if k or dx:
                    post(self.sums.at[k], self.landed_l.at[dx * at.nz + k], self.line_sent, self.line_here,
                         at.side_peer(dx, k)[1]).start()

    def wait(self):
        if self.count:
            drain(self.line_sent, self.landed_l.at[1:self.count + 1])
            drain(self.line_here, self.landed_l.at[1:self.count + 1])
        if self.at.team > 1:
            drain(self.plane_sent, self.landed_p)

    def total(self, dx):
        nz = self.at.nz
        total = self.sums[0] if dx == 0 else self.landed_l[dx * nz]
        for k in range(1, nz):
            total = total + self.landed_l[dx * nz + k]
        return total


class Couple:
    def __init__(self, at, block, cells, records, refs):
        self.at, self.cells, self.records = at, cells, records
        (self.table_c, self.table_n, self.wide, self.acc_f, self.acc_n, self.rest, self.hot_c, self.hot_n,
         self.factor, self.keep_c, self.keep_n, self.found, self.values) = refs
        self.rows_c, self.lanes = self.rest.shape
        self.rows_n = self.acc_n.shape[0] // 4
        self.sources, self.width = cells.shape[1:]
        _, self.bx, self.by, self.bz = block
        self.hy = self.by // 2
        self.plain = self.sources <= 16

    def chunks(self, step):
        if self.plain:
            for q in range(self.sources // 2):
                step(q)
        else:
            pl.loop(0, self.sources // 2)(step)

    def fresh(self, acc):
        if not self.plain:
            acc[...] = jnp.zeros_like(acc)

    def split_store(self, table, rows, c, value):
        hi = value.astype(BF16)
        table[c * rows:(c + 1) * rows] = hi
        table[(3 + c) * rows:(4 + c) * rows] = (value - hi.astype(F32)).astype(BF16)

    def pieces(self, nodes):
        at = self.at
        comps, pr, pw = nodes.shape[2:]
        lp = min(2, at.nx)
        rp = at.nx // lp
        for g in range(at.nx):
            r0, l0 = (g // lp) * pr, (g % lp) * pw
            for y in range(at.half):
                for z in range(at.nz):
                    for c in range(comps):
                        r = c * self.rows_n + (y * at.nz + z) * (rp * pr) + r0
                        yield g * at.half + y, z, c, slice(r, r + pr), slice(l0, l0 + pw)

    def both(self, read, q):
        return jnp.concatenate([read(2 * q), read(2 * q + 1)], axis=1)

    def cell(self, s, q):
        return self.both(lambda i: self.cells[s, pl.ds(i, 1), :], q)

    def left(self):
        return lax.broadcasted_iota(jnp.int32, (1, self.width), 1) < self.width // 2

    def weight(self, s, i):
        top, bottom = self.records(s, i), self.records(s, i + self.sources)
        return jnp.where(self.left(), top, pltpu.roll(bottom, self.width // 2, axis=1))

    def ident(self, s, i):
        top, bottom = self.records(s, i), self.records(s, i + self.sources)
        return jnp.where(self.left(), pltpu.roll(top, self.width // 2, axis=1), bottom)

    def hot(self, lane):
        lane_of = lax.broadcasted_iota(jnp.int32, (self.lanes, 2 * self.width), 0)
        return jnp.where(lane_of == lane, 1.0, 0.0).astype(BF16)

    def place_cells(self):
        def step(q):
            cell = self.cell(0, q)
            y = lax.rem(lax.div(cell, self.bz), self.by)
            x = lax.div(cell, self.by * self.bz)
            self.hot_c[q] = self.hot(lax.div(y, self.hy) * self.bz + lax.rem(cell, self.bz))
            self.keep_c[q] = x * self.hy + lax.rem(y, self.hy)

        self.chunks(step)

    def place_nodes(self, s):
        total = self.bx * self.by * self.bz
        line = self.rows_n // self.at.half

        def step(q):
            node = self.both(lambda i: self.ident(s, i), q).astype(jnp.int32)
            row = lax.div(node, self.lanes)
            y = lax.div(row, line)
            self.hot_n[s, q] = self.hot(lax.rem(node, self.lanes))
            self.keep_n[s, q] = jnp.where(lax.rem(y, 2) == self.at.par, lax.div(y, 2) * line + lax.rem(row, line), -1)
            weight = self.both(lambda i: self.weight(s, i), q)
            self.factor[s, q] = jnp.where(self.cell(s, q) < total, penalty * weight, 0.0)

        self.chunks(step)

    def find_all(self, table, rows, hots, keeps, out):
        def step(j):
            two = (2 * j, 2 * j + 1)
            hot = jnp.concatenate([hots[q] for q in two], axis=1)
            row = jnp.concatenate([keeps[q] for q in two], axis=1)
            for c, v in enumerate(self.find(table, rows, hot, row)):
                for i, q in enumerate(two):
                    out[q, c:c + 1] = v[:, 2 * i * self.width:2 * (i + 1) * self.width]

        if self.plain:
            for j in range(self.sources // 4):
                step(j)
        else:
            pl.loop(0, self.sources // 4)(step)

    def find(self, table, rows, hot, row):
        mask = lax.broadcasted_iota(jnp.int32, (rows, hot.shape[1]), 0) == row
        found = jnp.dot(table[...], hot, preferred_element_type=F32)
        found = found[:3 * rows] + found[3 * rows:]
        return [
            jnp.sum(jnp.where(mask, found[c * rows:(c + 1) * rows], 0.0), axis=0, keepdims=True) for c in range(3)
        ]

    def spread(self, hot, row, terms, acc, rows, first):
        mask = lax.broadcasted_iota(jnp.int32, (rows, 2 * self.width), 0) == row
        high = [t.astype(BF16).astype(F32) for t in terms]
        n = len(terms) * rows
        stack = len(terms) > 3 and rows == self.rows_c
        high, low = (
            jnp.concatenate([jnp.where(mask, t, 0.0).astype(BF16) for t in part], axis=0)
            for part in (high, [t - h for t, h in zip(terms, high)])
        )
        values = jnp.concatenate([high, low], axis=int(stack))
        hot = jnp.concatenate([hot, hot], axis=1) if stack else hot
        out = lax.dot_general(values, hot, (((1,), (1,)), ((), ())), preferred_element_type=F32)
        out = out if stack else out[:n] + out[n:]
        if first:
            acc[:n] = out
        else:
            acc[:n] += out

    def first(self, q):
        return self.plain and q == 0

    def find_cells(self, half):
        for c in range(3):
            value = half[c]
            top = value[:, :self.hy].reshape(self.rows_c, self.bz)
            low = value[:, self.hy:].reshape(self.rows_c, self.bz)
            self.split_store(self.table_c, self.rows_c, c, jnp.concatenate([top, low], axis=1))

        self.find_all(self.table_c, self.rows_c, self.hot_c, self.keep_c, self.found)

    def swap(self, src, dst, sem):
        copy = post(src, dst, sem.at[0], sem.at[1], self.at.mate)
        copy.start()
        return copy

    def weigh_found(self):
        def step(q):
            self.values[0, q] = self.found[q] * self.factor[0, q]

        self.chunks(step)

    def spread_nodes(self, s, incoming, weigh):
        if s == 0:
            self.fresh(self.acc_n)

        def step(q):
            terms = [incoming[q, c:c + 1] for c in range(3)] + ([self.factor[s, q]] if weigh else [])
            self.spread(self.hot_n[s, q], self.keep_n[s, q], terms, self.acc_n, self.rows_n, s == 0 and self.first(q))

        self.chunks(step)

    def store_terms(self, terms):
        for p, z, c, r, l in self.pieces(terms):
            terms[p, z, c] = self.acc_n[r, l]

    def find_nodes(self, s, outgoing):
        self.find_all(self.table_n, self.rows_n, self.hot_n.at[s], self.keep_n.at[s], outgoing)

    def load_nodes(self, nodes):
        for p, z, c, r, l in self.pieces(nodes):
            self.wide[r, l] = nodes[p, z, c]
        for c in range(3):
            self.split_store(self.table_n, self.rows_n, c, self.wide[c * self.rows_n:(c + 1) * self.rows_n])

    def spread_cells(self, incoming, weigh):
        self.fresh(self.acc_f)

        def step(q):
            factor = self.factor[0, q]
            terms = [factor * (self.found[q, c:c + 1] + incoming[q, c:c + 1]) for c in range(3)]
            terms += [factor] if weigh else []
            self.spread(self.hot_c[q], self.keep_c[q], terms, self.acc_f, self.rows_c, self.first(q))

        self.chunks(step)
        if weigh:
            self.rest[...] = 1.0 - self.acc_f[3 * self.rows_c:]

    def push(self, half, fluid, first):
        bx, hy, bz = self.bx, self.hy, self.bz
        rest = self.rest[...]
        for c in range(3):
            force = self.acc_f[c * self.rows_c:(c + 1) * self.rows_c]
            for s in (0, 1):
                y, l = slice(s * hy, (s + 1) * hy), slice(s * bz, (s + 1) * bz)
                fluid[c, first:first + bx, y] = (
                    half[c, :, y] * rest[:, l].reshape(bx, hy, bz) + force[:, l].reshape(bx, hy, bz))
        fluid[3, first:first + bx] = half[3]


def prepare(sizes, shell_raw, weights, elements, owned, counts, shell, rec, cells, joined, total):
    nx, _, nz = sizes
    pr, pw = shell.shape[2:]
    lp = min(2, nx)
    for g in range(nx):
        for r in range(pr):
            m = ((g // lp) * pr + r) * lp * pw + (g % lp) * pw
            for c in range(3):
                shell[g, c, r:r + 1, :] = shell_raw[c:c + 1, m:m + pw]
    ranks, slots = weights.shape[1:]
    joined[:, :slots] = weights[0]
    joined[:, slots:] = elements[0].astype(F32)
    for i in range(ranks):
        rec[i // nz, i % nz] = joined[i:i + 1, :]
    same = lax.broadcasted_iota(jnp.int32, (ranks, ranks), 0) == lax.broadcasted_iota(jnp.int32, (ranks, ranks), 1)
    count = jnp.sum(jnp.where(same, counts[...].astype(F32), 0.0), axis=1, keepdims=True)
    slot = lax.broadcasted_iota(jnp.int32, (ranks, slots), 1).astype(F32)
    value = jnp.where(slot < count, owned[0], total)
    cells[0, :, :slots] = value[:ranks // 2]
    cells[0, :, slots:] = value[ranks // 2:]


FAR = ((1, 1, 1), (0, 1, 1), (1, 0, 1), (0, 0, 1), (1, 1, 0))
NEAR = ((0, 1, 0), (1, 0, 0))


def whole_kernel(sizes, fluid_in, shell_in, weights_in, elements_in, owned_in, counts_in, fluid, out, *refs):
    refs = list(refs)
    take = lambda n: [refs.pop(0) for _ in range(n)]
    raw = take(5)
    joined, shell, rec, cells, sem_in = take(5)
    line0, line1, nodes0, nodes1, rec_line, records = take(6)
    half, = take(1)
    terms0, terms1, ours = take(3)
    reduce0, reduce1 = take(3), take(3)
    mine, last = take(2)
    result = fluid
    sem_r, sem_g0, sem_g1, sem_a0, sem_a1, sem_w, sem_m = take(7)
    swapped = take(4)
    couple_refs = take(13)
    sweep_refs = take(12), take(12)
    at = Place(sizes)
    first, second = [Sweep(at, half, *r) for r in sweep_refs]
    for sweep in (first, second):
        sweep.clear()
    at.greet()
    _, bx, by, bz = half.shape
    here = sweep_refs[0][0].at[:, 1:bx + 1]
    fetches = start_all([pltpu.make_async_copy(fluid_in, here, sem_in.at[0])])
    pairs = list(zip((shell_in, weights_in, elements_in, owned_in, counts_in), raw))
    fetches += start_all([pltpu.make_async_copy(src, dst, sem_in.at[i + 1]) for i, (src, dst) in enumerate(pairs)])
    fetches.pop(0).wait()
    first.pack()
    at.meet()
    first.start(FAR + NEAR)
    wait_all(fetches)
    prepare(sizes, *raw, shell, rec, cells, joined, bx * by * bz)
    sems = [sem_m.at[2 * i:2 * i + 2] for i in range(5)]
    read = lambda s, i: records[i // at.nz, i % at.nz, at.par if s == 0 else 1 - at.par]
    couple = Couple(at, half.shape, cells, read, couple_refs)
    gather = Gather(at, shell.at[at.x], line0, nodes0, sem_g0)
    for d in range(1, at.nz):
        z, device = at.line_peer(d)
        post(rec.at[:, z], rec_line.at[at.z], sem_r.at[0], sem_r.at[1], device).start()
    swaps = [couple.swap(cells.at[0], cells.at[1], sems[0])]
    gather.start()
    rec_line[at.z] = rec[:, at.z]
    couple.place_cells()
    if at.nz > 1:
        drain(sem_r.at[0], rec_line.at[:at.nz - 1])
        drain(sem_r.at[1], rec_line.at[:at.nz - 1])
    for d in range(1, at.plane):
        p, device = at.plane_peer(d)
        post(rec_line.at[:, pl.ds(2 * lax.div(p, 2), 2)], records.at[at.p], sem_r.at[2], sem_r.at[3], device).start()
    records[at.p] = rec_line[:, pl.ds(2 * lax.div(at.p, 2), 2)]
    first.wait()
    gather.own()
    first.finish()
    couple.find_cells(half)
    for d in range(1, at.nz):
        gather.forward(d)
    drain(sem_r.at[2], records.at[:at.plane - 1])
    drain(sem_r.at[3], records.at[:at.plane - 1])
    couple.place_nodes(0)
    couple.weigh_found()
    swaps[0].wait()
    swaps = [couple.swap(couple.values.at[0], couple.values.at[1], sems[1])]
    couple.place_nodes(1)
    couple.spread_nodes(0, couple.values.at[0], True)
    swaps[0].wait()
    couple.spread_nodes(1, couple.values.at[1], True)
    couple.store_terms(terms0)
    loads = Reduce(at, terms0, *reduce0, sem_a0)
    loads.start()

    gather.wait()
    couple.load_nodes(nodes0)
    couple.find_nodes(1, swapped[0])
    swaps = [couple.swap(swapped[0], swapped[1], sems[2])]
    couple.find_nodes(0, couple.found)
    swaps[0].wait()
    couple.spread_cells(swapped[1], True)
    couple.push(half, second.fx, 1)
    second.pack()
    second.start(FAR + NEAR)
    loads.forward(1)
    second.wait()
    second.finish()
    loads.wait()
    total = loads.total(0)
    ours[at.x] = 1.0 - relaxation * total[3:]
    mine[...] = shell[at.x] * (1.0 - relaxation * total[3:]) + relaxation * total[:3]
    gather = Gather(at, mine, line1, nodes1, sem_g1)
    gather.start()
    gather.own()
    for dx in range(1, at.nx):
        device = (lax.rem(at.x + dx, at.nx), at.y, at.z)
        post(ours.at[at.x], ours.at[at.x], sem_w.at[0], sem_w.at[1], device).start()
    couple.find_cells(half)
    couple.weigh_found()
    swaps = [couple.swap(couple.values.at[0], couple.values.at[1], sems[3])]
    couple.spread_nodes(0, couple.values.at[0], False)
    if at.nz > 1:
        gather.forward(1)
    swaps[0].wait()
    couple.spread_nodes(1, couple.values.at[1], False)
    for d in range(2, at.nz):
        gather.forward(d)
    couple.store_terms(terms1)
    loads = Reduce(at, terms1, *reduce1, sem_a1)
    loads.start()
    gather.wait()
    couple.load_nodes(nodes1)
    couple.find_nodes(1, swapped[2])
    swaps = [couple.swap(swapped[2], swapped[3], sems[4])]
    loads.forward(at.nx)
    couple.find_nodes(0, couple.found)
    swaps[0].wait()
    couple.spread_cells(swapped[3], False)
    couple.push(half, result, 0)
    if at.nx > 1:
        drain(sem_w.at[0], ours.at[:at.nx - 1])
        drain(sem_w.at[1], ours.at[:at.nx - 1])
    loads.wait()
    for dx in range(at.nx):
        x = lax.rem(at.x + at.nx - dx, at.nx)
        last[x] = nodes1[x * at.half + at.yc, at.z] * ours[x] + relaxation * loads.total(dx)
    pr, pw = shell.shape[2:]
    lp = min(2, at.nx)
    for g in range(at.nx):
        for r in range(pr):
            m = ((g // lp) * pr + r) * lp * pw + (g % lp) * pw
            for c in range(3):
                out[c:c + 1, m:m + pw] = last[g, c, r:r + 1, :]

def on_device(sizes, fluid_state, shell_disp, quad_weights, quad_elements, owner_cells, owner_counts):
    nx, ny, nz = sizes
    plane = nx * ny
    slots = quad_weights.shape[2]
    ranks = quad_weights.shape[1]
    block = fluid_state.shape
    nodes_here = shell_disp.shape[1]
    lanes = 2 * block[3]
    lp = min(2, nx)
    rp = nx // lp
    pr, pw = nodes_here // lanes // rp, lanes // lp
    piece = (3, pr, pw)
    rec_shape = (plane, nz, 1, 2 * slots)
    shell_shape = (nx,) + piece
    i32 = lambda s: pltpu.VMEM(s, jnp.int32)

    shape = lambda s: jax.ShapeDtypeStruct(s, F32)
    buf = lambda s: pltpu.VMEM(s, F32)
    line = (nz,) + piece
    team = plane // 2
    full = (team,) + line
    four, thin = (4, pr, pw), (1, pr, pw)
    sem = lambda n: pltpu.SemaphoreType.DMA((n,))

    def reduce_scratch(spread, item):
        return [buf((nz, max(team - 1, 1)) + item), buf((nz,) + item), buf((spread * nz,) + item)]

    rows_n = ny * nz * rp * pr // 2
    rows_c = block[1] * block[2] // 2
    steps, wide = ranks // 4, 4 * slots
    half16 = lambda *s: pltpu.VMEM(s, BF16)
    scratch = [
        buf(shell_disp.shape), buf(quad_weights.shape), i32(quad_elements.shape), i32(owner_cells.shape),
        i32(owner_counts.shape),
        buf((ranks, 2 * slots)), buf(shell_shape), buf(rec_shape), i32((2, ranks // 2, 2 * slots)), sem(6),
        buf(line), buf(line), buf(full), buf(full), buf((nz, plane, 1, 2 * slots)), buf((plane, nz, 2, 1, 2 * slots)),
        buf(block), buf((team, nz) + four), buf(full), buf((nx,) + thin),
        *reduce_scratch(1, four), *reduce_scratch(nx, piece),
        buf(piece), buf(shell_shape),
        sem(4), sem(3 + nz), sem(3 + nz), sem(3 + nz), sem(3 + nz), sem(2), sem(10),
        *[buf((steps, 3, wide))] * 4,
        half16(6 * rows_c, lanes), half16(6 * rows_n, lanes), buf((3 * rows_n, lanes)), buf((4 * rows_c, lanes)),
        buf((4 * rows_n, lanes)), buf((rows_c, lanes)),
        half16(steps, lanes, wide), half16(2, steps, lanes, wide), buf((2, steps, 1, wide)),
        i32((steps, 1, wide)), i32((2, steps, 1, wide)), buf((steps, 3, wide)), buf((2, steps, 3, wide)),
        *sweep_scratch(block), *sweep_scratch(block),
    ]
    anywhere, vmem = pl.BlockSpec(memory_space=pl.ANY), pl.BlockSpec(memory_space=pltpu.VMEM)
    fluid, out = pl.pallas_call(
        functools.partial(whole_kernel, sizes),
        out_shape=(buf(block), buf(shell_disp.shape)),
        in_specs=[anywhere] * 6, out_specs=(vmem, vmem),
        scratch_shapes=scratch,
        compiler_params=pltpu.CompilerParams(collective_id=0, has_side_effects=True, vmem_limit_bytes=56 << 20),
    )(fluid_state, shell_disp, quad_weights, quad_elements, owner_cells, owner_counts)
    return fluid, out


def solution(mesh):
    sizes = tuple(mesh.shape[a] for a in AXES)
    return jax.shard_map(
        functools.partial(on_device, sizes),
        mesh=mesh,
        in_specs=(
            P(None, "gx", "gy", "gz"),
            P(None, ("gy", "gz")),
            P(("gx", "gy", "gz"), None, None),
            P(("gx", "gy", "gz"), None, None),
            P(("gx", "gy", "gz"), None, None),
            P(("gx", "gy", "gz"), None),
        ),
        out_specs=(P(None, "gx", "gy", "gz"), P(None, ("gy", "gz"))),
        check_vma=False,
    )
```

```python
import functools
import itertools
import math

import jax
import jax.numpy as jnp
from jax import lax
from jax.experimental import pallas as pl
from jax.experimental.pallas import tpu as pltpu
from jax.sharding import PartitionSpec as P

ITERS = 2

advection = 0.2
penalty = 0.5
relaxation = 0.05
AXES = ("gx", "gy", "gz")
MESH = pl.DeviceIdType.MESH
F32 = jnp.float32
BF16 = jnp.bfloat16


class Place:
    def __init__(self, sizes):
        self.nx, self.ny, self.nz = sizes
        self.plane = self.nx * self.ny
        self.x, self.y, self.z = (lax.axis_index(a) for a in AXES)
        self.p = self.x * self.ny + self.y
        assert self.ny % 2 == 0
        self.half, self.yc, self.par = self.ny // 2, lax.div(self.y, 2), lax.rem(self.y, 2)
        self.team, self.h = self.nx * self.half, self.x * self.half + self.yc
        self.mate = (self.x, self.y + 1 - 2 * self.par, self.z)

    def team_peer(self, d):
        h = lax.rem(self.h + d, self.team)
        return h, (lax.div(h, self.half), 2 * lax.rem(h, self.half) + self.par, self.z)

    def plane_peer(self, d):
        p = lax.rem(self.p + d, self.plane)
        return p, (lax.div(p, self.ny), lax.rem(p, self.ny), self.z)

    def line_peer(self, d):
        z = lax.rem(self.z + d, self.nz)
        return z, (self.x, self.y, z)

    def peers(self):
        yield from (self.plane_peer(d)[1] for d in range(1, self.plane))
        for dx in range(self.nx):
            yield from (self.side_peer(dx, d)[1] for d in range(1, self.nz))

    def corners(self):
        sizes, place = (self.nx, self.ny, self.nz), (self.x, self.y, self.z)
        if self.nz > 1 and self.ny > 1:
            for d in itertools.product((-1, 0, 1), (-1, 1), (-1, 1)):
                if d[0] and self.nx == 1:
                    continue
                there = [p + v for p, v in zip(place, d)]
                ok = functools.reduce(jnp.logical_and, [
                    (t >= 0) if v < 0 else (t < n) for t, n, v in zip(there, sizes, d) if v])
                yield ok, tuple(jnp.clip(t, 0, n - 1) for t, n in zip(there, sizes))

    def greet(self):
        sem = pltpu.get_barrier_semaphore()
        for device in self.peers():
            pl.semaphore_signal(sem, inc=1, device_id=device, device_id_type=MESH)
        for ok, device in self.corners():
            @pl.when(ok)
            def _():
                pl.semaphore_signal(sem, inc=1, device_id=device, device_id_type=MESH)

    def meet(self):
        sem = pltpu.get_barrier_semaphore()
        many = self.plane - 1 + self.nx * (self.nz - 1)
        for ok, _ in self.corners():
            many += jnp.where(ok, 1, 0)
        pl.semaphore_wait(sem, many)

    def side_peer(self, dx, d):
        x, z = lax.rem(self.x + dx, self.nx), lax.rem(self.z + d, self.nz)
        return z, (x, self.y, z)


def send(src, dst, sems, k, device):
    return post(src, dst, sems.at[0, k], sems.at[1, k], device)


def post(src, dst, send_sem, recv_sem, device):
    return pltpu.make_async_remote_copy(
        src_ref=src, dst_ref=dst, send_sem=send_sem, recv_sem=recv_sem, device_id=device, device_id_type=MESH,
    )


def start_all(copies):
    for c in copies:
        c.start()
    return copies


def wait_all(copies):
    for c in copies:
        c.wait()


def drain(sem, ref):
    pltpu.make_async_copy(ref, ref, sem).wait()


class Sweep:
    def __init__(self, at, half, fx, ys, yh, xys, xyh, yb, zs, zh, xzh, yzh, xyzh, sem):
        self.at, self.half, self.fx, self.ys, self.yh, self.xys, self.xyh, self.yb = at, half, fx, ys, yh, xys, xyh, yb
        self.zs, self.zh, self.xzh, self.yzh, self.xyzh, self.sem = zs, zh, xzh, yzh, xyzh, sem
        self.nf, self.bx, self.by, self.bz = half.shape
        self.place = (at.x, at.y, at.z)
        self.sizes = (at.nx, at.ny, at.nz)
        self.kinds = [k for k in itertools.product((0, 1), repeat=3)
                      if any(k) and all(n > 1 for n, on in zip(self.sizes, k) if on)]

    def clear(self):
        for edge in (0, self.bx + 1):
            self.fx[:, edge] = jnp.zeros((self.nf, self.by, self.bz), F32)
        for ref in (self.yh, self.xys, self.xyh, self.zh, self.xzh, self.yzh, self.xyzh):
            ref[...] = jnp.zeros(ref.shape, F32)

    def ends(self, kind, d):
        sx, sy, sz = (int(v > 0) for v in d)
        bx, by = self.bx, self.by
        part = self.zs.at[by - 8:by] if sy else self.zs.at[0:8]
        return {
            (1, 0, 0): lambda: (self.fx.at[:, bx if sx else 1], self.fx.at[:, 0 if sx else bx + 1]),
            (0, 1, 0): lambda: (self.ys.at[sy], self.yh.at[1 - sy]),
            (1, 1, 0): lambda: (self.xys.at[2 * sx + sy], self.xyh.at[2 * (1 - sx) + 1 - sy]),
            (0, 0, 1): lambda: (self.zs, self.zh.at[1 - sz]),
            (1, 0, 1): lambda: (self.zs, self.xzh.at[2 * (1 - sx) + 1 - sz]),
            (0, 1, 1): lambda: (part, self.yzh.at[2 * (1 - sy) + 1 - sz]),
            (1, 1, 1): lambda: (part, self.xyzh.at[4 * (1 - sx) + 2 * (1 - sy) + 1 - sz]),
        }[kind]()

    def units(self, kind, n):
        if kind == (1, 0, 0):
            return self.fx.at[:, :n]
        return {
            (0, 1, 0): self.yh, (1, 1, 0): self.xyh, (0, 0, 1): self.zh,
            (1, 0, 1): self.xzh, (0, 1, 1): self.yzh, (1, 1, 1): self.xyzh,
        }[kind].at[:n]

    def start(self, kinds):
        for kind in kinds:
            if kind not in self.kinds:
                continue
            sems = [self.sem.at[2 * self.kinds.index(kind) + i] for i in (0, 1)]
            for d in itertools.product(*[(-1, 1) if on else (0,) for on in kind]):
                there = [p + v for p, v in zip(self.place, d)]
                ok = functools.reduce(jnp.logical_and, [
                    (t >= 0) if v < 0 else (t < n) for t, n, v in zip(there, self.sizes, d) if v])
                device = tuple(jnp.clip(t, 0, n - 1) for t, n in zip(there, self.sizes))
                src, dst = self.ends(kind, d)
                copy = post(src, dst, *sems, device)

                @pl.when(ok)
                def _():
                    copy.start()

    def wait(self):
        many = [jnp.where(p > 0, 1, 0) + jnp.where(p < n - 1, 1, 0) for p, n in zip(self.place, self.sizes)]
        for i, kind in enumerate(self.kinds):
            counts = [(m, (1,) if n == 2 else (1, 2)) for m, n, on in zip(many, self.sizes, kind) if on]
            for values in itertools.product(*[c for _, c in counts]):
                ref = self.units(kind, math.prod(values))
                ok = functools.reduce(jnp.logical_and, [m == v for (m, _), v in zip(counts, values)])

                @pl.when(ok)
                def _():
                    drain(self.sem.at[2 * i], ref)
                    drain(self.sem.at[2 * i + 1], ref)

    def pack(self):
        pair = lax.broadcasted_iota(jnp.int32, (self.by, self.bz), 1) // 2
        face = jnp.zeros((self.by, self.bz), F32)
        for c in range(self.nf):
            for x in range(self.bx):
                k = c * self.bx + x
                raw = self.fx[c, x + 1]
                face = jnp.where(pair == k, pltpu.roll(raw, (2 * k + 1) % self.bz, axis=1), face)
                for s, y in ((0, 0), (1, self.by - 1)):
                    self.ys[s, k:k + 1] = raw[y:y + 1]
                    if x in (0, self.bx - 1):
                        self.xys[2 * int(x > 0) + s, c:c + 1] = raw[y:y + 1]
        self.zs[...] = face

    def along(self, tile, low, high, axis):
        at = lax.broadcasted_iota(jnp.int32, tile.shape, axis)
        n = tile.shape[axis]
        return (jnp.where(at == 0, low, pltpu.roll(tile, 1, axis=axis)),
                jnp.where(at == n - 1, high, pltpu.roll(tile, n - 1, axis=axis)))

    def side_lines(self):
        for s in (0, 1):
            for c in range(self.nf):
                rows = slice(c * self.bx, (c + 1) * self.bx)
                tile = self.yh[s, rows]
                low, high = self.along(tile, self.xyh[s, c:c + 1], self.xyh[2 + s, c:c + 1], 0)
                self.yb[s, rows] = (low + high) + (tile + tile)

    def z_faces(self):
        def thrice(mid, left, right):
            lane = lax.broadcasted_iota(jnp.int32, mid[0].shape, 1)
            even = lane % 2 == 0
            x = (lane // 2) % self.bx
            mid, left, right = (jnp.where(even, *two) for two in (mid, left, right))
            w = 2 * (self.bx - 1)
            low = jnp.where(x == 0, pltpu.roll(left, self.bz - w, axis=1), pltpu.roll(mid, 2, axis=1))
            high = jnp.where(x == self.bx - 1, pltpu.roll(right, w, axis=1), pltpu.roll(mid, self.bz - 2, axis=1))
            return mid, (low + high) + (mid + mid)

        def ends(tile):
            even = lax.broadcasted_iota(jnp.int32, tile.shape, 1) % 2 == 0
            return jnp.where(even, tile, pltpu.roll(tile, self.bz - 2, axis=1))

        two = lambda ref, i: (ref[i], ref[i + 1])
        raw, face = thrice(two(self.zh, 0), two(self.xzh, 0), two(self.xzh, 2))
        _, low = thrice(two(self.yzh, 0), two(self.xyzh, 0), two(self.xyzh, 4))
        _, high = thrice(two(self.yzh, 2), two(self.xyzh, 2), two(self.xyzh, 6))
        low, high = self.along(face, low[7:8], high[0:1], 0)
        return ends(raw), ends((low + high) + (face + face))

    def finish(self):
        self.side_lines()
        raw_ends, smooth_ends = self.z_faces()
        for x in range(self.bx):
            u = [(0.5 * advection) * self.fx[c, x + 1] for c in range(3)]
            for c in (3, 0, 1, 2):
                k = c * self.bx + x
                below, raw, above = (self.fx[c, x + i] for i in range(3))
                gx = above - below
                s = (below + above) + (raw + raw)
                low, high = self.along(raw, self.yh[0, k:k + 1], self.yh[1, k:k + 1], 0)
                gy = high - low
                low, high = self.along(s, self.yb[0, k:k + 1], self.yb[1, k:k + 1], 0)
                s = (low + high) + (s + s)
                turn = (self.bz - 2 * k) % self.bz
                edge = pltpu.roll(raw_ends, turn, axis=1) if turn else raw_ends
                low, high = self.along(raw, edge, edge, 1)
                gz = high - low
                edge = pltpu.roll(smooth_ends, turn, axis=1) if turn else smooth_ends
                low, high = self.along(s, edge, edge, 1)
                s = (low + high) + (s + s)
                new = s * (1.0 / 64.0) - (u[0] * gx + u[1] * gy + u[2] * gz)
                if c == 3:
                    push = [(0.5 * advection) * g for g in (gx, gy, gz)]
                else:
                    new = new - push[c]
                self.half[c, x] = new


def sweep_scratch(block):
    nf, bx, by, bz = block
    rows = nf * bx
    assert 2 * rows == bz and by >= 8
    buf = lambda *s: pltpu.VMEM(s, F32)
    return [
        buf(nf, bx + 2, by, bz), buf(2, rows, bz), buf(2, rows, bz), buf(4, 8, bz), buf(4, 8, bz), buf(2, rows, bz),
        buf(by, bz), buf(2, by, bz), buf(4, by, bz), buf(4, 8, bz), buf(8, 8, bz), pltpu.SemaphoreType.DMA((14,)),
    ]


class Gather:
    def __init__(self, at, piece, line, nodes, sem):
        self.at, self.piece, self.line, self.nodes = at, piece, line, nodes
        self.line_sent, self.plane_sent, self.plane_here = (sem.at[i] for i in range(3))
        self.line_here = [sem.at[3 + d] for d in range(at.nz)]

    def start(self):
        at = self.at
        for d in range(1, at.nz):
            post(self.piece, self.line.at[at.z], self.line_sent, self.line_here[d], at.line_peer(d)[1]).start()

    def own(self):
        self.nodes[self.at.h, self.at.z] = self.piece[...]
        self.to_plane(self.piece, self.at.z)

    def to_plane(self, src, z):
        at = self.at
        for d in range(1, at.team):
            post(src, self.nodes.at[at.h, z], self.plane_sent, self.plane_here, at.team_peer(d)[1]).start()

    def forward(self, d):
        at = self.at
        z = lax.rem(at.z + at.nz - d, at.nz)
        drain(self.line_here[d], self.line.at[z])
        self.to_plane(self.line.at[z], z)
        self.nodes[at.h, z] = self.line[z]

    def wait(self):
        at = self.at
        if at.nz > 1:
            drain(self.line_sent, self.line.at[:at.nz - 1])
        if at.team > 1:
            drain(self.plane_sent, self.nodes.at[:at.team - 1])
            drain(self.plane_here, self.nodes.at[:at.team - 1])


class Reduce:
    def __init__(self, at, terms, landed_p, sums, landed_l, sem):
        self.at, self.terms, self.landed_p, self.sums, self.landed_l = at, terms, landed_p, sums, landed_l
        self.plane_sent, self.line_sent, self.line_here = (sem.at[i] for i in range(3))
        self.plane_here = [sem.at[3 + k] for k in range(at.nz)]
        self.order = list(range(1, at.nz)) + [0]

    def start(self):
        at = self.at
        for k in self.order:
            z = lax.rem(at.z + k, at.nz)
            for d in range(1, at.team):
                p, device = at.team_peer(d)
                post(self.terms.at[p, z], self.landed_p.at[k, d - 1], self.plane_sent, self.plane_here[k],
                     device).start()

    def forward(self, spread):
        at = self.at
        self.count = spread * at.nz - 1
        for k in self.order:
            z = lax.rem(at.z + k, at.nz)
            total = self.terms[at.h, z]
            if at.team > 1:
                drain(self.plane_here[k], self.landed_p.at[k])
            for d in range(1, at.team):
                total = total + self.landed_p[k, d - 1]
            self.sums[k] = total
            for dx in range(spread):
                if k or dx:
                    post(self.sums.at[k], self.landed_l.at[dx * at.nz + k], self.line_sent, self.line_here,
                         at.side_peer(dx, k)[1]).start()

    def wait(self):
        if self.count:
            drain(self.line_sent, self.landed_l.at[1:self.count + 1])
            drain(self.line_here, self.landed_l.at[1:self.count + 1])
        if self.at.team > 1:
            drain(self.plane_sent, self.landed_p)

    def total(self, dx):
        nz = self.at.nz
        total = self.sums[0] if dx == 0 else self.landed_l[dx * nz]
        for k in range(1, nz):
            total = total + self.landed_l[dx * nz + k]
        return total


class Couple:
    def __init__(self, at, block, cells, records, refs):
        self.at, self.cells, self.records = at, cells, records
        (self.table_c, self.table_n, self.wide, self.acc_f, self.acc_n, self.rest, self.hot_c, self.hot_n,
         self.factor, self.keep_c, self.keep_n, self.found, self.values) = refs
        self.rows_c, self.lanes = self.rest.shape
        self.rows_n = self.acc_n.shape[0] // 4
        self.sources, self.width = cells.shape[1:]
        _, self.bx, self.by, self.bz = block
        self.hy = self.by // 2
        self.plain = self.sources <= 16

    def chunks(self, step):
        if self.plain:
            for q in range(self.sources // 2):
                step(q)
        else:
            pl.loop(0, self.sources // 2)(step)

    def fresh(self, acc):
        if not self.plain:
            acc[...] = jnp.zeros_like(acc)

    def split_store(self, table, rows, c, value):
        hi = value.astype(BF16)
        table[c * rows:(c + 1) * rows] = hi
        table[(3 + c) * rows:(4 + c) * rows] = (value - hi.astype(F32)).astype(BF16)

    def pieces(self, nodes):
        at = self.at
        comps, pr, pw = nodes.shape[2:]
        lp = min(2, at.nx)
        rp = at.nx // lp
        for g in range(at.nx):
            r0, l0 = (g // lp) * pr, (g % lp) * pw
            for y in range(at.half):
                for z in range(at.nz):
                    for c in range(comps):
                        r = c * self.rows_n + (y * at.nz + z) * (rp * pr) + r0
                        yield g * at.half + y, z, c, slice(r, r + pr), slice(l0, l0 + pw)

    def both(self, read, q):
        return jnp.concatenate([read(2 * q), read(2 * q + 1)], axis=1)

    def cell(self, s, q):
        return self.both(lambda i: self.cells[s, pl.ds(i, 1), :], q)

    def left(self):
        return lax.broadcasted_iota(jnp.int32, (1, self.width), 1) < self.width // 2

    def weight(self, s, i):
        top, bottom = self.records(s, i), self.records(s, i + self.sources)
        return jnp.where(self.left(), top, pltpu.roll(bottom, self.width // 2, axis=1))

    def ident(self, s, i):
        top, bottom = self.records(s, i), self.records(s, i + self.sources)
        return jnp.where(self.left(), pltpu.roll(top, self.width // 2, axis=1), bottom)

    def hot(self, lane):
        lane_of = lax.broadcasted_iota(jnp.int32, (self.lanes, 2 * self.width), 0)
        return jnp.where(lane_of == lane, 1.0, 0.0).astype(BF16)

    def place_cells(self):
        def step(q):
            cell = self.cell(0, q)
            y = lax.rem(lax.div(cell, self.bz), self.by)
            x = lax.div(cell, self.by * self.bz)
            self.hot_c[q] = self.hot(lax.div(y, self.hy) * self.bz + lax.rem(cell, self.bz))
            self.keep_c[q] = x * self.hy + lax.rem(y, self.hy)

        self.chunks(step)

    def place_nodes(self, s):
        total = self.bx * self.by * self.bz
        line = self.rows_n // self.at.half

        def step(q):
            node = self.both(lambda i: self.ident(s, i), q).astype(jnp.int32)
            row = lax.div(node, self.lanes)
            y = lax.div(row, line)
            self.hot_n[s, q] = self.hot(lax.rem(node, self.lanes))
            self.keep_n[s, q] = jnp.where(lax.rem(y, 2) == self.at.par, lax.div(y, 2) * line + lax.rem(row, line), -1)
            weight = self.both(lambda i: self.weight(s, i), q)
            self.factor[s, q] = jnp.where(self.cell(s, q) < total, penalty * weight, 0.0)

        self.chunks(step)

    def find_all(self, table, rows, hots, keeps, out):
        def step(j):
            two = (2 * j, 2 * j + 1)
            hot = jnp.concatenate([hots[q] for q in two], axis=1)
            row = jnp.concatenate([keeps[q] for q in two], axis=1)
            for c, v in enumerate(self.find(table, rows, hot, row)):
                for i, q in enumerate(two):
                    out[q, c:c + 1] = v[:, 2 * i * self.width:2 * (i + 1) * self.width]

        if self.plain:
            for j in range(self.sources // 4):
                step(j)
        else:
            pl.loop(0, self.sources // 4)(step)

    def find(self, table, rows, hot, row):
        mask = lax.broadcasted_iota(jnp.int32, (rows, hot.shape[1]), 0) == row
        found = jnp.dot(table[...], hot, preferred_element_type=F32)
        found = found[:3 * rows] + found[3 * rows:]
        return [
            jnp.sum(jnp.where(mask, found[c * rows:(c + 1) * rows], 0.0), axis=0, keepdims=True) for c in range(3)
        ]

    def spread(self, hot, row, terms, acc, rows, first):
        mask = lax.broadcasted_iota(jnp.int32, (rows, 2 * self.width), 0) == row
        high = [t.astype(BF16).astype(F32) for t in terms]
        n = len(terms) * rows
        stack = len(terms) > 3 and rows == self.rows_c
        high, low = (
            jnp.concatenate([jnp.where(mask, t, 0.0).astype(BF16) for t in part], axis=0)
            for part in (high, [t - h for t, h in zip(terms, high)])
        )
        values = jnp.concatenate([high, low], axis=int(stack))
        hot = jnp.concatenate([hot, hot], axis=1) if stack else hot
        out = lax.dot_general(values, hot, (((1,), (1,)), ((), ())), preferred_element_type=F32)
        out = out if stack else out[:n] + out[n:]
        if first:
            acc[:n] = out
        else:
            acc[:n] += out

    def first(self, q):
        return self.plain and q == 0

    def find_cells(self, half):
        for c in range(3):
            value = half[c]
            top = value[:, :self.hy].reshape(self.rows_c, self.bz)
            low = value[:, self.hy:].reshape(self.rows_c, self.bz)
            self.split_store(self.table_c, self.rows_c, c, jnp.concatenate([top, low], axis=1))

        self.find_all(self.table_c, self.rows_c, self.hot_c, self.keep_c, self.found)

    def swap(self, src, dst, sem):
        copy = post(src, dst, sem.at[0], sem.at[1], self.at.mate)
        copy.start()
        return copy

    def weigh_found(self):
        def step(q):
            self.values[0, q] = self.found[q] * self.factor[0, q]

        self.chunks(step)

    def spread_nodes(self, s, incoming, weigh):
        if s == 0:
            self.fresh(self.acc_n)

        def step(q):
            terms = [incoming[q, c:c + 1] for c in range(3)] + ([self.factor[s, q]] if weigh else [])
            self.spread(self.hot_n[s, q], self.keep_n[s, q], terms, self.acc_n, self.rows_n, s == 0 and self.first(q))

        self.chunks(step)

    def store_terms(self, terms):
        for p, z, c, r, l in self.pieces(terms):
            terms[p, z, c] = self.acc_n[r, l]

    def find_nodes(self, s, outgoing):
        self.find_all(self.table_n, self.rows_n, self.hot_n.at[s], self.keep_n.at[s], outgoing)

    def load_nodes(self, nodes):
        for p, z, c, r, l in self.pieces(nodes):
            self.wide[r, l] = nodes[p, z, c]
        for c in range(3):
            self.split_store(self.table_n, self.rows_n, c, self.wide[c * self.rows_n:(c + 1) * self.rows_n])

    def spread_cells(self, incoming, weigh):
        self.fresh(self.acc_f)

        def step(q):
            factor = self.factor[0, q]
            terms = [factor * (self.found[q, c:c + 1] + incoming[q, c:c + 1]) for c in range(3)]
            terms += [factor] if weigh else []
            self.spread(self.hot_c[q], self.keep_c[q], terms, self.acc_f, self.rows_c, self.first(q))

        self.chunks(step)
        if weigh:
            self.rest[...] = 1.0 - self.acc_f[3 * self.rows_c:]

    def push(self, half, fluid, first):
        bx, hy, bz = self.bx, self.hy, self.bz
        rest = self.rest[...]
        for c in range(3):
            force = self.acc_f[c * self.rows_c:(c + 1) * self.rows_c]
            for s in (0, 1):
                y, l = slice(s * hy, (s + 1) * hy), slice(s * bz, (s + 1) * bz)
                fluid[c, first:first + bx, y] = (
                    half[c, :, y] * rest[:, l].reshape(bx, hy, bz) + force[:, l].reshape(bx, hy, bz))
        fluid[3, first:first + bx] = half[3]


def prepare(sizes, shell_raw, weights, elements, owned, counts, shell, rec, cells, joined, total):
    nx, _, nz = sizes
    pr, pw = shell.shape[2:]
    lp = min(2, nx)
    for g in range(nx):
        for r in range(pr):
            m = ((g // lp) * pr + r) * lp * pw + (g % lp) * pw
            for c in range(3):
                shell[g, c, r:r + 1, :] = shell_raw[c:c + 1, m:m + pw]
    ranks, slots = weights.shape[1:]
    joined[:, :slots] = weights[0]
    joined[:, slots:] = elements[0].astype(F32)
    for i in range(ranks):
        rec[i // nz, i % nz] = joined[i:i + 1, :]
    same = lax.broadcasted_iota(jnp.int32, (ranks, ranks), 0) == lax.broadcasted_iota(jnp.int32, (ranks, ranks), 1)
    count = jnp.sum(jnp.where(same, counts[...].astype(F32), 0.0), axis=1, keepdims=True)
    slot = lax.broadcasted_iota(jnp.int32, (ranks, slots), 1).astype(F32)
    value = jnp.where(slot < count, owned[0], total)
    cells[0, :, :slots] = value[:ranks // 2]
    cells[0, :, slots:] = value[ranks // 2:]


FAR = ((1, 1, 1), (0, 1, 1), (1, 0, 1), (0, 0, 1), (1, 1, 0))
NEAR = ((0, 1, 0), (1, 0, 0))


def whole_kernel(sizes, fluid_in, shell_in, weights_in, elements_in, owned_in, counts_in, fluid, out, *refs):
    refs = list(refs)
    take = lambda n: [refs.pop(0) for _ in range(n)]
    raw = take(5)
    joined, shell, rec, cells, sem_in = take(5)
    line0, line1, nodes0, nodes1, rec_line, records = take(6)
    half, = take(1)
    terms0, terms1, ours = take(3)
    reduce0, reduce1 = take(3), take(3)
    mine, last = take(2)
    result = fluid
    sem_r, sem_g0, sem_g1, sem_a0, sem_a1, sem_w, sem_m = take(7)
    swapped = take(4)
    couple_refs = take(13)
    sweep_refs = take(12), take(12)
    at = Place(sizes)
    first, second = [Sweep(at, half, *r) for r in sweep_refs]
    for sweep in (first, second):
        sweep.clear()
    at.greet()
    _, bx, by, bz = half.shape
    here = sweep_refs[0][0].at[:, 1:bx + 1]
    fetches = start_all([pltpu.make_async_copy(fluid_in, here, sem_in.at[0])])
    pairs = list(zip((shell_in, weights_in, elements_in, owned_in, counts_in), raw))
    fetches += start_all([pltpu.make_async_copy(src, dst, sem_in.at[i + 1]) for i, (src, dst) in enumerate(pairs)])
    fetches.pop(0).wait()
    first.pack()
    at.meet()
    first.start(FAR + NEAR)
    wait_all(fetches)
    prepare(sizes, *raw, shell, rec, cells, joined, bx * by * bz)
    sems = [sem_m.at[2 * i:2 * i + 2] for i in range(5)]
    read = lambda s, i: records[i // at.nz, i % at.nz, at.par if s == 0 else 1 - at.par]
    couple = Couple(at, half.shape, cells, read, couple_refs)
    gather = Gather(at, shell.at[at.x], line0, nodes0, sem_g0)
    for d in range(1, at.nz):
        z, device = at.line_peer(d)
        post(rec.at[:, z], rec_line.at[at.z], sem_r.at[0], sem_r.at[1], device).start()
    swaps = [couple.swap(cells.at[0], cells.at[1], sems[0])]
    gather.start()
    rec_line[at.z] = rec[:, at.z]
    couple.place_cells()
    if at.nz > 1:
        drain(sem_r.at[0], rec_line.at[:at.nz - 1])
        drain(sem_r.at[1], rec_line.at[:at.nz - 1])
    for d in range(1, at.plane):
        p, device = at.plane_peer(d)
        post(rec_line.at[:, pl.ds(2 * lax.div(p, 2), 2)], records.at[at.p], sem_r.at[2], sem_r.at[3], device).start()
    records[at.p] = rec_line[:, pl.ds(2 * lax.div(at.p, 2), 2)]
    first.wait()
    gather.own()
    first.finish()
    couple.find_cells(half)
    for d in range(1, at.nz):
        gather.forward(d)
    drain(sem_r.at[2], records.at[:at.plane - 1])
    drain(sem_r.at[3], records.at[:at.plane - 1])
    couple.place_nodes(0)
    couple.weigh_found()
    swaps[0].wait()
    swaps = [couple.swap(couple.values.at[0], couple.values.at[1], sems[1])]
    couple.place_nodes(1)
    couple.spread_nodes(0, couple.values.at[0], True)
    swaps[0].wait()
    couple.spread_nodes(1, couple.values.at[1], True)
    couple.store_terms(terms0)
    loads = Reduce(at, terms0, *reduce0, sem_a0)
    loads.start()

    gather.wait()
    couple.load_nodes(nodes0)
    couple.find_nodes(1, swapped[0])
    swaps = [couple.swap(swapped[0], swapped[1], sems[2])]
    couple.find_nodes(0, couple.found)
    swaps[0].wait()
    couple.spread_cells(swapped[1], True)
    couple.push(half, second.fx, 1)
    second.pack()
    second.start(FAR + NEAR)
    loads.forward(1)
    second.wait()
    second.finish()
    loads.wait()
    total = loads.total(0)
    ours[at.x] = 1.0 - relaxation * total[3:]
    mine[...] = shell[at.x] * (1.0 - relaxation * total[3:]) + relaxation * total[:3]
    gather = Gather(at, mine, line1, nodes1, sem_g1)
    gather.start()
    gather.own()
    for dx in range(1, at.nx):
        device = (lax.rem(at.x + dx, at.nx), at.y, at.z)
        post(ours.at[at.x], ours.at[at.x], sem_w.at[0], sem_w.at[1], device).start()
    couple.find_cells(half)
    couple.weigh_found()
    swaps = [couple.swap(couple.values.at[0], couple.values.at[1], sems[3])]
    couple.spread_nodes(0, couple.values.at[0], False)
    for d in range(1, at.nz):
        gather.forward(d)
    swaps[0].wait()
    couple.spread_nodes(1, couple.values.at[1], False)
    couple.store_terms(terms1)
    loads = Reduce(at, terms1, *reduce1, sem_a1)
    loads.start()
    gather.wait()
    couple.load_nodes(nodes1)
    couple.find_nodes(1, swapped[2])
    swaps = [couple.swap(swapped[2], swapped[3], sems[4])]
    loads.forward(at.nx)
    couple.find_nodes(0, couple.found)
    swaps[0].wait()
    couple.spread_cells(swapped[3], False)
    couple.push(half, result, 0)
    if at.nx > 1:
        drain(sem_w.at[0], ours.at[:at.nx - 1])
        drain(sem_w.at[1], ours.at[:at.nx - 1])
    loads.wait()
    for dx in range(at.nx):
        x = lax.rem(at.x + at.nx - dx, at.nx)
        last[x] = nodes1[x * at.half + at.yc, at.z] * ours[x] + relaxation * loads.total(dx)
    pr, pw = shell.shape[2:]
    lp = min(2, at.nx)
    for g in range(at.nx):
        for r in range(pr):
            m = ((g // lp) * pr + r) * lp * pw + (g % lp) * pw
            for c in range(3):
                out[c:c + 1, m:m + pw] = last[g, c, r:r + 1, :]

def on_device(sizes, fluid_state, shell_disp, quad_weights, quad_elements, owner_cells, owner_counts):
    nx, ny, nz = sizes
    plane = nx * ny
    slots = quad_weights.shape[2]
    ranks = quad_weights.shape[1]
    block = fluid_state.shape
    nodes_here = shell_disp.shape[1]
    lanes = 2 * block[3]
    lp = min(2, nx)
    rp = nx // lp
    pr, pw = nodes_here // lanes // rp, lanes // lp
    piece = (3, pr, pw)
    rec_shape = (plane, nz, 1, 2 * slots)
    shell_shape = (nx,) + piece
    i32 = lambda s: pltpu.VMEM(s, jnp.int32)

    shape = lambda s: jax.ShapeDtypeStruct(s, F32)
    buf = lambda s: pltpu.VMEM(s, F32)
    line = (nz,) + piece
    team = plane // 2
    full = (team,) + line
    four, thin = (4, pr, pw), (1, pr, pw)
    sem = lambda n: pltpu.SemaphoreType.DMA((n,))

    def reduce_scratch(spread, item):
        return [buf((nz, max(team - 1, 1)) + item), buf((nz,) + item), buf((spread * nz,) + item)]

    rows_n = ny * nz * rp * pr // 2
    rows_c = block[1] * block[2] // 2
    steps, wide = ranks // 4, 4 * slots
    half16 = lambda *s: pltpu.VMEM(s, BF16)
    scratch = [
        buf(shell_disp.shape), buf(quad_weights.shape), i32(quad_elements.shape), i32(owner_cells.shape),
        i32(owner_counts.shape),
        buf((ranks, 2 * slots)), buf(shell_shape), buf(rec_shape), i32((2, ranks // 2, 2 * slots)), sem(6),
        buf(line), buf(line), buf(full), buf(full), buf((nz, plane, 1, 2 * slots)), buf((plane, nz, 2, 1, 2 * slots)),
        buf(block), buf((team, nz) + four), buf(full), buf((nx,) + thin),
        *reduce_scratch(1, four), *reduce_scratch(nx, piece),
        buf(piece), buf(shell_shape),
        sem(4), sem(3 + nz), sem(3 + nz), sem(3 + nz), sem(3 + nz), sem(2), sem(10),
        *[buf((steps, 3, wide))] * 4,
        half16(6 * rows_c, lanes), half16(6 * rows_n, lanes), buf((3 * rows_n, lanes)), buf((4 * rows_c, lanes)),
        buf((4 * rows_n, lanes)), buf((rows_c, lanes)),
        half16(steps, lanes, wide), half16(2, steps, lanes, wide), buf((2, steps, 1, wide)),
        i32((steps, 1, wide)), i32((2, steps, 1, wide)), buf((steps, 3, wide)), buf((2, steps, 3, wide)),
        *sweep_scratch(block), *sweep_scratch(block),
    ]
    anywhere, vmem = pl.BlockSpec(memory_space=pl.ANY), pl.BlockSpec(memory_space=pltpu.VMEM)
    fluid, out = pl.pallas_call(
        functools.partial(whole_kernel, sizes),
        out_shape=(buf(block), buf(shell_disp.shape)),
        in_specs=[anywhere] * 6, out_specs=(vmem, vmem),
        scratch_shapes=scratch,
        compiler_params=pltpu.CompilerParams(collective_id=0, has_side_effects=True, vmem_limit_bytes=56 << 20),
    )(fluid_state, shell_disp, quad_weights, quad_elements, owner_cells, owner_counts)
    return fluid, out


def solution(mesh):
    sizes = tuple(mesh.shape[a] for a in AXES)
    return jax.shard_map(
        functools.partial(on_device, sizes),
        mesh=mesh,
        in_specs=(
            P(None, "gx", "gy", "gz"),
            P(None, ("gy", "gz")),
            P(("gx", "gy", "gz"), None, None),
            P(("gx", "gy", "gz"), None, None),
            P(("gx", "gy", "gz"), None, None),
            P(("gx", "gy", "gz"), None),
        ),
        out_specs=(P(None, "gx", "gy", "gz"), P(None, ("gy", "gz"))),
        check_vma=False,
    )
```
